32 devices in a mesh: dp: 4 (over y, x), expert: 8 (over z, core).
Axes of the slice: x: 2, y: 2, z: 4, core: 2. Of those that a mesh axis runs over, the one named last changes fastest.
Arguments:
- block_input: bfloat16 [6304, 768], P(('dp', 'expert')), may hold values from -12 to 12
- w_qkv: bfloat16 [768, 2304], P('dp'), may hold values from -0.21875 to 0.21875
- b_q: bfloat16 [768], P('dp'), may hold values from -3 to 3
- b_v: bfloat16 [768], P('dp'), may hold values from -3 to 3
- w_proj: bfloat16 [768, 768], P('dp'), may hold values from -1.75 to 1.75
- b_proj: bfloat16 [768], P('dp'), may hold values from -3 to 3
- ln1_gain: bfloat16 [768], P('dp'), may hold values from 0.099609375 to 1.8984375
- ln1_bias: bfloat16 [768], P('dp'), may hold values from -3 to 3
- ln2_gain: bfloat16 [768], P('dp'), may hold values from 0.099609375 to 1.8984375
- ln2_bias: bfloat16 [768], P('dp'), may hold values from -3 to 3
- w_router: bfloat16 [768, 8], P('dp'), may hold values from -0.4375 to 0.4375
- w_in: bfloat16 [8, 768, 3072], P('expert'), may hold values from -0.21875 to 0.21875
- b_in: bfloat16 [8, 3072], P('expert'), may hold values from -3 to 3
- w_out: bfloat16 [8, 3072, 768], P('expert'), may hold values from -0.109375 to 0.109375
- b_out: bfloat16 [8, 768], P('expert'), may hold values from -3 to 3
- routes: int32 [6304, 2], P(('dp', 'expert')), may hold values from 0 to 7, as said below
- slot_index: int32 [6304, 2], P(('dp', 'expert')), may hold values from 0 to 49, as said below
- d_out: bfloat16 [6304, 768], P(('dp', 'expert')), may hold values from -6 to 6
Outputs:
- block_out: bfloat16 [6304, 768], P(('dp', 'expert'))
- grad_input: float32 [6304, 768], P(('dp', 'expert'))
- d_w_qkv: float32 [768, 2304], P('dp')
- d_b_q: float32 [768], P('dp')
- d_b_v: float32 [768], P('dp')
- d_w_proj: float32 [768, 768], P('dp')
- d_b_proj: float32 [768], P('dp')
- d_ln1_gain: float32 [768], P('dp')
- d_ln1_bias: float32 [768], P('dp')
- d_ln2_gain: float32 [768], P('dp')
- d_ln2_bias: float32 [768], P('dp')
- d_w_router: float32 [768, 8], P('dp')
- d_w_in: float32 [8, 768, 3072], P('expert', 'dp')
- d_b_in: float32 [8, 3072], P('expert', 'dp')
- d_w_out: float32 [8, 3072, 768], P('expert', 'dp')
- d_b_out: float32 [8, 768], P('expert', 'dp')
The draws below stay inside these ranges and needn't reach their ends.
Inputs may be any that keep to these rules, and one draw needn't show every extreme that they name: `routes`: each token names two different experts. slot_index[t, k] is the arrival position of choice k of token t at expert routes[t, k] among the tokens of one device, all first choices in token order before all second choices; 49 marks a choice that arrives beyond capacity and is dropped. In every draw one expert receives more than 49 first choices from every device.
All inputs are finite; a program needn't handle non-finite values.
Results may differ from the reference program's by a relative error of at most 0.012.
The reference program's roundings to bfloat16 on the way count: a program that leaves them out, or rounds other values in their place, can miss the bound.
Values may be sent and summed in bfloat16 or wider, within the bound.
No kernel may reach another device: no remote copies, remote signals or barrier semaphores. Data moves between devices by JAX's collectives and lax.ppermute only.
A program may use at most 128 MiB of HBM per device.

```python
import math
import jax
import jax.numpy as jnp
from jax import lax

D = 768
HEADS = 12
HEAD_DIM = 64
FF = 3072
SEQ = 197
EXPERTS = 8
TOK_DEV = 197
TOKENS = 6304
CAP = 49


def route_plan(key):
    blocks = TOKENS // TOK_DEV
    k_order, k_left, k_right, k_shift, k_hot = jax.random.split(jax.random.fold_in(key, 5), 5)
    expert_order = jax.random.permutation(k_order, EXPERTS).astype(jnp.int32)
    pick_rank = jnp.minimum(jax.random.randint(k_left, (blocks, TOK_DEV), 0, EXPERTS), jax.random.randint(k_right, (blocks, TOK_DEV), 0, EXPERTS))
    first_choice = expert_order[pick_rank]
    token_ranks = jax.vmap(lambda sub_key: jax.random.permutation(sub_key, TOK_DEV))(jax.random.split(k_hot, blocks))
    first_choice = jnp.where(token_ranks <= CAP, expert_order[0], first_choice).astype(jnp.int32)
    second = ((first_choice + 1 + jax.random.randint(k_shift, (blocks, TOK_DEV), 0, EXPERTS - 1)) % EXPERTS).astype(jnp.int32)
    labels = jnp.arange(EXPERTS, dtype=jnp.int32)
    first_hot = (first_choice[:, :, None] == labels[None, None, :]).astype(jnp.int32)
    second_hot = (second[:, :, None] == labels[None, None, :]).astype(jnp.int32)
    first_pos = jnp.sum((jnp.cumsum(first_hot, axis=1) - first_hot) * first_hot, axis=2)
    second_base = jnp.sum(first_hot, axis=1, keepdims=True) + jnp.cumsum(second_hot, axis=1) - second_hot
    second_pos = jnp.sum(second_base * second_hot, axis=2)
    route_table = jnp.stack([first_choice, second], axis=2).reshape(TOKENS, 2)
    slot_table = jnp.minimum(jnp.stack([first_pos, second_pos], axis=2), CAP).reshape(TOKENS, 2)
    return (route_table.astype(jnp.int32), slot_table.astype(jnp.int32))


def draw_routes(key, part):
    return route_plan(key)[0]


def draw_slot_index(key, part):
    return route_plan(key)[1]


def raised(entries, rng, source, target, parts, factor):
    owner, partner = [(jnp.arange(entries.shape[axis_at]) // (entries.shape[axis_at] // parts)).reshape([-1 if axis == axis_at else 1 for axis in range(entries.ndim)]) for axis_at in (source, target)]
    chosen = jax.random.permutation(rng, parts)[partner]
    strong = (owner == chosen) | (owner == (partner + parts // 2) % parts)
    return jnp.where(strong, factor * entries, entries)


def level_of(key, shape, cuts, least, top_value):
    loudness = 1.0
    for position, shards_of in cuts:
        steps = jax.random.uniform(jax.random.fold_in(jax.random.fold_in(key, 6), position), (shards_of,), jnp.float32, least / len(cuts), top_value / len(cuts))
        loudness = loudness * jnp.repeat(jnp.exp(steps), shape[position] // shards_of).reshape((-1,) + (1,) * (len(shape) - 1 - position))
    return loudness


def scatter_about(own_key, shape, width, reach, shards=(), held_as=jnp.bfloat16):
    gain = level_of(own_key, shape, shards, -0.22, 0.18) if shards else 1.0
    result = jax.random.normal(own_key, shape, jnp.float32) * width * gain
    return jnp.minimum(jnp.maximum(result, -reach), reach).astype(held_as)


def heavy_noise(rng, extent, scale, bound, cuts, heavy, kind=jnp.bfloat16):
    array = scale * jax.random.normal(rng, extent, jnp.float32)
    if cuts:
        array = array * level_of(rng, extent, cuts, -0.22, 0.18)
    return jnp.clip(raised(array, jax.random.fold_in(rng, 3), *heavy), -bound, bound).astype(kind)


def setup_inputs(seed: int = 0) -> dict:
    key_list = jax.random.split(jax.random.key(seed), 19)
    block_input = heavy_noise(key_list[0], (TOKENS, D), 1.0, 12.0, ((0, 32),), (0, 1, 32, 2.75))
    w_qkv = scatter_about(key_list[1], (D, 3 * D), D ** -0.5, 0.21875, ((0, 4),))
    b_q = scatter_about(key_list[2], (D,), 0.5, 3.0, ((0, 4),))
    b_v = scatter_about(key_list[3], (D,), 0.5, 3.0, ((0, 4),))
    w_proj = scatter_about(key_list[4], (D, D), (D // 64) ** -0.5, 1.75, ((0, 4),))
    b_proj = scatter_about(key_list[5], (D,), 0.5, 3.0, ((0, 4),))
    ln1_gain = jnp.clip(1.0 + 0.18 * jax.random.normal(key_list[6], (D,), jnp.float32), 0.099609375, 1.8984375).astype(jnp.bfloat16)
    ln1_bias = scatter_about(key_list[7], (D,), 0.5, 3.0, ((0, 4),))
    ln2_gain = jnp.clip(1.0 + 0.18 * jax.random.normal(key_list[8], (D,), jnp.float32), 0.099609375, 1.8984375).astype(jnp.bfloat16)
    ln2_bias = scatter_about(key_list[9], (D,), 0.5, 3.0, ((0, 4),))
    w_router = scatter_about(key_list[10], (D, EXPERTS), (D // 4) ** -0.5, 0.4375, ((0, 4),))
    w_in = scatter_about(key_list[11], (EXPERTS, D, FF), D ** -0.5, 0.21875, ((0, 8),))
    b_in = scatter_about(key_list[12], (EXPERTS, FF), 0.5, 3.0, ((0, 8),))
    w_out = scatter_about(key_list[13], (EXPERTS, FF, D), FF ** -0.5, 0.109375, ((0, 8),))
    b_out = scatter_about(key_list[14], (EXPERTS, D), 0.5, 3.0, ((0, 8),))
    routes = draw_routes(jax.random.fold_in(key_list[18], 71), 0)
    slot_index = draw_slot_index(jax.random.fold_in(key_list[18], 71), 0)
    d_out = scatter_about(key_list[17], (TOKENS, D), 1.0, 6.0, ((0, 32),))
    return {"block_input": block_input, "w_qkv": w_qkv, "b_q": b_q, "b_v": b_v, "w_proj": w_proj, "b_proj": b_proj, "ln1_gain": ln1_gain, "ln1_bias": ln1_bias, "ln2_gain": ln2_gain, "ln2_bias": ln2_bias, "w_router": w_router, "w_in": w_in, "b_in": b_in, "w_out": w_out, "b_out": b_out, "routes": routes, "slot_index": slot_index, "d_out": d_out}


NORM_EPS = 1e-06
SQRT_HALF = 0.7071067811865476
INV_ROOT_TWO_PI = 0.3989422804014327

def widen(values):
    return lax.optimization_barrier(values).astype(jnp.float32)

def normalize(values):
    center = values - lax.optimization_barrier(jnp.mean(values, axis=-1, keepdims=True))
    inv_std = lax.rsqrt(lax.optimization_barrier(jnp.mean(center * center, axis=-1, keepdims=True)) + NORM_EPS)
    return (center * inv_std, inv_std)

def norm_back(grad_in, normed, inv_std, gain_vec):
    scaled = grad_in * gain_vec
    mean_plain = lax.optimization_barrier(jnp.mean(scaled, axis=-1, keepdims=True))
    mean_mixed = lax.optimization_barrier(jnp.mean(scaled * normed, axis=-1, keepdims=True))
    return inv_std * (scaled - mean_plain - normed * mean_mixed)

def gelu_value(pre_act):
    return 0.5 * pre_act * (1.0 + lax.erf(pre_act * SQRT_HALF))

def gelu_slope(pre_act):
    return 0.5 * (1.0 + lax.erf(pre_act * SQRT_HALF)) + pre_act * INV_ROOT_TWO_PI * jnp.exp(-0.5 * pre_act * pre_act)

def by_heads(values, images):
    return widen(values).reshape(images, SEQ, HEADS, HEAD_DIM)

def slot_tables(routes, slot_table, experts, capacity):
    kept_mask = slot_table < capacity
    target = jnp.where(kept_mask, routes * capacity + slot_table, -1).reshape(-1)
    slot_match = target[:, None] == lax.broadcasted_iota(jnp.int32, (1, experts * capacity), 1)
    filled = jnp.any(slot_match, axis=0)
    choice_ids = lax.broadcasted_iota(jnp.int32, (target.shape[0], 1), 0)
    source = lax.optimization_barrier(jnp.sum(jnp.where(slot_match, choice_ids, 0), axis=0, dtype=jnp.int32))
    return (kept_mask.reshape(-1), jnp.maximum(target, 0), filled, source)

def one_block(weights, block_in):
    w_qkv, b_q, b_v, w_proj, b_proj, gain_one, bias_one, gain_two, bias_two, w_router, w_in, b_in, w_out, b_out = weights
    x_block, grad_block, route_block, slot_block = block_in
    tokens = x_block.shape[0]
    images = tokens // SEQ
    experts = w_in.shape[0]
    score_scale = 1.0 / math.sqrt(HEAD_DIM)
    resid = x_block.astype(jnp.float32)
    normed_one, inv_one = normalize(resid)
    a_in = (normed_one * gain_one + bias_one).astype(jnp.bfloat16)
    qkv = jnp.dot(a_in, w_qkv, preferred_element_type=jnp.float32)
    queries = (qkv[:, :D] + b_q).astype(jnp.bfloat16)
    key_vecs = qkv[:, D:2 * D].astype(jnp.bfloat16)
    values = (qkv[:, 2 * D:] + b_v).astype(jnp.bfloat16)
    query_heads = by_heads(queries, images)
    key_heads = by_heads(key_vecs, images)
    value_heads = by_heads(values, images)
    scores = jnp.einsum('bqhd,bkhd->bhqk', query_heads, key_heads) * score_scale
    row_max = lax.optimization_barrier(jnp.max(scores, axis=-1, keepdims=True))
    exp_scores = jnp.exp(scores - row_max)
    row_total = lax.optimization_barrier(jnp.sum(exp_scores, axis=-1, keepdims=True))
    log_total = row_max + jnp.log(row_total)
    probs_low = (exp_scores / row_total).astype(jnp.bfloat16)
    context = jnp.einsum('bhqk,bkhd->bqhd', widen(probs_low), value_heads).reshape(tokens, D).astype(jnp.bfloat16)
    hidden = resid + jnp.dot(context, w_proj, preferred_element_type=jnp.float32) + b_proj
    normed_two, inv_two = normalize(hidden)
    y_in = (normed_two * gain_two + bias_two).astype(jnp.bfloat16)
    logits = jnp.dot(y_in, w_router, preferred_element_type=jnp.float32)
    route_hot = (route_block[:, :, None] == jnp.arange(experts, dtype=jnp.int32)[None, None, :]).astype(jnp.float32)
    chosen = lax.optimization_barrier(jnp.sum(logits[:, None, :] * route_hot, axis=-1))
    first_gate = jax.nn.sigmoid(chosen[:, 0] - chosen[:, 1])
    gate_vals = jnp.stack([first_gate, 1.0 - first_gate], axis=1)
    kept_flat, fetch_index, filled, source = slot_tables(route_block, slot_block, experts, CAP)
    sent_slots = jnp.where(filled[:, None], y_in[source // 2], 0).astype(jnp.bfloat16).reshape(experts, CAP, D)
    pre_act = jnp.einsum('ecd,edf->ecf', widen(sent_slots), w_in) + b_in[:, None, :]
    activated = gelu_value(pre_act).astype(jnp.bfloat16)
    expert_out = (jnp.einsum('ecf,efd->ecd', widen(activated), w_out) + b_out[:, None, :]).astype(jnp.bfloat16)
    picked = jnp.where(kept_flat[:, None], widen(expert_out).reshape(experts * CAP, D)[fetch_index], 0.0).reshape(tokens, 2, D)
    block_out = (hidden + lax.optimization_barrier(jnp.sum(gate_vals[:, :, None] * picked, axis=1))).astype(jnp.bfloat16)
    grad_out = grad_block.astype(jnp.float32)
    d_choice = (gate_vals[:, :, None] * grad_out[:, None, :]).reshape(2 * tokens, D).astype(jnp.bfloat16)
    d_sent = jnp.where(filled[:, None], d_choice[source], 0).astype(jnp.bfloat16).reshape(experts, CAP, D)
    d_gate = lax.optimization_barrier(jnp.sum(grad_out[:, None, :] * picked, axis=-1))
    d_diff = (d_gate[:, 0] - d_gate[:, 1]) * gate_vals[:, 0] * gate_vals[:, 1]
    d_logits = (d_diff[:, None] * (route_hot[:, 0] - route_hot[:, 1])).astype(jnp.bfloat16)
    sent_wide = widen(d_sent)
    d_b_out = lax.optimization_barrier(jnp.sum(sent_wide, axis=1))
    d_w_out = jnp.einsum('ecf,ecd->efd', widen(activated), sent_wide)
    d_pre = jnp.einsum('ecd,efd->ecf', sent_wide, w_out) * gelu_slope(pre_act)
    d_b_in = lax.optimization_barrier(jnp.sum(d_pre, axis=1))
    d_pre_low = d_pre.astype(jnp.bfloat16)
    d_w_in = jnp.einsum('ecd,ecf->edf', widen(sent_slots), widen(d_pre_low))
    d_expert_in = jnp.einsum('ecf,edf->ecd', widen(d_pre_low), w_in).astype(jnp.bfloat16)
    back_rows = jnp.where(kept_flat[:, None], widen(d_expert_in).reshape(experts * CAP, D)[fetch_index], 0.0).reshape(tokens, 2, D)
    d_w_router = jnp.dot(y_in.T, d_logits, preferred_element_type=jnp.float32)
    d_y = lax.optimization_barrier(jnp.sum(back_rows, axis=1)) + jnp.dot(d_logits, w_router.T, preferred_element_type=jnp.float32)
    d_gain_two = lax.optimization_barrier(jnp.sum(d_y * normed_two, axis=0))
    d_bias_two = lax.optimization_barrier(jnp.sum(d_y, axis=0))
    d_hidden = grad_out + norm_back(d_y, normed_two, inv_two, gain_two)
    d_b_proj = lax.optimization_barrier(jnp.sum(d_hidden, axis=0))
    d_hidden_low = d_hidden.astype(jnp.bfloat16)
    d_w_proj = jnp.dot(context.T, d_hidden_low, preferred_element_type=jnp.float32)
    d_context = jnp.dot(d_hidden_low, w_proj.T, preferred_element_type=jnp.float32).astype(jnp.bfloat16)
    grad_heads = by_heads(d_context, images)
    probs = jnp.exp(jnp.einsum('bqhd,bkhd->bhqk', query_heads, key_heads) * score_scale - log_total)
    d_probs = jnp.einsum('bqhd,bkhd->bhqk', grad_heads, value_heads)
    d_values = jnp.einsum('bhqk,bqhd->bkhd', widen(probs.astype(jnp.bfloat16)), grad_heads).reshape(tokens, D)
    row_delta = lax.optimization_barrier(jnp.sum(probs * d_probs, axis=-1, keepdims=True))
    d_scores = (probs * (d_probs - row_delta) * score_scale).astype(jnp.bfloat16)
    d_queries = jnp.einsum('bhqk,bkhd->bqhd', widen(d_scores), key_heads).reshape(tokens, D)
    d_keys = jnp.einsum('bhqk,bqhd->bkhd', widen(d_scores), query_heads).reshape(tokens, D)
    d_b_q = lax.optimization_barrier(jnp.sum(d_queries, axis=0))
    d_b_v = lax.optimization_barrier(jnp.sum(d_values, axis=0))
    d_qkv = jnp.concatenate([d_queries, d_keys, d_values], axis=1).astype(jnp.bfloat16)
    d_w_qkv = jnp.dot(a_in.T, d_qkv, preferred_element_type=jnp.float32)
    d_a = jnp.dot(d_qkv, w_qkv.T, preferred_element_type=jnp.float32)
    d_gain_one = lax.optimization_barrier(jnp.sum(d_a * normed_one, axis=0))
    d_bias_one = lax.optimization_barrier(jnp.sum(d_a, axis=0))
    d_input = d_hidden + norm_back(d_a, normed_one, inv_one, gain_one)
    grads = (d_w_qkv, d_b_q, d_b_v, d_w_proj, d_b_proj, d_gain_one, d_bias_one, d_gain_two, d_bias_two, d_w_router, d_w_in, d_b_in, d_w_out, d_b_out)
    return (block_out, d_input, grads)

def reference(block_input, w_qkv, b_q, b_v, w_proj, b_proj, ln1_gain, ln1_bias, ln2_gain, ln2_bias, w_router, w_in, b_in, w_out, b_out, routes, slot_index, d_out):
    blocks = block_input.shape[0] // TOK_DEV
    weights = (w_qkv, b_q.astype(jnp.float32), b_v.astype(jnp.float32), w_proj, b_proj.astype(jnp.float32), ln1_gain.astype(jnp.float32), ln1_bias.astype(jnp.float32), ln2_gain.astype(jnp.float32), ln2_bias.astype(jnp.float32), w_router, w_in.astype(jnp.float32), b_in.astype(jnp.float32), w_out.astype(jnp.float32), b_out.astype(jnp.float32))
    stacked = (block_input.reshape(blocks, TOK_DEV, D), d_out.reshape(blocks, TOK_DEV, D), routes.reshape(blocks, TOK_DEV, 2), slot_index.reshape(blocks, TOK_DEV, 2))
    zero_grads = tuple((jnp.zeros(member.shape, jnp.float32) for member in weights))

    def scan_step(running, block_in):
        out_block, dx_block, grads = one_block(weights, block_in)
        return (jax.tree.map(jnp.add, running, grads), (out_block, dx_block))
    totals, (out_blocks, dx_blocks) = lax.scan(scan_step, zero_grads, stacked)
    return (out_blocks.reshape(-1, D), dx_blocks.reshape(-1, D), totals[0], totals[1], totals[2], totals[3], totals[4], totals[5], totals[6], totals[7], totals[8], totals[9], totals[10], totals[11], totals[12], totals[13])
```

```python
import math

import jax
import jax.numpy as jnp
from jax import lax
from jax.experimental import pallas as pl
from jax.experimental.pallas import tpu as pltpu
from jax.sharding import PartitionSpec as P

HEAD_DIM = 64
SEQ = 197


NORM_EPS = 1e-06
SQRT_HALF = 0.7071067811865476
INV_ROOT_TWO_PI = 0.3989422804014327


def normalize(values):
    center = values - jnp.mean(values, axis=-1, keepdims=True)
    inv_std = lax.rsqrt(jnp.mean(center * center, axis=-1, keepdims=True) + NORM_EPS)
    return (center * inv_std, inv_std)


def norm_back(grad_in, normed, inv_std, gain_vec):
    scaled = grad_in * gain_vec
    mean_plain = jnp.mean(scaled, axis=-1, keepdims=True)
    mean_mixed = jnp.mean(scaled * normed, axis=-1, keepdims=True)
    return inv_std * (scaled - mean_plain - normed * mean_mixed)


def gelu_value(pre_act):
    return 0.5 * pre_act * (1.0 + lax.erf(pre_act * SQRT_HALF))


def gelu_slope(pre_act):
    return 0.5 * (1.0 + lax.erf(pre_act * SQRT_HALF)) + pre_act * INV_ROOT_TWO_PI * jnp.exp(
        -0.5 * pre_act * pre_act
    )


def by_heads(values, images):
    return values.reshape(images, SEQ, values.shape[1] // HEAD_DIM, HEAD_DIM)


def swap(values, axis, mask):
    size = lax.axis_size(axis)
    return lax.ppermute(values, axis, [(index, index ^ mask) for index in range(size)])


def place_rows(pieces, starts, rows_out):
    count = len(pieces)

    def body(starts_ref, *refs):
        sems = refs[-1]
        out_ref = refs[count]
        copies = []
        for index in range(count):
            rows = refs[index].shape[0]
            offset = pl.multiple_of(starts_ref[index], 16)
            copies.append(
                pltpu.make_async_copy(
                    refs[index], out_ref.at[pl.ds(offset, rows)], sems.at[index]
                )
            )
        for copy in copies:
            copy.start()
        for copy in copies:
            copy.wait()

    return pl.pallas_call(
        body,
        out_shape=jax.ShapeDtypeStruct((rows_out,) + pieces[0].shape[1:], pieces[0].dtype),
        in_specs=[pl.BlockSpec(memory_space=pltpu.SMEM)]
        + [pl.BlockSpec(memory_space=pl.ANY)] * count,
        out_specs=pl.BlockSpec(memory_space=pl.ANY),
        scratch_shapes=[pltpu.SemaphoreType.DMA((count,))],
        cost_estimate=pl.CostEstimate(
            flops=0,
            bytes_accessed=2 * rows_out * pieces[0].shape[1] * pieces[0].dtype.itemsize,
            transcendentals=0,
        ),
    )(starts, *pieces)


def gather_shared(shard):
    groups = lax.axis_size("dp")
    rows = shard.shape[0]
    if groups != 4:
        return lax.all_gather(shard, "dp", axis=0, tiled=True)
    me = lax.axis_index("dp")
    core = lax.axis_index("expert") % 2
    half = rows // 2
    part = half // 2
    mine = lax.dynamic_slice_in_dim(shard, core * half, half, 0)
    from_one = swap(mine, "dp", 1)
    from_two = swap(mine, "dp", 2)
    far_low = swap(from_one[:part], "dp", 2)
    far_high = swap(from_two[part:], "dp", 1)
    other_one = swap(from_one, "expert", 1)
    other_two = swap(from_two, "expert", 1)
    other_low = swap(far_low, "expert", 1)
    other_high = swap(far_high, "expert", 1)
    base_mine = core * half
    base_other = (1 - core) * half
    one, two, far = (me ^ 1) * rows, (me ^ 2) * rows, (me ^ 3) * rows
    starts = [
        me * rows,
        one + base_mine,
        two + base_mine,
        far + base_mine,
        far + base_mine + part,
        one + base_other,
        two + base_other,
        far + base_other,
        far + base_other + part,
    ]
    pieces = [
        shard,
        from_one,
        from_two,
        far_low,
        far_high,
        other_one,
        other_two,
        other_low,
        other_high,
    ]
    return place_rows(pieces, jnp.stack(starts).astype(jnp.int32), groups * rows)


def gather_rows(rows):
    groups = lax.axis_size("dp")
    if groups != 4:
        return [rows] + [swap(rows, "dp", mask) for mask in range(1, groups)]
    half = rows.shape[0] // 2
    from_one = swap(rows, "dp", 1)
    from_two = swap(rows, "dp", 2)
    return [
        rows,
        from_one,
        from_two,
        swap(from_one[:half], "dp", 2),
        swap(from_two[half:], "dp", 1),
    ]


def exchange(blocks):
    return [blocks[0]] + [swap(blocks[mask], "expert", mask) for mask in range(1, len(blocks))]


def in_order(pieces, me, axis):
    stack = jnp.stack(pieces)
    return jnp.concatenate(
        [
            lax.dynamic_index_in_dim(stack, me ^ index, 0, keepdims=False)
            for index in range(len(pieces))
        ],
        axis=axis,
    )


def reduce_all(partial):
    groups = lax.axis_size("dp")
    layers = lax.axis_size("expert") // 2
    me = lax.axis_index("dp")
    slot = lax.axis_index("expert")
    core, layer = slot % 2, slot // 2
    rows, columns = partial.shape
    half = columns // 2
    keep = lax.dynamic_slice_in_dim(partial, core * half, half, 1)
    give = lax.dynamic_slice_in_dim(partial, (1 - core) * half, half, 1).astype(jnp.bfloat16)
    keep = keep + swap(give, "expert", 1).astype(jnp.float32)
    share = rows // groups
    low = keep.astype(jnp.bfloat16)
    total = lax.dynamic_slice_in_dim(keep, me * share, share, 0)
    for mask in range(1, groups):
        piece = lax.dynamic_slice_in_dim(low, (me ^ mask) * share, share, 0)
        total = total + swap(piece, "dp", mask).astype(jnp.float32)
    part = share // layers
    low = total.astype(jnp.bfloat16)
    done = lax.dynamic_slice_in_dim(total, layer * part, part, 0)
    for mask in range(1, layers):
        piece = lax.dynamic_slice_in_dim(low, (layer ^ mask) * part, part, 0)
        done = done + swap(piece, "expert", 2 * mask).astype(jnp.float32)
    done = done.astype(jnp.bfloat16)
    pieces = [done] + [swap(done, "expert", 2 * mask) for mask in range(1, layers)]
    column = in_order(pieces, layer, 0)
    other = swap(column, "expert", 1)
    return in_order([column, other], core, 1).astype(jnp.float32)


def per_device(
    block_input,
    w_qkv,
    b_q,
    b_v,
    w_proj,
    b_proj,
    ln1_gain,
    ln1_bias,
    ln2_gain,
    ln2_bias,
    w_router,
    w_in,
    b_in,
    w_out,
    b_out,
    routes,
    slot_index,
    d_out,
):
    tokens = block_input.shape[0]
    width = block_input.shape[1]
    images = tokens // SEQ
    hidden_units = w_in.shape[2]
    experts = w_in.shape[0] * lax.axis_size("expert")
    groups = lax.axis_size("dp")
    capacity = 2 * tokens // experts
    slots = -(-(capacity + 1) // 8) * 8
    score_scale = 1.0 / math.sqrt(HEAD_DIM)
    dp_me = lax.axis_index("dp")
    expert_me = lax.axis_index("expert")
    vectors = jnp.stack([b_q, b_v, b_proj, ln1_gain, ln1_bias, ln2_gain, ln2_bias], axis=1)
    side = 128
    side_cols = jnp.concatenate([vectors, w_router], axis=1)
    side_cols = jnp.pad(side_cols, ((0, 0), (0, side - side_cols.shape[1])))
    full_qkv = gather_shared(jnp.concatenate([w_qkv, side_cols], axis=1))
    full_proj = gather_shared(w_proj)
    kept = slot_index < capacity
    target = jnp.where(kept, (routes ^ expert_me) * slots + slot_index, -1)
    slot_ids = lax.broadcasted_iota(jnp.int32, (1, experts * slots), 1)
    hot_first = target[:, :1] == slot_ids
    hot_second = target[:, 1:] == slot_ids
    hot_low = (hot_first | hot_second).astype(jnp.bfloat16)

    def to_slots(values):
        return jnp.einsum(
            "ts,td->sd", hot_low, values, preferred_element_type=jnp.float32
        ).astype(jnp.bfloat16)

    def split(values):
        return list(values.reshape(experts, slots, width))

    grad_slots = jnp.concatenate(exchange(split(to_slots(d_out))), axis=0)
    grad_all = gather_rows(grad_slots)

    side_full = full_qkv[:, 3 * width :]
    wide_vectors = side_full[:, :7].astype(jnp.float32).T
    bias_q, bias_v, bias_proj, gain_one, bias_one, gain_two, bias_two = (
        wide_vectors[index] for index in range(7)
    )
    full_router = side_full[:, 7 : 7 + experts]
    resid = block_input.astype(jnp.float32)
    normed_one, inv_one = normalize(resid)
    a_in = (normed_one * gain_one + bias_one).astype(jnp.bfloat16)
    qkv = jnp.dot(a_in, full_qkv, preferred_element_type=jnp.float32)
    queries = (qkv[:, :width] + bias_q).astype(jnp.bfloat16)
    key_vecs = qkv[:, width : 2 * width].astype(jnp.bfloat16)
    values = (qkv[:, 2 * width : 3 * width] + bias_v).astype(jnp.bfloat16)
    query_heads = by_heads(queries, images)
    key_heads = by_heads(key_vecs, images)
    value_heads = by_heads(values, images)
    scores = (
        jnp.einsum("bqhd,bkhd->bhqk", query_heads, key_heads, preferred_element_type=jnp.float32)
        * score_scale
    )
    row_max = jnp.max(scores, axis=-1, keepdims=True)
    exp_scores = jnp.exp(scores - row_max)
    row_total = jnp.sum(exp_scores, axis=-1, keepdims=True)
    log_total = row_max + jnp.log(row_total)
    probs_low = (exp_scores / row_total).astype(jnp.bfloat16)
    context = (
        jnp.einsum("bhqk,bkhd->bqhd", probs_low, value_heads, preferred_element_type=jnp.float32)
        .reshape(tokens, width)
        .astype(jnp.bfloat16)
    )
    hidden = resid + jnp.dot(context, full_proj, preferred_element_type=jnp.float32) + bias_proj
    normed_two, inv_two = normalize(hidden)
    y_in = (normed_two * gain_two + bias_two).astype(jnp.bfloat16)
    logits = jnp.dot(y_in, full_router, preferred_element_type=jnp.float32)
    route_hot = (routes[:, :, None] == lax.broadcasted_iota(jnp.int32, (1, 1, experts), 2)).astype(
        jnp.float32
    )
    chosen = jnp.sum(logits[:, None, :] * route_hot, axis=-1)
    first_gate = jax.nn.sigmoid(chosen[:, 0] - chosen[:, 1])
    second_gate = 1.0 - first_gate

    slot_gates = jnp.sum(
        jnp.where(hot_first, first_gate[:, None], 0.0)
        + jnp.where(hot_second, second_gate[:, None], 0.0),
        axis=0,
    ).reshape(experts, 1, slots)
    terms = []
    rest = slot_gates
    for _ in range(3):
        term = lax.reduce_precision(rest, 8, 7)
        rest = rest - term
        terms.append(jnp.pad(term, ((0, 0), (0, 0), (0, 128 - slots))))
    gate_row = jnp.pad(
        jnp.concatenate(terms, axis=2), ((0, 0), (0, 0), (0, width - 3 * 128))
    ).astype(jnp.bfloat16)
    row_ids = lax.broadcasted_iota(jnp.int32, (1, slots, 1), 1)
    sent = jnp.where(
        row_ids == capacity, gate_row, to_slots(y_in).reshape(experts, slots, width)
    )
    recv_rows = jnp.concatenate(exchange(list(sent)), axis=0)
    recv_all = gather_rows(recv_rows)

    def gated(rows, grads):
        blocks = rows.shape[0] // slots
        line = rows.reshape(blocks, slots, width)[:, capacity, : 3 * 128].astype(jnp.float32)
        line = line[:, :128] + line[:, 128:256] + line[:, 256:384]
        column = line[:, :slots].reshape(blocks, slots, 1)
        wide = grads.reshape(blocks, slots, width).astype(jnp.float32)
        return (column * wide).astype(jnp.bfloat16).reshape(blocks * slots, width)

    weight_in, weight_out = w_in[0], w_out[0]
    bias_in = b_in[0].astype(jnp.float32)
    bias_out = b_out[0].astype(jnp.float32)
    d_sent = gated(recv_rows, grad_slots)
    pre_act = jnp.dot(recv_rows, weight_in, preferred_element_type=jnp.float32) + bias_in
    activated = gelu_value(pre_act).astype(jnp.bfloat16)
    expert_out = (
        jnp.dot(activated, weight_out, preferred_element_type=jnp.float32) + bias_out
    ).astype(jnp.bfloat16)
    d_pre = jnp.einsum(
        "cd,fd->cf", d_sent, weight_out, preferred_element_type=jnp.float32
    ) * gelu_slope(pre_act)
    d_expert_in = jnp.einsum(
        "cf,df->cd", d_pre.astype(jnp.bfloat16), weight_in, preferred_element_type=jnp.float32
    ).astype(jnp.bfloat16)
    returned = jnp.concatenate(exchange(split(expert_out)), axis=0)
    d_returned = jnp.concatenate(exchange(split(d_expert_in)), axis=0)

    units = hidden_units // groups
    share = width // groups
    rows_all = jnp.concatenate(recv_all, axis=0)
    sent_all = gated(rows_all, jnp.concatenate(grad_all, axis=0))
    my_in = lax.dynamic_slice_in_dim(weight_in, dp_me * units, units, 1)
    my_out = lax.dynamic_slice_in_dim(weight_out, dp_me * units, units, 0)
    my_bias = lax.dynamic_slice_in_dim(bias_in, dp_me * units, units, 0)
    pre_all = jnp.dot(rows_all, my_in, preferred_element_type=jnp.float32) + my_bias
    act_all = gelu_value(pre_all).astype(jnp.bfloat16)
    part_w_out = jnp.einsum("cf,cd->fd", act_all, sent_all, preferred_element_type=jnp.float32)
    d_pre_all = jnp.einsum(
        "cd,fd->cf", sent_all, my_out, preferred_element_type=jnp.float32
    ) * gelu_slope(pre_all)
    part_b_in = jnp.sum(d_pre_all, axis=0)
    d_pre_low = d_pre_all.astype(jnp.bfloat16)
    d_w_in = jnp.einsum("cd,cf->df", rows_all, d_pre_low, preferred_element_type=jnp.float32)
    sum_sent = jnp.sum(sent_all.astype(jnp.float32), axis=0)
    part_b_out = lax.dynamic_slice_in_dim(sum_sent, dp_me * share, share, 0)
    pieces = [lax.dynamic_slice_in_dim(d_w_in, dp_me * share, share, 0)]
    for mask in range(1, groups):
        piece = lax.dynamic_slice_in_dim(d_w_in, (dp_me ^ mask) * share, share, 0)
        pieces.append(swap(piece.astype(jnp.bfloat16), "dp", mask).astype(jnp.float32))
    part_w_in = in_order(pieces, dp_me, 1)

    def from_slots(hot, values):
        return jnp.dot(hot.astype(jnp.bfloat16), values, preferred_element_type=jnp.float32)

    picked_first = from_slots(hot_first, returned)
    picked_second = from_slots(hot_second, returned)
    block_out = (
        hidden + (first_gate[:, None] * picked_first + second_gate[:, None] * picked_second)
    ).astype(jnp.bfloat16)
    grad_out = d_out.astype(jnp.float32)
    d_gate_diff = jnp.sum(grad_out * picked_first, axis=-1) - jnp.sum(
        grad_out * picked_second, axis=-1
    )
    d_diff = d_gate_diff * first_gate * second_gate
    d_logits = (d_diff[:, None] * (route_hot[:, 0] - route_hot[:, 1])).astype(jnp.bfloat16)
    d_w_router = jnp.einsum("td,te->de", y_in, d_logits, preferred_element_type=jnp.float32)
    d_y = from_slots(hot_low, d_returned) + jnp.einsum(
        "te,de->td", d_logits, full_router, preferred_element_type=jnp.float32
    )
    d_gain_two = jnp.sum(d_y * normed_two, axis=0)
    d_bias_two = jnp.sum(d_y, axis=0)
    d_hidden = grad_out + norm_back(d_y, normed_two, inv_two, gain_two)
    d_b_proj = jnp.sum(d_hidden, axis=0)
    d_hidden_low = d_hidden.astype(jnp.bfloat16)
    d_w_proj = jnp.einsum("td,te->de", context, d_hidden_low, preferred_element_type=jnp.float32)
    d_context = jnp.einsum(
        "te,de->td", d_hidden_low, full_proj, preferred_element_type=jnp.float32
    ).astype(jnp.bfloat16)
    early_side = jnp.concatenate(
        [jnp.stack([d_b_proj, d_gain_two, d_bias_two], axis=1), d_w_router], axis=1
    )
    early_side = jnp.pad(early_side, ((0, 0), (0, 256 - early_side.shape[1])))
    early = reduce_all(jnp.concatenate([d_w_proj, early_side], axis=1))
    grad_heads = by_heads(d_context, images)
    probs = jnp.exp(
        jnp.einsum("bqhd,bkhd->bhqk", query_heads, key_heads, preferred_element_type=jnp.float32)
        * score_scale
        - log_total
    )
    d_probs = jnp.einsum(
        "bqhd,bkhd->bhqk", grad_heads, value_heads, preferred_element_type=jnp.float32
    )
    d_values = jnp.einsum(
        "bhqk,bqhd->bkhd",
        probs.astype(jnp.bfloat16),
        grad_heads,
        preferred_element_type=jnp.float32,
    ).reshape(tokens, width)
    row_delta = jnp.sum(probs * d_probs, axis=-1, keepdims=True)
    d_scores = (probs * (d_probs - row_delta) * score_scale).astype(jnp.bfloat16)
    d_queries = jnp.einsum(
        "bhqk,bkhd->bqhd", d_scores, key_heads, preferred_element_type=jnp.float32
    ).reshape(tokens, width)
    d_keys = jnp.einsum(
        "bhqk,bqhd->bkhd", d_scores, query_heads, preferred_element_type=jnp.float32
    ).reshape(tokens, width)
    d_b_q = jnp.sum(d_queries, axis=0)
    d_b_v = jnp.sum(d_values, axis=0)
    d_qkv = jnp.concatenate(
        [d_queries, d_keys, d_values, jnp.zeros((tokens, side), jnp.float32)], axis=1
    ).astype(jnp.bfloat16)
    d_w_qkv = jnp.einsum(
        "td,te->de", a_in, d_qkv[:, : 3 * width], preferred_element_type=jnp.float32
    )
    d_a = jnp.einsum("te,de->td", d_qkv, full_qkv, preferred_element_type=jnp.float32)
    d_gain_one = jnp.sum(d_a * normed_one, axis=0)
    d_bias_one = jnp.sum(d_a, axis=0)
    d_input = d_hidden + norm_back(d_a, normed_one, inv_one, gain_one)
    late_side = jnp.stack([d_b_q, d_b_v, d_gain_one, d_bias_one], axis=1)
    late_side = jnp.pad(late_side, ((0, 0), (0, 256 - late_side.shape[1])))
    late = reduce_all(jnp.concatenate([d_w_qkv, late_side], axis=1))
    return (
        block_out,
        d_input,
        late[:, : 3 * width],
        late[:, 3 * width],
        late[:, 3 * width + 1],
        early[:, :width],
        early[:, width],
        late[:, 3 * width + 2],
        late[:, 3 * width + 3],
        early[:, width + 1],
        early[:, width + 2],
        early[:, width + 3 : width + 3 + experts],
        part_w_in[None],
        part_b_in[None],
        part_w_out[None],
        part_b_out[None],
    )


def solution(mesh):
    return jax.shard_map(
        per_device,
        mesh=mesh,
        in_specs=(
            P(("dp", "expert"), None),
            P("dp", None),
            P("dp"),
            P("dp"),
            P("dp", None),
            P("dp"),
            P("dp"),
            P("dp"),
            P("dp"),
            P("dp"),
            P("dp", None),
            P("expert", None, None),
            P("expert", None),
            P("expert", None, None),
            P("expert", None),
            P(("dp", "expert"), None),
            P(("dp", "expert"), None),
            P(("dp", "expert"), None),
        ),
        out_specs=(
            P(("dp", "expert"), None),
            P(("dp", "expert"), None),
            P("dp", None),
            P("dp"),
            P("dp"),
            P("dp", None),
            P("dp"),
            P("dp"),
            P("dp"),
            P("dp"),
            P("dp"),
            P("dp", None),
            P("expert", "dp", None),
            P("expert", "dp"),
            P("expert", "dp", None),
            P("expert", "dp"),
        ),
        check_vma=False,
    )
```

```python
import functools
import math

import jax
import jax.numpy as jnp
from jax import lax
from jax.experimental import pallas as pl
from jax.experimental.pallas import tpu as pltpu
from jax.sharding import PartitionSpec as P

HEAD_DIM = 64
SEQ = 197


NORM_EPS = 1e-06
SQRT_HALF = 0.7071067811865476
INV_ROOT_TWO_PI = 0.3989422804014327


def normalize(values):
    center = values - jnp.mean(values, axis=-1, keepdims=True)
    inv_std = lax.rsqrt(jnp.mean(center * center, axis=-1, keepdims=True) + NORM_EPS)
    return (center * inv_std, inv_std)


def norm_back(grad_in, normed, inv_std, gain_vec):
    scaled = grad_in * gain_vec
    mean_plain = jnp.mean(scaled, axis=-1, keepdims=True)
    mean_mixed = jnp.mean(scaled * normed, axis=-1, keepdims=True)
    return inv_std * (scaled - mean_plain - normed * mean_mixed)


def gelu_value(pre_act):
    return 0.5 * pre_act * (1.0 + lax.erf(pre_act * SQRT_HALF))


def gelu_slope(pre_act):
    return 0.5 * (1.0 + lax.erf(pre_act * SQRT_HALF)) + pre_act * INV_ROOT_TWO_PI * jnp.exp(
        -0.5 * pre_act * pre_act
    )


def swap(values, axis, mask):
    size = lax.axis_size(axis)
    return lax.ppermute(values, axis, [(index, index ^ mask) for index in range(size)])


def gather_shared(shard):
    groups = lax.axis_size("dp")
    rows = shard.shape[0]
    if groups != 4:
        return [lax.all_gather(shard, "dp", axis=0, tiled=True)], [jnp.int32(0)]
    me = lax.axis_index("dp")
    core = lax.axis_index("expert") % 2
    half = rows // 2
    part = half // 2
    mine = lax.dynamic_slice_in_dim(shard, core * half, half, 0)
    from_one = swap(mine, "dp", 1)
    from_two = swap(mine, "dp", 2)
    far_low = swap(from_one[:part], "dp", 2)
    far_high = swap(from_two[part:], "dp", 1)
    other_one = swap(from_one, "expert", 1)
    other_two = swap(from_two, "expert", 1)
    other_low = swap(far_low, "expert", 1)
    other_high = swap(far_high, "expert", 1)
    base = core * half
    other = half - base
    one, two, far = (me ^ 1) * rows, (me ^ 2) * rows, (me ^ 3) * rows
    starts = [me * rows, one + base, two + base, far + base, far + base + part]
    starts += [one + other, two + other, far + other, far + other + part]
    pieces = [shard, from_one, from_two, far_low, far_high]
    pieces += [other_one, other_two, other_low, other_high]
    return pieces, starts


def gather_rows(rows):
    groups = lax.axis_size("dp")
    if groups != 4:
        return [rows] + [swap(rows, "dp", mask) for mask in range(1, groups)]
    half = rows.shape[0] // 2
    from_one = swap(rows, "dp", 1)
    from_two = swap(rows, "dp", 2)
    return [
        rows,
        from_one,
        from_two,
        swap(from_one[:half], "dp", 2),
        swap(from_two[half:], "dp", 1),
    ]


def exchange(blocks):
    return [blocks[0]] + [swap(blocks[mask], "expert", mask) for mask in range(1, len(blocks))]


def in_order(pieces, me, axis):
    stack = jnp.stack(pieces)
    return jnp.concatenate(
        [
            lax.dynamic_index_in_dim(stack, me ^ index, 0, keepdims=False)
            for index in range(len(pieces))
        ],
        axis=axis,
    )


VMEM = pl.BlockSpec(memory_space=pltpu.VMEM)
SMEM = pl.BlockSpec(memory_space=pltpu.SMEM)
NARROW = jnp.bfloat16
WIDE = jnp.float32
MIB = 1024 * 1024


def like(shape, dtype):
    return jax.ShapeDtypeStruct(shape, dtype)


def run(body, outs, operands, flops, moved, mib, scalars=0, scratch=(), name=None):
    return pl.pallas_call(
        body,
        out_shape=outs,
        in_specs=[SMEM] * scalars + [VMEM] * (len(operands) - scalars),
        out_specs=jax.tree.map(lambda _: VMEM, outs),
        scratch_shapes=list(scratch),
        compiler_params=pltpu.CompilerParams(vmem_limit_bytes=mib * MIB),
        cost_estimate=pl.CostEstimate(flops=flops, bytes_accessed=moved, transcendentals=0),
        name=name,
    )(*operands)


def mm(left, right):
    return jnp.dot(left, right, preferred_element_type=WIDE)


def mm_rows(left, right):
    return lax.dot_general(left, right, (((1,), (1,)), ((), ())), preferred_element_type=WIDE)


def mm_cols(left, right):
    return lax.dot_general(left, right, (((0,), (0,)), ((), ())), preferred_element_type=WIDE)


def head_masks(rows):
    lanes = lax.broadcasted_iota(jnp.int32, (rows, 2 * HEAD_DIM), 1)
    return [lanes < HEAD_DIM, lanes >= HEAD_DIM]


def join_body(count, *refs):
    out_ref, wide_ref = refs[count], refs[count + 1]
    at = 0
    for ref in refs[:count]:
        wide_ref[at : at + ref.shape[0], :] = ref[...].astype(WIDE)
        at += ref.shape[0]
    out_ref[...] = wide_ref[...].astype(NARROW)


def join(pieces):
    rows = sum(piece.shape[0] for piece in pieces)
    columns = pieces[0].shape[1]
    return run(
        functools.partial(join_body, len(pieces)),
        like((rows, columns), NARROW),
        pieces,
        rows * columns,
        4 * rows * columns,
        16,
        scratch=[pltpu.VMEM((rows, columns), WIDE)],
        name="join",
    )


def slot_rows(targets, total, tokens):
    ids = lax.broadcasted_iota(jnp.int32, (total, tokens), 0)
    return ids == targets[0:1, :], ids == targets[1:2, :]


def grad_slots_body(experts, d_ref, routes_ref, targets_ref, *outs):
    tokens, width = d_ref.shape
    slots = outs[0].shape[0]
    first, second = slot_rows(targets_ref[...], experts * slots, tokens)
    first, second = first.astype(NARROW), second.astype(NARROW)
    rows = mm(first + second, d_ref[...]).astype(NARROW)
    lanes = lax.broadcasted_iota(jnp.int32, (tokens, 128), 1)
    other_first = (lanes == routes_ref[:, 1:2]).astype(NARROW)
    other_second = (lanes == routes_ref[:, 0:1]).astype(NARROW)
    marks = (mm(first, other_first) + mm(second, other_second)).astype(NARROW)
    for index, out in enumerate(outs):
        out[:, :width] = rows[index * slots : (index + 1) * slots, :]
        out[:, width:] = marks[index * slots : (index + 1) * slots, :]


def attend_body(count, parts, *refs):
    starts_ref, x_ref, columns_ref = refs[0], refs[1], refs[2]
    pieces = refs[3 : 3 + count]
    full_ref, vec_ref, a_ref, qkv_ref, ctx_ref, lse_ref, asel_ref, csel_ref = refs[3 + count :]
    for index, piece in enumerate(pieces):
        rows = piece.shape[0]
        at = starts_ref[index] if count > 1 else 0
        if count > 1:
            at = pl.multiple_of(at, 16)
        full_ref[pl.ds(at, rows), :] = piece[...]
    tokens, width = x_ref.shape
    side = jnp.transpose(full_ref[:, 3 * width :].astype(WIDE))
    vec_ref[...] = side[: vec_ref.shape[0], :]
    bias_q, bias_v = vec_ref[0:1, :], vec_ref[1:2, :]
    gain, bias = vec_ref[3:4, :], vec_ref[4:5, :]
    normed, _ = normalize(x_ref[...].astype(WIDE))
    a_ref[...] = (normed * gain + bias).astype(NARROW)
    a_in = a_ref[...]
    qkv_ref[:, :width] = (mm(a_in, full_ref[:, :width]) + bias_q).astype(NARROW)
    qkv_ref[:, width : 2 * width] = mm(a_in, full_ref[:, width : 2 * width]).astype(NARROW)
    qkv_ref[:, 2 * width :] = (
        mm(a_in, full_ref[:, 2 * width : 3 * width]) + bias_v
    ).astype(NARROW)
    masks = head_masks(tokens)
    lanes = lax.broadcasted_iota(jnp.int32, (tokens, 128), 1)
    lse_all = jnp.zeros((tokens, 128), WIDE)
    pair = 2 * HEAD_DIM
    for group in range(width // pair):
        at = group * pair
        query = qkv_ref[:, at : at + pair]
        keys = qkv_ref[:, width + at : width + at + pair]
        values = qkv_ref[:, 2 * width + at : 2 * width + at + pair]
        outs = []
        for index in range(2):
            scores = mm_rows(jnp.where(masks[index], query, 0), keys) * (
                1.0 / math.sqrt(HEAD_DIM)
            )
            top = jnp.max(scores, axis=-1, keepdims=True)
            exps = jnp.exp(scores - top)
            total = jnp.sum(exps, axis=-1, keepdims=True)
            lse_all = jnp.where(lanes == 2 * group + index, top + jnp.log(total), lse_all)
            outs.append(mm((exps / total).astype(NARROW), values))
        ctx_ref[:, at : at + pair] = jnp.where(masks[0], outs[0], outs[1]).astype(NARROW)
    lse_ref[...] = lse_all
    ids = lax.broadcasted_iota(jnp.int32, (width, columns_ref.shape[1]), 0)
    hot = (ids == columns_ref[0:1, :]).astype(NARROW)
    asel_ref[...] = mm(a_in, hot).astype(NARROW)
    csel_ref[...] = mm(ctx_ref[...], hot).astype(NARROW)


def middle_body(count, experts, *refs):
    starts_ref, ctx_ref, x_ref, vec_ref, targets_ref = refs[:5]
    pieces = refs[5 : 5 + count]
    full_ref, hidden_ref, y_ref = refs[5 + count : 8 + count]
    outs = refs[8 + count :]
    for index, piece in enumerate(pieces):
        rows = piece.shape[0]
        at = starts_ref[index] if count > 1 else 0
        if count > 1:
            at = pl.multiple_of(at, 16)
        full_ref[pl.ds(at, rows), :] = piece[...]
    hidden = x_ref[...].astype(WIDE) + mm(ctx_ref[...], full_ref[...]) + vec_ref[2:3, :]
    hidden_ref[...] = hidden
    normed, _ = normalize(hidden)
    y_in = (normed * vec_ref[5:6, :] + vec_ref[6:7, :]).astype(NARROW)
    y_ref[...] = y_in
    slots = outs[0].shape[0]
    first, second = slot_rows(targets_ref[...], experts * slots, x_ref.shape[0])
    rows = mm((first | second).astype(NARROW), y_in).astype(NARROW)
    for index, out in enumerate(outs):
        out[...] = rows[index * slots : (index + 1) * slots, :]


def slot_gates(rows, marks, router, mine):
    logits = mm_rows(rows, router)
    lanes = lax.broadcasted_iota(jnp.int32, logits.shape, 1)
    own = jnp.sum(jnp.where(lanes == mine, logits, 0.0), axis=-1, keepdims=True)
    other = jnp.sum(
        marks[:, : logits.shape[1]].astype(WIDE) * logits, axis=-1, keepdims=True
    )
    return 1.0 / (1.0 + jnp.exp(other - own))


def gelu_parts(pre_act):
    half = 0.5 * (1.0 + lax.erf(pre_act * SQRT_HALF))
    slope = half + pre_act * INV_ROOT_TWO_PI * jnp.exp(-0.5 * pre_act * pre_act)
    return pre_act * half, slope


def expert_body(experts, me_ref, rows_ref, marked_ref, vec_ref, in_ref, bin_ref, out_ref, bout_ref, *refs):
    fresh = refs[:experts]
    back = refs[experts : 2 * experts]
    sent_ref, acc_ref, dacc_ref = refs[2 * experts :]
    step = pl.program_id(0)
    width = rows_ref.shape[1]

    @pl.when(step == 0)
    def _():
        router = vec_ref[8:32, :].astype(NARROW)
        gate = slot_gates(rows_ref[...], marked_ref[:, width:], router, me_ref[0])
        sent_ref[...] = (gate * marked_ref[:, :width].astype(WIDE)).astype(NARROW)
        acc_ref[...] = jnp.zeros_like(acc_ref)
        dacc_ref[...] = jnp.zeros_like(dacc_ref)

    weight_in, weight_out = in_ref[...], out_ref[...]
    pre_act = mm(rows_ref[...], weight_in) + bin_ref[...].astype(WIDE)
    act, slope = gelu_parts(pre_act)
    acc_ref[...] += mm(act.astype(NARROW), weight_out)
    d_pre = mm_rows(sent_ref[...], weight_out) * slope
    dacc_ref[...] += mm_rows(d_pre.astype(NARROW), weight_in)

    @pl.when(step == pl.num_programs(0) - 1)
    def _():
        bias = bout_ref[...].astype(WIDE)
        slots = fresh[0].shape[0]
        for index in range(experts):
            at = index * slots
            fresh[index][...] = (acc_ref[at : at + slots, :] + bias).astype(NARROW)
            back[index][...] = dacc_ref[at : at + slots, :].astype(NARROW)


def expert(me, rows, marked, vec, weight_in, b_in, weight_out, b_out, experts, slots, chunk):
    total, width = rows.shape
    hidden_units = weight_in.shape[1]
    whole = lambda array: pl.BlockSpec(array.shape, lambda step: (0, 0))
    block = like((slots, width), NARROW)
    return pl.pallas_call(
        functools.partial(expert_body, experts),
        grid=(hidden_units // chunk,),
        out_shape=[block] * (2 * experts),
        in_specs=[
            SMEM,
            whole(rows),
            whole(marked),
            whole(vec),
            pl.BlockSpec((width, chunk), lambda step: (0, step)),
            pl.BlockSpec((1, chunk), lambda step: (0, step)),
            pl.BlockSpec((chunk, width), lambda step: (step, 0)),
            whole(b_out),
        ],
        out_specs=[pl.BlockSpec((slots, width), lambda step: (0, 0))] * (2 * experts),
        scratch_shapes=[
            pltpu.VMEM((total, width), NARROW),
            pltpu.VMEM((total, width), WIDE),
            pltpu.VMEM((total, width), WIDE),
        ],
        compiler_params=pltpu.CompilerParams(vmem_limit_bytes=32 * MIB),
        cost_estimate=pl.CostEstimate(
            flops=8 * total * width * hidden_units,
            bytes_accessed=4 * width * hidden_units,
            transcendentals=0,
        ),
        name="expert",
    )(me, rows, marked, vec, weight_in, b_in, weight_out, b_out)


def weights_body(count, me_ref, vec_ref, in_ref, bin_ref, out_ref, *refs):
    rows_in, marked_in = refs[:count], refs[count : 2 * count]
    dout_ref, din_ref, dbin_ref, dbout_ref, rows_ref, sent_ref = refs[2 * count :]
    width = in_ref.shape[0]

    @pl.when(pl.program_id(0) == 0)
    def _():
        router = vec_ref[8:32, :].astype(NARROW)
        at = 0
        total = jnp.zeros((1, width), WIDE)
        for rows, marked in zip(rows_in, marked_in):
            size = rows.shape[0]
            gate = slot_gates(rows[...], marked[:, width:], router, me_ref[0])
            sent = (gate * marked[:, :width].astype(WIDE)).astype(NARROW)
            rows_ref[at : at + size, :] = rows[...]
            sent_ref[at : at + size, :] = sent
            total += jnp.sum(sent.astype(WIDE), axis=0, keepdims=True)
            at += size
        dbout_ref[...] = total

    pre_act = mm(rows_ref[...], in_ref[...]) + bin_ref[...].astype(WIDE)
    act, slope = gelu_parts(pre_act)
    dout_ref[...] = mm_cols(act.astype(NARROW), sent_ref[...])
    d_pre = mm_rows(sent_ref[...], out_ref[...]) * slope
    dbin_ref[...] = jnp.sum(d_pre, axis=0, keepdims=True)
    din_ref[...] = mm_cols(rows_ref[...], d_pre.astype(NARROW))


def expert_weights(me, vec, my_in, my_bias, my_out, rows, marked, chunk):
    count = len(rows)
    width, units = my_in.shape
    total = sum(piece.shape[0] for piece in rows)
    whole = lambda array: pl.BlockSpec(array.shape, lambda step: (0, 0))
    return pl.pallas_call(
        functools.partial(weights_body, count),
        grid=(units // chunk,),
        out_shape=[
            like((units, width), WIDE),
            like((width, units), WIDE),
            like((1, units), WIDE),
            like((1, width), WIDE),
        ],
        in_specs=[
            SMEM,
            whole(vec),
            pl.BlockSpec((width, chunk), lambda step: (0, step)),
            pl.BlockSpec((1, chunk), lambda step: (0, step)),
            pl.BlockSpec((chunk, width), lambda step: (step, 0)),
        ]
        + [whole(piece) for piece in rows + marked],
        out_specs=[
            pl.BlockSpec((chunk, width), lambda step: (step, 0)),
            pl.BlockSpec((width, chunk), lambda step: (0, step)),
            pl.BlockSpec((1, chunk), lambda step: (0, step)),
            pl.BlockSpec((1, width), lambda step: (0, 0)),
        ],
        scratch_shapes=[
            pltpu.VMEM((total, width), NARROW),
            pltpu.VMEM((total, width), NARROW),
        ],
        compiler_params=pltpu.CompilerParams(vmem_limit_bytes=(36 if count < 8 else 60) * MIB),
        cost_estimate=pl.CostEstimate(
            flops=8 * total * width * units,
            bytes_accessed=16 * total * width,
            transcendentals=0,
        ),
        name="expert_weights",
    )(me, vec, my_in, my_bias, my_out, *rows, *marked)


def combine_body(experts, *refs):
    hidden_ref, y_ref, d_ref, vec_ref, full_ref, routes_ref, targets_ref = refs[:7]
    fresh = refs[7 : 7 + experts]
    back = refs[7 + experts : 7 + 2 * experts]
    out_ref, dh_ref, dhlow_ref, dctx_ref, sums_ref, ret_ref, dret_ref = refs[7 + 2 * experts :]
    tokens, width = hidden_ref.shape
    slots = fresh[0].shape[0]
    for index in range(experts):
        at = index * slots
        ret_ref[at : at + slots, :] = fresh[index][...].astype(WIDE)
        dret_ref[at : at + slots, :] = back[index][...].astype(WIDE)
    lanes = lax.broadcasted_iota(jnp.int32, (tokens, experts * slots), 1)
    first = lanes == targets_ref[:, 0:1]
    second = lanes == targets_ref[:, 1:2]
    returned = ret_ref[...].astype(NARROW)
    picked_first = mm(first.astype(NARROW), returned)
    picked_second = mm(second.astype(NARROW), returned)
    router = vec_ref[8:32, :].astype(NARROW)
    y_in = y_ref[...]
    logits = mm_rows(y_in, router)
    names = lax.broadcasted_iota(jnp.int32, logits.shape, 1)
    hot_first = (names == routes_ref[:, 0:1]).astype(WIDE)
    hot_second = (names == routes_ref[:, 1:2]).astype(WIDE)
    chosen_first = jnp.sum(logits * hot_first, axis=-1, keepdims=True)
    chosen_second = jnp.sum(logits * hot_second, axis=-1, keepdims=True)
    gate_first = 1.0 / (1.0 + jnp.exp(chosen_second - chosen_first))
    gate_second = 1.0 - gate_first
    hidden = hidden_ref[...]
    out_ref[...] = (
        hidden + (gate_first * picked_first + gate_second * picked_second)
    ).astype(NARROW)
    grad = d_ref[...].astype(WIDE)
    d_gate = jnp.sum(grad * picked_first, axis=-1, keepdims=True) - jnp.sum(
        grad * picked_second, axis=-1, keepdims=True
    )
    d_diff = d_gate * gate_first * gate_second
    d_logits = (d_diff * (hot_first - hot_second)).astype(NARROW)
    sums_ref[8:32, :] = mm_cols(d_logits, y_in)
    d_y = mm((first | second).astype(NARROW), dret_ref[...].astype(NARROW)) + mm(
        d_logits, router
    )
    normed, inv_std = normalize(hidden)
    d_hidden = grad + norm_back(d_y, normed, inv_std, vec_ref[5:6, :])
    sums_ref[0:8, :] = jnp.zeros((8, width), WIDE)
    sums_ref[0:1, :] = jnp.sum(d_hidden, axis=0, keepdims=True)
    sums_ref[1:2, :] = jnp.sum(d_y * normed, axis=0, keepdims=True)
    sums_ref[2:3, :] = jnp.sum(d_y, axis=0, keepdims=True)
    dh_ref[...] = d_hidden
    low = d_hidden.astype(NARROW)
    dhlow_ref[...] = low
    dctx_ref[...] = mm_rows(low, full_ref[...]).astype(NARROW)


def attend_back_body(start, qkv_ref, dctx_ref, lse_ref, out_ref, sums_ref):
    tokens = qkv_ref.shape[0]
    width = dctx_ref.shape[1]
    columns = out_ref.shape[1] // 3
    masks = head_masks(tokens)
    lanes = lax.broadcasted_iota(jnp.int32, (tokens, 128), 1)
    pair = 2 * HEAD_DIM
    scale = 1.0 / math.sqrt(HEAD_DIM)
    sums_ref[...] = jnp.zeros_like(sums_ref)
    for group in range(columns // pair):
        to = group * pair
        at = start + to
        query = qkv_ref[:, at : at + pair]
        keys = qkv_ref[:, width + at : width + at + pair]
        values = qkv_ref[:, 2 * width + at : 2 * width + at + pair]
        grads = dctx_ref[:, at : at + pair]
        d_query = d_keys = d_values = None
        for index in range(2):
            zero = jnp.zeros_like(query)
            query_h = jnp.where(masks[index], query, zero)
            keys_h = jnp.where(masks[index], keys, zero)
            grads_h = jnp.where(masks[index], grads, zero)
            head = (start + to) // HEAD_DIM + index
            lse = jnp.sum(jnp.where(lanes == head, lse_ref[...], 0.0), axis=-1, keepdims=True)
            probs = jnp.exp(mm_rows(query_h, keys) * scale - lse)
            d_probs = mm_rows(grads_h, values)
            delta = jnp.sum(probs * d_probs, axis=-1, keepdims=True)
            d_scores = (probs * (d_probs - delta) * scale).astype(NARROW)
            new_values = mm_cols(probs.astype(NARROW), grads_h)
            new_query = mm(d_scores, keys_h)
            new_keys = mm_cols(d_scores, query_h)
            d_values = new_values if d_values is None else d_values + new_values
            d_query = new_query if d_query is None else d_query + new_query
            d_keys = new_keys if d_keys is None else d_keys + new_keys
        out_ref[:, to : to + pair] = d_query.astype(NARROW)
        out_ref[:, columns + to : columns + to + pair] = d_keys.astype(NARROW)
        out_ref[:, 2 * columns + to : 2 * columns + to + pair] = d_values.astype(NARROW)
        sums_ref[0:1, to : to + pair] = jnp.sum(d_query, axis=0, keepdims=True)
        sums_ref[1:2, to : to + pair] = jnp.sum(d_values, axis=0, keepdims=True)


def finish_body(low_ref, high_ref, full_ref, x_ref, vec_ref, dh_ref, dx_ref, sums_ref):
    width = x_ref.shape[1]
    columns = low_ref.shape[1] // 3
    d_a = None
    for half, ref in enumerate((low_ref, high_ref)):
        for third in range(3):
            at = third * width + half * columns
            new = mm_rows(
                ref[:, third * columns : (third + 1) * columns], full_ref[:, at : at + columns]
            )
            d_a = new if d_a is None else d_a + new
    normed, inv_std = normalize(x_ref[...].astype(WIDE))
    sums_ref[...] = jnp.zeros_like(sums_ref)
    sums_ref[0:1, :] = jnp.sum(d_a * normed, axis=0, keepdims=True)
    sums_ref[1:2, :] = jnp.sum(d_a, axis=0, keepdims=True)
    dx_ref[...] = dh_ref[...] + norm_back(d_a, normed, inv_std, vec_ref[3:4, :])


def outer_body(groups, left_ref, left_other_ref, right_ref, right_other_ref, own_ref, *outs):
    rows = own_ref.shape[0]
    total = mm_cols(left_ref[...], right_ref[...]) + mm_cols(
        left_other_ref[...], right_other_ref[...]
    )
    own_ref[...] = total[:rows, :]
    for index in range(1, groups):
        outs[index - 1][...] = total[index * rows : (index + 1) * rows, :].astype(NARROW)


def outer(left, left_other, right, right_other, groups):
    tokens, rows = left.shape
    columns = right.shape[1]
    block = rows // groups
    return run(
        functools.partial(outer_body, groups),
        [like((block, columns), WIDE)] + [like((block, columns), NARROW)] * (groups - 1),
        [left, left_other, right, right_other],
        4 * tokens * rows * columns,
        6 * rows * columns,
        24,
        name="outer",
    )


def reduce_blocks(own, others):
    layers = lax.axis_size("expert") // 2
    total = own
    for mask, block in enumerate(others, 1):
        total = total + swap(block, "dp", mask).astype(WIDE)
    part = own.shape[0] // layers
    done = total[:part]
    low = total.astype(NARROW)
    for mask in range(1, layers):
        piece = swap(low[mask * part : (mask + 1) * part], "expert", 2 * mask)
        done = done + piece.astype(WIDE)
    done = done.astype(NARROW)
    return jnp.concatenate(
        [done] + [swap(done, "expert", 2 * mask) for mask in range(1, layers)], axis=0
    )


def expert_weights_plain(me, vec, my_in, my_bias, my_out, rows, marked):
    rows, marked = jnp.concatenate(rows, axis=0), jnp.concatenate(marked, axis=0)
    width = rows.shape[1]
    gate = slot_gates(rows, marked[:, width:], vec[8:32].astype(NARROW), me)
    sent = (gate * marked[:, :width].astype(WIDE)).astype(NARROW)
    act, slope = gelu_parts(mm(rows, my_in) + my_bias.astype(WIDE))
    d_pre = mm_rows(sent, my_out) * slope
    return (
        mm_cols(act.astype(NARROW), sent),
        mm_cols(rows, d_pre.astype(NARROW)),
        jnp.sum(d_pre, axis=0, keepdims=True),
        jnp.sum(sent.astype(WIDE), axis=0, keepdims=True),
    )


def per_device(
    block_input,
    w_qkv,
    b_q,
    b_v,
    w_proj,
    b_proj,
    ln1_gain,
    ln1_bias,
    ln2_gain,
    ln2_bias,
    w_router,
    w_in,
    b_in,
    w_out,
    b_out,
    routes,
    slot_index,
    d_out,
):
    tokens, width = block_input.shape
    hidden_units = w_in.shape[2]
    experts = w_in.shape[0] * lax.axis_size("expert")
    groups = lax.axis_size("dp")
    layers = lax.axis_size("expert") // 2
    capacity = 2 * tokens // experts
    slots = -(-capacity // 8) * 8
    dp_me = lax.axis_index("dp")
    expert_me = lax.axis_index("expert")
    core, layer = expert_me % 2, expert_me // 2
    vectors = jnp.stack([b_q, b_v, b_proj, ln1_gain, ln1_bias, ln2_gain, ln2_bias], axis=1)
    side_cols = jnp.concatenate([vectors, jnp.zeros_like(vectors[:, :1]), w_router], axis=1)
    side_cols = jnp.pad(side_cols, ((0, 0), (0, 128 - side_cols.shape[1])))
    qkv_pieces, qkv_starts = gather_shared(jnp.concatenate([w_qkv, side_cols], axis=1))
    proj_pieces, proj_starts = gather_shared(w_proj)
    starts = jnp.stack(qkv_starts).astype(jnp.int32)
    me = expert_me.reshape(1).astype(jnp.int32)
    targets = jnp.where(slot_index < capacity, (routes ^ expert_me) * slots + slot_index, -1)
    targets_row = targets.T
    share = width // groups
    part = share // (2 * layers)
    order = jnp.arange(width // 2, dtype=jnp.int32)
    group_of = order // (share // 2)
    layer_of = order // part % layers
    spot = (group_of ^ dp_me) * share + (layer_of ^ layer) * part + order % part
    chosen_columns = jnp.concatenate(
        [spot + core * (share // 2), spot + (1 - core) * (share // 2)]
    )[None].astype(jnp.int32)

    total = experts * slots
    marked_blocks = run(
        functools.partial(grad_slots_body, experts),
        [like((slots, width + 128), NARROW)] * experts,
        [d_out, routes, targets_row],
        2 * total * tokens * width,
        4 * total * width,
        16,
        name="grad_slots",
    )
    marked = join(exchange(marked_blocks))
    marked_all = gather_rows(marked)

    count = len(qkv_pieces)
    wide = w_qkv.shape[1] + 128
    full_qkv, vec, a_in, qkv, context, log_total, a_sel, ctx_sel = run(
        functools.partial(attend_body, count, part),
        [
            like((width, wide), NARROW),
            like((32, width), WIDE),
            like((tokens, width), NARROW),
            like((tokens, 3 * width), NARROW),
            like((tokens, width), NARROW),
            like((tokens, 128), WIDE),
            like((tokens, width), NARROW),
            like((tokens, width), NARROW),
        ],
        [starts, block_input, chosen_columns] + qkv_pieces,
        10 * tokens * width * width,
        4 * width * wide,
        40,
        scalars=1,
        name="attend",
    )
    half = width // 2
    a_keep, ctx_keep = a_sel[:, :half], ctx_sel[:, :half]
    a_other = swap(a_sel[:, half:], "expert", 1)
    ctx_other = swap(ctx_sel[:, half:], "expert", 1)
    middle = run(
        functools.partial(middle_body, count, experts),
        [
            like((width, width), NARROW),
            like((tokens, width), WIDE),
            like((tokens, width), NARROW),
        ]
        + [like((slots, width), NARROW)] * experts,
        [jnp.stack(proj_starts).astype(jnp.int32), context, block_input, vec, targets_row]
        + proj_pieces,
        4 * tokens * width * width,
        4 * width * width,
        24,
        scalars=1,
        name="middle",
    )
    full_proj, hidden, y_in = middle[:3]
    rows = join(exchange(middle[3:]))
    rows_all = gather_rows(rows)
    weight_in, weight_out = w_in[0], w_out[0]
    results = expert(
        me, rows, marked, vec, weight_in, b_in, weight_out, b_out, experts, slots, 512
    )
    d_returned = exchange(results[experts:])
    returned = exchange(results[:experts])

    units = hidden_units // groups
    my_in = lax.dynamic_slice_in_dim(weight_in, dp_me * units, units, 1)
    my_out = lax.dynamic_slice_in_dim(weight_out, dp_me * units, units, 0)
    my_bias = lax.dynamic_slice_in_dim(b_in, dp_me * units, units, 1)
    if groups == 4:
        part_w_out, d_w_in, part_b_in, sum_sent = expert_weights(
            me, vec, my_in, my_bias, my_out, rows_all, marked_all, 256
        )
    else:
        part_w_out, d_w_in, part_b_in, sum_sent = expert_weights_plain(
            expert_me, vec, my_in, my_bias, my_out, rows_all, marked_all
        )
    part_b_out = lax.dynamic_slice_in_dim(sum_sent[0], dp_me * share, share, 0)
    pieces = [lax.dynamic_slice_in_dim(d_w_in, dp_me * share, share, 0)]
    for mask in range(1, groups):
        piece = lax.dynamic_slice_in_dim(d_w_in, (dp_me ^ mask) * share, share, 0)
        pieces.append(swap(piece.astype(NARROW), "dp", mask).astype(WIDE))
    part_w_in = in_order(pieces, dp_me, 1)

    block_out, d_hidden, d_hidden_low, d_context, early_sums = run(
        functools.partial(combine_body, experts),
        [
            like((tokens, width), NARROW),
            like((tokens, width), WIDE),
            like((tokens, width), NARROW),
            like((tokens, width), NARROW),
            like((32, width), WIDE),
        ],
        [hidden, y_in, d_out, vec, full_proj, routes, targets] + returned + d_returned,
        6 * tokens * total * width + 2 * tokens * width * width,
        4 * width * width,
        24,
        scratch=[pltpu.VMEM((total, width), WIDE)] * 2,
        name="combine",
    )
    hidden_other = swap(d_hidden_low, "expert", 1)
    proj_blocks = outer(ctx_keep, ctx_other, d_hidden_low, hidden_other, groups)
    proj_sum = reduce_blocks(proj_blocks[0], proj_blocks[1:])

    def back(start):
        return run(
            functools.partial(attend_back_body, start),
            [like((tokens, 3 * half), NARROW), like((8, half), WIDE)],
            [qkv, d_context, log_total],
            16 * tokens * 256 * width,
            8 * tokens * width,
            24,
            name="attend_back",
        )

    d_low, low_sums = back(0)
    low_other = swap(d_low, "expert", 1)
    d_high, high_sums = back(half)
    high_other = swap(d_high, "expert", 1)
    low_blocks = outer(a_keep, a_other, d_low, low_other, groups)
    low_sum = reduce_blocks(low_blocks[0], low_blocks[1:])
    high_blocks = outer(a_keep, a_other, d_high, high_other, groups)
    high_sum = reduce_blocks(high_blocks[0], high_blocks[1:])
    d_input, late_sums = run(
        finish_body,
        [like((tokens, width), WIDE), like((8, width), WIDE)],
        [d_low, d_high, full_qkv, block_input, vec, d_hidden],
        6 * tokens * width * width,
        6 * width * width,
        24,
        name="finish",
    )
    sums = jnp.concatenate(
        [
            early_sums[:3],
            jnp.concatenate([low_sums[:2], high_sums[:2]], axis=1),
            late_sums[:2],
            jnp.zeros((1, width), WIDE),
            early_sums[8 : 8 + experts],
        ],
        axis=0,
    )
    vector_sum = lax.dynamic_slice_in_dim(sums, dp_me * share, share, 1)
    for mask in range(1, groups):
        piece = lax.dynamic_slice_in_dim(sums, (dp_me ^ mask) * share, share, 1)
        vector_sum = vector_sum + swap(piece, "dp", mask)
    for mask in range(layers.bit_length() - 1):
        vector_sum = vector_sum + swap(vector_sum, "expert", 2 << mask)
    vector_sum = vector_sum + swap(vector_sum, "expert", 1)

    gathered = jnp.concatenate([proj_sum, low_sum, high_sum], axis=1)
    gathered = jnp.concatenate([gathered, swap(gathered, "expert", 1)], axis=0)
    place = jnp.arange(share // 2, dtype=jnp.int32)
    place = (place // part ^ layer) * part + place % part
    place = jnp.concatenate([place + core * (share // 2), place + (1 - core) * (share // 2)])
    hot = (jnp.arange(share, dtype=jnp.int32)[:, None] == place[None, :]).astype(NARROW)
    ordered = jnp.dot(hot, gathered, preferred_element_type=WIDE)
    third = half
    columns = [
        ordered[:, width + side * 3 * third + index * third :][:, :third]
        for index in range(3)
        for side in range(2)
    ]
    return (
        block_out,
        d_input,
        jnp.concatenate(columns, axis=1),
        vector_sum[3],
        vector_sum[4],
        ordered[:, :width],
        vector_sum[0],
        vector_sum[5],
        vector_sum[6],
        vector_sum[1],
        vector_sum[2],
        vector_sum[8 : 8 + experts].T,
        part_w_in[None],
        part_b_in,
        part_w_out[None],
        part_b_out[None],
    )


def solution(mesh):
    return jax.shard_map(
        per_device,
        mesh=mesh,
        in_specs=(
            P(("dp", "expert"), None),
            P("dp", None),
            P("dp"),
            P("dp"),
            P("dp", None),
            P("dp"),
            P("dp"),
            P("dp"),
            P("dp"),
            P("dp"),
            P("dp", None),
            P("expert", None, None),
            P("expert", None),
            P("expert", None, None),
            P("expert", None),
            P(("dp", "expert"), None),
            P(("dp", "expert"), None),
            P(("dp", "expert"), None),
        ),
        out_specs=(
            P(("dp", "expert"), None),
            P(("dp", "expert"), None),
            P("dp", None),
            P("dp"),
            P("dp"),
            P("dp", None),
            P("dp"),
            P("dp"),
            P("dp"),
            P("dp"),
            P("dp"),
            P("dp", None),
            P("expert", "dp", None),
            P("expert", "dp"),
            P("expert", "dp", None),
            P("expert", "dp"),
        ),
        check_vma=False,
    )
```

```python
import functools
import math

import jax
import jax.numpy as jnp
from jax import lax
from jax.experimental import pallas as pl
from jax.experimental.pallas import tpu as pltpu
from jax.sharding import PartitionSpec as P

HEAD_DIM = 64
SEQ = 197


NORM_EPS = 1e-06
SQRT_HALF = 0.7071067811865476
INV_ROOT_TWO_PI = 0.3989422804014327


def normalize(values):
    center = values - jnp.mean(values, axis=-1, keepdims=True)
    inv_std = lax.rsqrt(jnp.mean(center * center, axis=-1, keepdims=True) + NORM_EPS)
    return (center * inv_std, inv_std)


def norm_back(grad_in, normed, inv_std, gain_vec):
    scaled = grad_in * gain_vec
    mean_plain = jnp.mean(scaled, axis=-1, keepdims=True)
    mean_mixed = jnp.mean(scaled * normed, axis=-1, keepdims=True)
    return inv_std * (scaled - mean_plain - normed * mean_mixed)


def gelu_value(pre_act):
    return 0.5 * pre_act * (1.0 + lax.erf(pre_act * SQRT_HALF))


def gelu_slope(pre_act):
    return 0.5 * (1.0 + lax.erf(pre_act * SQRT_HALF)) + pre_act * INV_ROOT_TWO_PI * jnp.exp(
        -0.5 * pre_act * pre_act
    )


def swap(values, axis, mask):
    size = lax.axis_size(axis)
    return lax.ppermute(values, axis, [(index, index ^ mask) for index in range(size)])


def gather_shared(shard, mine):
    groups = lax.axis_size("dp")
    rows = shard.shape[0]
    if groups != 4:
        return [lax.all_gather(shard, "dp", axis=0, tiled=True)], [jnp.int32(0)]
    me = lax.axis_index("dp")
    core = lax.axis_index("expert") % 2
    half = rows // 2
    part = half // 2
    from_one = swap(mine, "dp", 1)
    from_two = swap(mine, "dp", 2)
    far_low = swap(from_one[:part], "dp", 2)
    far_high = swap(from_two[part:], "dp", 1)
    other_one = swap(from_one, "expert", 1)
    other_two = swap(from_two, "expert", 1)
    other_low = swap(far_low, "expert", 1)
    other_high = swap(far_high, "expert", 1)
    base = core * half
    other = half - base
    one, two, far = (me ^ 1) * rows, (me ^ 2) * rows, (me ^ 3) * rows
    starts = [me * rows, one + base, two + base, far + base, far + base + part]
    starts += [one + other, two + other, far + other, far + other + part]
    pieces = [shard, from_one, from_two, far_low, far_high]
    pieces += [other_one, other_two, other_low, other_high]
    return pieces, starts


def after(values, *marks):
    return lax.optimization_barrier((values, marks))[0]


def gather_rows(rows, first_mark, second_mark):
    groups = lax.axis_size("dp")
    rows_later = after(rows, first_mark)
    if groups != 4:
        return [rows] + [swap(rows_later, "dp", mask) for mask in range(1, groups)]
    half = rows.shape[0] // 2
    from_one = swap(rows_later, "dp", 1)
    from_two = swap(rows_later, "dp", 2)
    one, two = after((from_one, from_two), second_mark)
    return [rows, one, two, swap(one[:half], "dp", 2), swap(two[half:], "dp", 1)]


def exchange(blocks):
    return [blocks[0]] + [swap(blocks[mask], "expert", mask) for mask in range(1, len(blocks))]


def in_order(pieces, me, axis):
    stack = jnp.stack(pieces)
    return jnp.concatenate(
        [
            lax.dynamic_index_in_dim(stack, me ^ index, 0, keepdims=False)
            for index in range(len(pieces))
        ],
        axis=axis,
    )


VMEM = pl.BlockSpec(memory_space=pltpu.VMEM)
SMEM = pl.BlockSpec(memory_space=pltpu.SMEM)
NARROW = jnp.bfloat16
WIDE = jnp.float32
MIB = 1024 * 1024


def like(shape, dtype):
    return jax.ShapeDtypeStruct(shape, dtype)


def run(body, outs, operands, flops, moved, mib, scalars=0, scratch=(), name=None):
    return pl.pallas_call(
        body,
        out_shape=outs,
        in_specs=[SMEM] * scalars + [VMEM] * (len(operands) - scalars),
        out_specs=jax.tree.map(lambda _: VMEM, outs),
        scratch_shapes=list(scratch),
        compiler_params=pltpu.CompilerParams(vmem_limit_bytes=mib * MIB),
        cost_estimate=pl.CostEstimate(flops=1, bytes_accessed=1, transcendentals=0),
        name=name,
    )(*operands)


def mm(left, right):
    return jnp.dot(left, right, preferred_element_type=WIDE)


def mm_rows(left, right):
    return lax.dot_general(left, right, (((1,), (1,)), ((), ())), preferred_element_type=WIDE)


def mm_cols(left, right):
    return lax.dot_general(left, right, (((0,), (0,)), ((), ())), preferred_element_type=WIDE)


def head_masks(rows):
    lanes = lax.broadcasted_iota(jnp.int32, (rows, 2 * HEAD_DIM), 1)
    return [lanes < HEAD_DIM, lanes >= HEAD_DIM]


def join_body(count, *refs):
    out_ref, wide_ref = refs[count], refs[count + 1]
    at = 0
    for ref in refs[:count]:
        wide_ref[at : at + ref.shape[0], :] = ref[...].astype(WIDE)
        at += ref.shape[0]
    out_ref[...] = wide_ref[...].astype(NARROW)


def join(pieces):
    rows = sum(piece.shape[0] for piece in pieces)
    columns = pieces[0].shape[1]
    return run(
        functools.partial(join_body, len(pieces)),
        like((rows, columns), NARROW),
        pieces,
        rows * columns,
        4 * rows * columns,
        16,
        scratch=[pltpu.VMEM((rows, columns), WIDE)],
        name="join",
    )


def slot_rows(targets, total, tokens):
    ids = lax.broadcasted_iota(jnp.int32, (total, tokens), 0)
    return ids == targets[0:1, :], ids == targets[1:2, :]


def grad_slots_body(experts, d_ref, routes_ref, targets_ref, out_ref):
    tokens, width = d_ref.shape
    slots = out_ref.shape[1]
    first, second = slot_rows(targets_ref[...], experts * slots, tokens)
    first, second = first.astype(NARROW), second.astype(NARROW)
    rows = mm(first + second, d_ref[...]).astype(NARROW)
    lanes = lax.broadcasted_iota(jnp.int32, (tokens, 128), 1)
    other_first = (lanes == routes_ref[:, 1:2]).astype(NARROW)
    other_second = (lanes == routes_ref[:, 0:1]).astype(NARROW)
    marks = (mm(first, other_first) + mm(second, other_second)).astype(NARROW)
    for index in range(experts):
        out_ref[index, :, :width] = rows[index * slots : (index + 1) * slots, :]
        out_ref[index, :, width:] = marks[index * slots : (index + 1) * slots, :]


def order_body(me_ref, blocks_ref, out_ref, wide_ref):
    experts, slots, _ = blocks_ref.shape
    for index in range(experts):
        at = index * slots
        wide_ref[at : at + slots, :] = blocks_ref[me_ref[0] ^ index].astype(WIDE)
    out_ref[...] = wide_ref[...].astype(NARROW)


def attend_body(count, *refs):
    starts_ref, x_ref, columns_ref = refs[0], refs[1], refs[2]
    pieces = refs[3 : 3 + count]
    full_ref, proj_ref, vec_ref, qkv_ref, ctx_ref, lse_ref, keep_ref, give_ref = refs[
        3 + count : 11 + count
    ]
    side_ref = refs[11 + count]
    tokens, width = x_ref.shape
    for index, piece in enumerate(pieces):
        rows = piece.shape[0]
        at = starts_ref[index] if count > 1 else 0
        if count > 1:
            at = pl.multiple_of(at, 16)
        full_ref[pl.ds(at, rows), :] = piece[:, : 3 * width]
        proj_ref[pl.ds(at, rows), :] = piece[:, 3 * width : 4 * width]
        side_ref[pl.ds(at, rows), :] = piece[:, 4 * width :]
    side = jnp.transpose(side_ref[...].astype(WIDE))
    vec_ref[...] = side[: vec_ref.shape[0], :]
    bias_q, bias_v = vec_ref[0:1, :], vec_ref[1:2, :]
    gain, bias = vec_ref[3:4, :], vec_ref[4:5, :]
    normed, _ = normalize(x_ref[...].astype(WIDE))
    a_in = (normed * gain + bias).astype(NARROW)
    qkv_ref[:, :width] = (mm(a_in, full_ref[:, :width]) + bias_q).astype(NARROW)
    qkv_ref[:, width : 2 * width] = mm(a_in, full_ref[:, width : 2 * width]).astype(NARROW)
    qkv_ref[:, 2 * width :] = (
        mm(a_in, full_ref[:, 2 * width : 3 * width]) + bias_v
    ).astype(NARROW)
    masks = head_masks(tokens)
    lanes = lax.broadcasted_iota(jnp.int32, (tokens, 128), 1)
    lse_all = jnp.zeros((tokens, 128), WIDE)
    pair = 2 * HEAD_DIM
    for group in range(width // pair):
        at = group * pair
        query = qkv_ref[:, at : at + pair]
        keys = qkv_ref[:, width + at : width + at + pair]
        values = qkv_ref[:, 2 * width + at : 2 * width + at + pair]
        outs = []
        for index in range(2):
            scores = mm_rows(jnp.where(masks[index], query, 0), keys) * (
                1.0 / math.sqrt(HEAD_DIM)
            )
            top = jnp.max(scores, axis=-1, keepdims=True)
            exps = jnp.exp(scores - top)
            total = jnp.sum(exps, axis=-1, keepdims=True)
            lse_all = jnp.where(lanes == 2 * group + index, top + jnp.log(total), lse_all)
            outs.append(mm((exps / total).astype(NARROW), values))
        ctx_ref[:, at : at + pair] = jnp.where(masks[0], outs[0], outs[1]).astype(NARROW)
    lse_ref[...] = lse_all
    ids = lax.broadcasted_iota(jnp.int32, (width, columns_ref.shape[1]), 0)
    hot = (ids == columns_ref[0:1, :]).astype(NARROW)
    half = width // 2
    chosen = mm(a_in, hot).astype(NARROW)
    keep_ref[:, :half] = chosen[:, :half]
    give_ref[:, :half] = chosen[:, half:]
    chosen = mm(ctx_ref[...], hot).astype(NARROW)
    keep_ref[:, half:] = chosen[:, :half]
    give_ref[:, half:] = chosen[:, half:]


def middle_body(experts, ctx_ref, x_ref, vec_ref, targets_ref, full_ref, hidden_ref, y_ref, *outs):
    hidden = x_ref[...].astype(WIDE) + mm(ctx_ref[...], full_ref[...]) + vec_ref[2:3, :]
    hidden_ref[...] = hidden
    normed, _ = normalize(hidden)
    y_in = (normed * vec_ref[5:6, :] + vec_ref[6:7, :]).astype(NARROW)
    y_ref[...] = y_in
    slots = outs[0].shape[0]
    first, second = slot_rows(targets_ref[...], experts * slots, x_ref.shape[0])
    rows = mm((first | second).astype(NARROW), y_in).astype(NARROW)
    for index, out in enumerate(outs):
        out[...] = rows[index * slots : (index + 1) * slots, :]


def in_terms(values):
    high = values.astype(NARROW)
    rest = values - high.astype(WIDE)
    middle = rest.astype(NARROW)
    return high, middle, (rest - middle.astype(WIDE)).astype(NARROW)


def slot_gates(rows, marks, router, mine):
    logits = mm_rows(rows, router)
    lanes = lax.broadcasted_iota(jnp.int32, logits.shape, 1)
    own = jnp.sum(jnp.where(lanes == mine, logits, 0.0), axis=-1, keepdims=True)
    other = jnp.sum(
        marks[:, : logits.shape[1]].astype(WIDE) * logits, axis=-1, keepdims=True
    )
    return 1.0 / (1.0 + jnp.exp(other - own))


def gelu_parts(pre_act):
    half = 0.5 * (1.0 + lax.erf(pre_act * SQRT_HALF))
    slope = half + pre_act * INV_ROOT_TWO_PI * jnp.exp(-0.5 * pre_act * pre_act)
    return pre_act * half, slope


def expert_body(experts, spare, me_ref, rows_ref, marked_ref, vec_ref, in_ref, bin_ref, out_ref, bout_ref, *refs):
    fresh_ref = refs[0]
    back_ref, sent_ref, acc_ref, dacc_ref = refs[1:]
    step = pl.program_id(0)
    width = rows_ref.shape[1]

    @pl.when(step == 0)
    def _():
        router = vec_ref[8:32, :].astype(NARROW)
        gate = slot_gates(rows_ref[...], marked_ref[:, width:], router, me_ref[0])
        sent_ref[...] = (gate * marked_ref[:, :width].astype(WIDE)).astype(NARROW)
        acc_ref[...] = jnp.zeros_like(acc_ref)
        dacc_ref[...] = jnp.zeros_like(dacc_ref)

    weight_in, weight_out = in_ref[...], out_ref[...]
    pre_act = mm(rows_ref[...], weight_in) + bin_ref[...].astype(WIDE)
    act, slope = gelu_parts(pre_act)
    acc_ref[...] += mm(act.astype(NARROW), weight_out)
    d_pre = mm_rows(sent_ref[...], weight_out) * slope
    dacc_ref[...] += mm_rows(d_pre.astype(NARROW), weight_in)

    @pl.when(step == pl.num_programs(0) - 1)
    def _():
        bias = bout_ref[...].astype(WIDE)
        slots = back_ref.shape[1]
        lanes = lax.broadcasted_iota(jnp.int32, (slots, 128), 1)
        lines = lax.broadcasted_iota(jnp.int32, (slots, 128), 0)
        line_hot = (lanes == lines).astype(NARROW)
        spare_hot = ((lines == lanes + spare) & (lanes < 3)).astype(NARROW)
        grads = marked_ref[:, :width].astype(WIDE)
        fresh_all = (acc_ref[...] + bias).astype(NARROW).astype(WIDE)
        acc_ref[...] = fresh_all
        terms = [
            term.astype(WIDE)
            for term in in_terms(jnp.sum(grads * fresh_all, axis=-1, keepdims=True))
        ]
        for index in range(experts):
            at = index * slots
            fresh_ref[me_ref[0] ^ index] = acc_ref[at : at + slots, :].astype(NARROW)
            mine = jnp.zeros((slots, 128), WIDE)
            for place, term in enumerate(terms):
                mine = jnp.where(lanes == place, term[at : at + slots, :], mine)
            packed = mm(spare_hot, mm_cols(mine.astype(NARROW), line_hot).astype(NARROW))
            back_ref[me_ref[0] ^ index, :, :128] = (dacc_ref[at : at + slots, :128] + packed).astype(NARROW)
            back_ref[me_ref[0] ^ index, :, 128:] = dacc_ref[at : at + slots, 128:].astype(
                NARROW
            )


def expert(me, rows, marked, vec, weight_in, b_in, weight_out, b_out, experts, slots, spare, chunk):
    total, width = rows.shape
    hidden_units = weight_in.shape[1]
    whole = lambda array: pl.BlockSpec(array.shape, lambda step: (0, 0))
    block = like((experts, slots, width), NARROW)
    return pl.pallas_call(
        functools.partial(expert_body, experts, spare),
        grid=(hidden_units // chunk,),
        out_shape=[block, block],
        in_specs=[
            SMEM,
            whole(rows),
            whole(marked),
            whole(vec),
            pl.BlockSpec((width, chunk), lambda step: (0, step)),
            pl.BlockSpec((1, chunk), lambda step: (0, step)),
            pl.BlockSpec((chunk, width), lambda step: (step, 0)),
            whole(b_out),
        ],
        out_specs=[pl.BlockSpec((experts, slots, width), lambda step: (0, 0, 0))] * 2,
        scratch_shapes=[
            pltpu.VMEM((total, width), NARROW),
            pltpu.VMEM((total, width), WIDE),
            pltpu.VMEM((total, width), WIDE),
        ],
        compiler_params=pltpu.CompilerParams(vmem_limit_bytes=58 * MIB),
        cost_estimate=pl.CostEstimate(flops=1, bytes_accessed=1, transcendentals=0),
        name="expert",
    )(me, rows, marked, vec, weight_in, b_in, weight_out, b_out)


def weights_body(count, me_ref, vec_ref, in_ref, bin_ref, out_ref, *refs):
    rows_in, marked_in = refs[:count], refs[count : 2 * count]
    dout_ref, own_ref = refs[2 * count : 2 * count + 2]
    others = refs[2 * count + 2 : -5]
    dbin_ref, dbout_ref, rows_ref, sent_ref, din_ref = refs[-5:]
    width = in_ref.shape[0]

    @pl.when(pl.program_id(0) == 0)
    def _():
        router = vec_ref[8:32, :].astype(NARROW)
        at = 0
        total = jnp.zeros((1, width), WIDE)
        for rows, marked in zip(rows_in, marked_in):
            size = rows.shape[0]
            gate = slot_gates(rows[...], marked[:, width:], router, me_ref[0])
            sent = (gate * marked[:, :width].astype(WIDE)).astype(NARROW)
            rows_ref[at : at + size, :] = rows[...]
            sent_ref[at : at + size, :] = sent
            total += jnp.sum(sent.astype(WIDE), axis=0, keepdims=True)
            at += size
        dbout_ref[...] = total

    pre_act = mm(rows_ref[...], in_ref[...]) + bin_ref[...].astype(WIDE)
    act, slope = gelu_parts(pre_act)
    dout_ref[...] = mm_cols(act.astype(NARROW), sent_ref[...])
    d_pre = mm_rows(sent_ref[...], out_ref[...]) * slope
    dbin_ref[...] = jnp.sum(d_pre, axis=0, keepdims=True)
    din_ref[...] = mm_cols(rows_ref[...], d_pre.astype(NARROW))
    share = own_ref.shape[0]
    for mask, out in enumerate((own_ref,) + others):
        at = pl.multiple_of((me_ref[1] ^ mask) * share, 8)
        out[...] = din_ref[pl.ds(at, share), :].astype(out.dtype)


def expert_weights(me, vec, my_in, my_bias, my_out, rows, marked, groups, chunk):
    count = len(rows)
    width, units = my_in.shape
    share = width // groups
    total = sum(piece.shape[0] for piece in rows)
    whole = lambda array: pl.BlockSpec(array.shape, lambda step: (0, 0))
    return pl.pallas_call(
        functools.partial(weights_body, count),
        grid=(units // chunk,),
        out_shape=[
            like((units, width), WIDE),
            like((share, units), WIDE),
        ]
        + [like((share, units), NARROW)] * (groups - 1)
        + [
            like((1, units), WIDE),
            like((1, width), WIDE),
        ],
        in_specs=[
            SMEM,
            whole(vec),
            pl.BlockSpec((width, chunk), lambda step: (0, step)),
            pl.BlockSpec((1, chunk), lambda step: (0, step)),
            pl.BlockSpec((chunk, width), lambda step: (step, 0)),
        ]
        + [whole(piece) for piece in rows + marked],
        out_specs=[
            pl.BlockSpec((chunk, width), lambda step: (step, 0)),
        ]
        + [pl.BlockSpec((share, chunk), lambda step: (0, step))] * groups
        + [
            pl.BlockSpec((1, chunk), lambda step: (0, step)),
            pl.BlockSpec((1, width), lambda step: (0, 0)),
        ],
        scratch_shapes=[
            pltpu.VMEM((total, width), NARROW),
            pltpu.VMEM((total, width), NARROW),
            pltpu.VMEM((width, chunk), WIDE),
        ],
        compiler_params=pltpu.CompilerParams(vmem_limit_bytes=58 * MIB),
        cost_estimate=pl.CostEstimate(flops=1, bytes_accessed=1, transcendentals=0),
        name="expert_weights",
    )(me, vec, my_in, my_bias, my_out, *rows, *marked)


def combine_body(experts, spare, *refs):
    hidden_ref, y_ref, d_ref, vec_ref, full_ref, routes_ref, slot_ref, targets_ref = refs[:8]
    back_ref, gate_ref, dh_ref, dctx_ref, sums_ref, dret_ref = refs[8:]
    tokens, width = hidden_ref.shape
    slots = back_ref.shape[1]
    for index in range(experts):
        at = index * slots
        dret_ref[at : at + slots, :] = back_ref[index].astype(WIDE)
    d_returned = dret_ref[...].astype(NARROW)
    lanes = lax.broadcasted_iota(jnp.int32, (tokens, experts * slots), 1)
    places = lax.broadcasted_iota(jnp.int32, (tokens, 128), 1)
    d_gates = []
    for choice in range(2):
        target = targets_ref[:, choice : choice + 1]
        slot = slot_ref[:, choice : choice + 1]
        line = jnp.where(target < 0, -8, target - slot + spare)
        found = None
        for term in range(3):
            hot = (lanes == line + term).astype(NARROW)
            new = mm(hot, d_returned[:, :128])
            found = new if found is None else found + new
        d_gates.append(
            jnp.sum(jnp.where(places == slot, found, 0.0), axis=-1, keepdims=True)
        )
    router = vec_ref[8:32, :].astype(NARROW)
    y_in = y_ref[...]
    logits = mm_rows(y_in, router)
    names = lax.broadcasted_iota(jnp.int32, logits.shape, 1)
    hot_first = (names == routes_ref[:, 0:1]).astype(WIDE)
    hot_second = (names == routes_ref[:, 1:2]).astype(WIDE)
    chosen_first = jnp.sum(logits * hot_first, axis=-1, keepdims=True)
    chosen_second = jnp.sum(logits * hot_second, axis=-1, keepdims=True)
    gate_first = 1.0 / (1.0 + jnp.exp(chosen_second - chosen_first))
    gate_second = 1.0 - gate_first
    gate_ref[...] = jnp.broadcast_to(gate_first, gate_ref.shape)
    grad = d_ref[...].astype(WIDE)
    d_diff = (d_gates[0] - d_gates[1]) * gate_first * gate_second
    d_logits = (d_diff * (hot_first - hot_second)).astype(NARROW)
    sums_ref[8:32, :] = mm_cols(d_logits, y_in)
    hot = ((lanes == targets_ref[:, 0:1]) | (lanes == targets_ref[:, 1:2])).astype(NARROW)
    d_y = mm(hot, d_returned) + mm(d_logits, router)
    normed, inv_std = normalize(hidden_ref[...])
    d_hidden = grad + norm_back(d_y, normed, inv_std, vec_ref[5:6, :])
    sums_ref[0:8, :] = jnp.zeros((8, width), WIDE)
    sums_ref[0:1, :] = jnp.sum(d_hidden, axis=0, keepdims=True)
    sums_ref[1:2, :] = jnp.sum(d_y * normed, axis=0, keepdims=True)
    sums_ref[2:3, :] = jnp.sum(d_y, axis=0, keepdims=True)
    dh_ref[...] = d_hidden
    dctx_ref[...] = mm_rows(d_hidden.astype(NARROW), full_ref[...]).astype(NARROW)


def output_body(hidden_ref, gate_ref, targets_ref, fresh_ref, out_ref, ret_ref):
    tokens = hidden_ref.shape[0]
    experts, slots, _ = fresh_ref.shape
    for index in range(experts):
        at = index * slots
        ret_ref[at : at + slots, :] = fresh_ref[index].astype(WIDE)
    returned = ret_ref[...].astype(NARROW)
    lanes = lax.broadcasted_iota(jnp.int32, (tokens, experts * slots), 1)
    first = mm((lanes == targets_ref[:, 0:1]).astype(NARROW), returned)
    second = mm((lanes == targets_ref[:, 1:2]).astype(NARROW), returned)
    gate = gate_ref[:, 0:1]
    out_ref[...] = (hidden_ref[...] + (gate * first + (1.0 - gate) * second)).astype(NARROW)


def back_body(qkv_ref, dctx_ref, lse_ref, full_ref, x_ref, vec_ref, dh_ref, early_ref, dx_ref, out_ref):
    tokens, width = dctx_ref.shape
    masks = head_masks(tokens)
    lanes = lax.broadcasted_iota(jnp.int32, (tokens, 128), 1)
    pair = 2 * HEAD_DIM
    scale = 1.0 / math.sqrt(HEAD_DIM)
    out_ref[tokens:, :] = jnp.zeros((out_ref.shape[0] - tokens, out_ref.shape[1]), NARROW)
    out_ref[:tokens, :width] = dh_ref[...].astype(NARROW)
    sums_q, sums_v = [], []
    for group in range(width // pair):
        at = group * pair
        query = qkv_ref[:, at : at + pair]
        keys = qkv_ref[:, width + at : width + at + pair]
        values = qkv_ref[:, 2 * width + at : 2 * width + at + pair]
        grads = dctx_ref[:, at : at + pair]
        d_query = d_keys = d_values = None
        for index in range(2):
            zero = jnp.zeros_like(query)
            query_h = jnp.where(masks[index], query, zero)
            keys_h = jnp.where(masks[index], keys, zero)
            grads_h = jnp.where(masks[index], grads, zero)
            head = 2 * group + index
            lse = jnp.sum(jnp.where(lanes == head, lse_ref[...], 0.0), axis=-1, keepdims=True)
            probs = jnp.exp(mm_rows(query_h, keys) * scale - lse)
            d_probs = mm_rows(grads_h, values)
            delta = jnp.sum(probs * d_probs, axis=-1, keepdims=True)
            d_scores = (probs * (d_probs - delta) * scale).astype(NARROW)
            new_values = mm_cols(probs.astype(NARROW), grads_h)
            new_query = mm(d_scores, keys_h)
            new_keys = mm_cols(d_scores, query_h)
            d_values = new_values if d_values is None else d_values + new_values
            d_query = new_query if d_query is None else d_query + new_query
            d_keys = new_keys if d_keys is None else d_keys + new_keys
        out_ref[:tokens, width + at : width + at + pair] = d_query.astype(NARROW)
        out_ref[:tokens, 2 * width + at : 2 * width + at + pair] = d_keys.astype(NARROW)
        out_ref[:tokens, 3 * width + at : 3 * width + at + pair] = d_values.astype(NARROW)
        sums_q.append(jnp.sum(d_query, axis=0, keepdims=True))
        sums_v.append(jnp.sum(d_values, axis=0, keepdims=True))
    d_a = mm_rows(out_ref[:tokens, width:], full_ref[...])
    normed, inv_std = normalize(x_ref[...].astype(WIDE))
    dx_ref[...] = dh_ref[...] + norm_back(d_a, normed, inv_std, vec_ref[3:4, :])
    rows = lax.broadcasted_iota(jnp.int32, (32, width), 0)
    sums = early_ref[...]
    new_rows = (
        jnp.concatenate(sums_q, axis=1),
        jnp.concatenate(sums_v, axis=1),
        jnp.sum(d_a * normed, axis=0, keepdims=True),
        jnp.sum(d_a, axis=0, keepdims=True),
    )
    for place, new in enumerate(new_rows, 3):
        sums = jnp.where(rows == place, new, sums)
    base = out_ref.shape[0] - 32
    for place, term in enumerate(in_terms(sums)):
        out_ref[base:, place * width : (place + 1) * width] = term


def outer_body(groups, columns_ref, keep_ref, other_ref, own_d_ref, other_d_ref, own_ref, *refs):
    outs, turned_ref = refs[:-1], refs[-1]
    tokens = keep_ref.shape[0]
    width = keep_ref.shape[1]
    half = width // 2
    rows = own_ref.shape[0]
    base = own_d_ref.shape[0] - 32
    sums = jnp.zeros((32, width), WIDE)
    for ref in (own_d_ref, other_d_ref):
        mine = ref[base:, :width].astype(WIDE) + ref[base:, width : 2 * width].astype(WIDE)
        sums = sums + (mine + ref[base:, 2 * width : 3 * width].astype(WIDE))
    turned_ref[...] = jnp.zeros_like(turned_ref)
    turned_ref[0:32, :] = sums
    turned = jnp.transpose(turned_ref[...]).astype(NARROW)
    ids = lax.broadcasted_iota(jnp.int32, (width, half), 0)
    hot = (ids == columns_ref[0:1, :half]).astype(NARROW)
    blocks = (
        (0, width, half),
        (width, 4 * width, 0),
        (4 * width, 4 * width + 128, None),
    )
    for low, high, left in blocks:
        if left is None:
            total = mm_cols(hot, turned)
        else:
            total = mm_cols(keep_ref[:, left : left + half], own_d_ref[:tokens, low:high])
            total = total + mm_cols(
                other_ref[:, left : left + half], other_d_ref[:tokens, low:high]
            )
        own_ref[:, low:high] = total[:rows, :]
        for index in range(1, groups):
            outs[index - 1][:, low:high] = total[index * rows : (index + 1) * rows, :].astype(
                NARROW
            )


def sum_body(count, layers, own_ref, *refs):
    total = own_ref[...]
    for ref in refs[:count]:
        total = total + ref[...].astype(WIDE)
    part = own_ref.shape[0] // layers
    for index, out in enumerate(refs[count:]):
        out[...] = total[index * part : (index + 1) * part, :].astype(out.dtype)


def sum_blocks(own, others, layers, first):
    rows, columns = own.shape
    part = rows // layers
    return run(
        functools.partial(sum_body, len(others), layers),
        [like((part, columns), first)] + [like((part, columns), NARROW)] * (layers - 1),
        [own] + others,
        rows * columns,
        12 * rows * columns,
        16,
        name="sum_blocks",
    )


def ordered_body(experts, layers, width, place_ref, low_ref, high_ref, *outs):
    qkv_ref, proj_ref, router_ref = outs[:3]
    rows = qkv_ref.shape[0]
    half = rows // 2
    ids = lax.broadcasted_iota(jnp.int32, (rows, half), 0)
    hot_low = (ids == place_ref[0:1, :]).astype(NARROW)
    hot_high = (ids == place_ref[1:2, :]).astype(NARROW)

    def pick(low, high):
        return mm(hot_low, low_ref[:, low:high]) + mm(hot_high, high_ref[:, low:high])

    proj_ref[...] = pick(0, width)
    qkv_ref[...] = pick(width, 4 * width)
    side = pick(4 * width, 4 * width + 128)
    router_ref[...] = side[:, 8 : 8 + experts]
    lanes = lax.broadcasted_iota(jnp.int32, (rows, rows), 1)
    lines = lax.broadcasted_iota(jnp.int32, (rows, rows), 0)
    for index, out in enumerate(outs[3:]):
        out[...] = jnp.sum(
            jnp.where(lanes == lines, side[:, index : index + 1], 0.0), axis=0, keepdims=True
        )


def spread_body(me_ref, *refs):
    out_ref = refs[-1]
    units = refs[0].shape[1]
    for mask, ref in enumerate(refs[:-1]):
        at = pl.multiple_of((me_ref[1] ^ mask) * units, 128)
        out_ref[:, pl.ds(at, units)] = ref[...].astype(WIDE)


def pack_body(core_ref, qkv_ref, proj_ref, router_ref, vectors_ref, out_ref, mine_ref, mark_ref):
    share, width = proj_ref.shape
    lanes = lax.broadcasted_iota(jnp.int32, (share, share), 1)
    lines = lax.broadcasted_iota(jnp.int32, (share, share), 0)
    places = lax.broadcasted_iota(jnp.int32, (share, 128), 1)
    spread = (
        lax.broadcasted_iota(jnp.int32, (router_ref.shape[1], 128), 0) + 8
        == lax.broadcasted_iota(jnp.int32, (router_ref.shape[1], 128), 1)
    ).astype(NARROW)
    side = mm(router_ref[...], spread)
    for index in range(vectors_ref.shape[0]):
        line = vectors_ref[index : index + 1, :]
        column = jnp.sum(jnp.where(lanes == lines, line, 0.0), axis=-1, keepdims=True)
        side = jnp.where(places == index, column, side)
    out_ref[:, : 3 * width] = qkv_ref[...]
    out_ref[:, 3 * width : 4 * width] = proj_ref[...]
    out_ref[:, 4 * width :] = side.astype(NARROW)
    rows = mine_ref.shape[0]
    at = pl.multiple_of(core_ref[0] * rows, 8)
    mine_ref[...] = out_ref[pl.ds(at, rows), :]
    mark_ref[...] = jnp.zeros_like(mark_ref)


def expert_weights_plain(me, vec, my_in, my_bias, my_out, rows, marked):
    rows, marked = jnp.concatenate(rows, axis=0), jnp.concatenate(marked, axis=0)
    width = rows.shape[1]
    gate = slot_gates(rows, marked[:, width:], vec[8:32].astype(NARROW), me)
    sent = (gate * marked[:, :width].astype(WIDE)).astype(NARROW)
    act, slope = gelu_parts(mm(rows, my_in) + my_bias.astype(WIDE))
    d_pre = mm_rows(sent, my_out) * slope
    return (
        mm_cols(act.astype(NARROW), sent),
        mm_cols(rows, d_pre.astype(NARROW)),
        jnp.sum(d_pre, axis=0, keepdims=True),
        jnp.sum(sent.astype(WIDE), axis=0, keepdims=True),
    )


def per_device(
    block_input,
    w_qkv,
    b_q,
    b_v,
    w_proj,
    b_proj,
    ln1_gain,
    ln1_bias,
    ln2_gain,
    ln2_bias,
    w_router,
    w_in,
    b_in,
    w_out,
    b_out,
    routes,
    slot_index,
    d_out,
):
    tokens, width = block_input.shape
    hidden_units = w_in.shape[2]
    experts = w_in.shape[0] * lax.axis_size("expert")
    groups = lax.axis_size("dp")
    layers = lax.axis_size("expert") // 2
    capacity = 2 * tokens // experts
    slots = -(-(capacity + 3) // 8) * 8
    total = experts * slots
    share = width // groups
    half = width // 2
    dp_me = lax.axis_index("dp")
    expert_me = lax.axis_index("expert")
    core, layer = expert_me % 2, expert_me // 2
    me = jnp.stack([expert_me, dp_me]).astype(jnp.int32)
    vectors = jnp.stack([b_q, b_v, b_proj, ln1_gain, ln1_bias, ln2_gain, ln2_bias]).astype(WIDE)
    wide = 4 * width + 128
    shard, mine, mark = run(
        pack_body,
        [
            like((share, wide), NARROW),
            like((share // 2, wide), NARROW),
            like((16, 128), NARROW),
        ],
        [core.reshape(1).astype(jnp.int32), w_qkv, w_proj, w_router, vectors],
        0,
        6 * share * wide,
        58,
        scalars=1,
        name="pack",
    )
    pieces, starts = gather_shared(shard, mine)
    d_late, routes, slot_index = after(
        (d_out, routes, slot_index), swap(mark, "expert", 1)
    )
    targets = jnp.where(slot_index < capacity, (routes ^ expert_me) * slots + slot_index, -1)
    targets_row = targets.T
    device_targets = jnp.where(slot_index < capacity, routes * slots + slot_index, -1)
    part = share // (2 * layers)
    order = jnp.arange(half, dtype=jnp.int32)
    spot = (order // (share // 2) ^ dp_me) * share + (
        order // part % layers ^ layer
    ) * part + order % part
    chosen_columns = jnp.concatenate(
        [spot + core * (share // 2), spot + (1 - core) * (share // 2)]
    )[None].astype(jnp.int32)

    marked_blocks = run(
        functools.partial(grad_slots_body, experts),
        like((experts, slots, width + 128), NARROW),
        [d_late, routes, device_targets.T],
        2 * total * tokens * width,
        4 * total * width,
        16,
        name="grad_slots",
    )
    marked_blocks = lax.all_to_all(marked_blocks, "expert", 0, 0, tiled=True)
    marked = run(
        order_body,
        like((total, width + 128), NARROW),
        [me, marked_blocks],
        total * width,
        4 * total * width,
        16,
        scalars=1,
        scratch=[pltpu.VMEM((total, width + 128), WIDE)],
        name="order",
    )

    full_qkv, full_proj, vec, qkv, context, log_total, keep, give = run(
        functools.partial(attend_body, len(pieces)),
        [
            like((width, 3 * width), NARROW),
            like((width, width), NARROW),
            like((32, width), WIDE),
            like((tokens, 3 * width), NARROW),
            like((tokens, width), NARROW),
            like((tokens, 128), WIDE),
            like((tokens, width), NARROW),
            like((tokens, width), NARROW),
        ],
        [jnp.stack(starts).astype(jnp.int32), block_input, chosen_columns] + pieces,
        10 * tokens * width * width,
        4 * width * wide,
        58,
        scalars=1,
        scratch=[pltpu.VMEM((width, 128), NARROW)],
        name="attend",
    )
    middle = run(
        functools.partial(middle_body, experts),
        [like((tokens, width), WIDE), like((tokens, width), NARROW)]
        + [like((slots, width), NARROW)] * experts,
        [context, block_input, vec, targets_row, full_proj],
        4 * tokens * width * width,
        4 * width * width,
        58,
        name="middle",
    )
    hidden, y_in = middle[:2]
    rows = join(exchange(middle[2:]))
    weight_in, weight_out = w_in[0], w_out[0]
    results = expert(
        me, rows, marked, vec, weight_in, b_in, weight_out, b_out, experts, slots, capacity, 512
    )
    fresh, d_expert_in = results
    d_returned = lax.all_to_all(d_expert_in, "expert", 0, 0, tiled=True)
    other = swap(after(give, fresh), "expert", 1)
    units = hidden_units // groups
    my_in, my_out, my_bias = (
        lax.dynamic_slice_in_dim(array, dp_me * units, units, axis)
        for array, axis in zip(after((weight_in, weight_out, b_in), y_in), (1, 0, 1))
    )
    marked_all = gather_rows(marked, y_in, rows)
    rows_all = gather_rows(rows, rows, fresh)
    d_returned, rows_all, marked_all, my_in, my_out, my_bias, other = lax.optimization_barrier(
        (d_returned, rows_all, marked_all, my_in, my_out, my_bias, other)
    )

    gates, d_hidden, d_context, early_sums = run(
        functools.partial(combine_body, experts, capacity),
        [
            like((tokens, 128), WIDE),
            like((tokens, width), WIDE),
            like((tokens, width), NARROW),
            like((32, width), WIDE),
        ],
        [hidden, y_in, d_out, vec, full_proj, routes, slot_index, device_targets, d_returned],
        2 * tokens * total * width + 2 * tokens * width * width,
        4 * width * width,
        24,
        scratch=[pltpu.VMEM((total, width), WIDE)],
        name="combine",
    )
    d_input, d_all = run(
        back_body,
        [like((tokens, width), WIDE), like((240, 4 * width), NARROW)],
        [qkv, d_context, log_total, full_qkv, block_input, vec, d_hidden, early_sums],
        40 * tokens * 256 * width,
        8 * tokens * width,
        32,
        name="back",
    )
    d_other = swap(d_all, "expert", 1)
    sums = run(
        functools.partial(outer_body, groups),
        [like((share // 2, wide), WIDE)] + [like((share // 2, wide), NARROW)] * (groups - 1),
        [chosen_columns, keep, other, d_all, d_other],
        4 * tokens * half * wide,
        6 * half * wide,
        24,
        scratch=[pltpu.VMEM((128, width), WIDE)],
        name="outer",
    )
    rows_all, marked_all = after((rows_all, marked_all), sums[0])
    if groups == 4:
        grads = expert_weights(
            me, vec, my_in, my_bias, my_out, rows_all, marked_all, groups, 256
        )
        part_w_out, blocks, (part_b_in, sum_sent) = grads[0], grads[1:-2], grads[-2:]
    else:
        part_w_out, d_w_in, part_b_in, sum_sent = expert_weights_plain(
            expert_me, vec, my_in, my_bias, my_out, rows_all, marked_all
        )
        blocks = [
            lax.dynamic_slice_in_dim(d_w_in, (dp_me ^ mask) * share, share, 0).astype(
                NARROW if mask else WIDE
            )
            for mask in range(groups)
        ]
    part_b_out = lax.dynamic_slice_in_dim(sum_sent[0], dp_me * share, share, 0)
    returned = lax.all_to_all(after(fresh, sums[0]), "expert", 0, 0, tiled=True)
    returned = after(returned, part_b_in)
    block_out = run(
        output_body,
        like((tokens, width), NARROW),
        [hidden, gates, device_targets, returned],
        4 * tokens * total * width,
        8 * tokens * width,
        24,
        scratch=[pltpu.VMEM((total, width), WIDE)],
        name="output",
    )
    sums = [sums[0]] + [swap(sums[mask], "dp", mask) for mask in range(1, groups)]
    sums, block_out, part_b_in, part_b_out = lax.optimization_barrier(
        (sums, block_out, part_b_in, part_b_out)
    )
    sums = sum_blocks(sums[0], sums[1:], layers, WIDE)
    blocks = [blocks[0]] + [
        swap(after(blocks[mask], sums[0]), "dp", mask) for mask in range(1, groups)
    ]
    sums = [sums[0]] + [swap(sums[mask], "expert", 2 * mask) for mask in range(1, layers)]
    done = sum_blocks(sums[0], sums[1:], 1, NARROW)[0]
    if groups == 4:
        part_w_in = run(
            spread_body,
            like((share, hidden_units), WIDE),
            [me] + blocks,
            share * hidden_units,
            8 * share * hidden_units,
            24,
            scalars=1,
            name="spread",
        )
    else:
        part_w_in = in_order([block.astype(WIDE) for block in blocks], dp_me, 1)
    done_pieces = [done] + [swap(done, "expert", 2 * mask) for mask in range(1, layers)]
    done_pieces, part_w_in = lax.optimization_barrier((done_pieces, part_w_in))
    low = join(done_pieces)
    high = swap(low, "expert", 1)

    place = jnp.arange(share // 2, dtype=jnp.int32)
    place = (place // part ^ layer) * part + place % part
    place = jnp.stack([place + core * (share // 2), place + (1 - core) * (share // 2)])
    finals = run(
        functools.partial(ordered_body, experts, layers, width),
        [
            like((share, 3 * width), WIDE),
            like((share, width), WIDE),
            like((share, experts), WIDE),
        ]
        + [like((1, share), WIDE)] * 7,
        [place.astype(jnp.int32), low, high],
        2 * share * share * wide,
        8 * share * wide,
        24,
        name="ordered",
    )
    vector_sum = [value[0] for value in finals[3:]]
    return (
        block_out,
        d_input,
        finals[0],
        vector_sum[3],
        vector_sum[4],
        finals[1],
        vector_sum[0],
        vector_sum[5],
        vector_sum[6],
        vector_sum[1],
        vector_sum[2],
        finals[2],
        part_w_in[None],
        part_b_in,
        part_w_out[None],
        part_b_out[None],
    )


def solution(mesh):
    return jax.shard_map(
        per_device,
        mesh=mesh,
        in_specs=(
            P(("dp", "expert"), None),
            P("dp", None),
            P("dp"),
            P("dp"),
            P("dp", None),
            P("dp"),
            P("dp"),
            P("dp"),
            P("dp"),
            P("dp"),
            P("dp", None),
            P("expert", None, None),
            P("expert", None),
            P("expert", None, None),
            P("expert", None),
            P(("dp", "expert"), None),
            P(("dp", "expert"), None),
            P(("dp", "expert"), None),
        ),
        out_specs=(
            P(("dp", "expert"), None),
            P(("dp", "expert"), None),
            P("dp", None),
            P("dp"),
            P("dp"),
            P("dp", None),
            P("dp"),
            P("dp"),
            P("dp"),
            P("dp"),
            P("dp"),
            P("dp", None),
            P("expert", "dp", None),
            P("expert", "dp"),
            P("expert", "dp", None),
            P("expert", "dp"),
        ),
        check_vma=False,
    )
```

```python
import functools
import math

import jax
import jax.numpy as jnp
from jax import lax
from jax.experimental import pallas as pl
from jax.experimental.pallas import tpu as pltpu
from jax.sharding import PartitionSpec as P

HEAD_DIM = 64
SEQ = 197


NORM_EPS = 1e-06
SQRT_HALF = 0.7071067811865476
INV_ROOT_TWO_PI = 0.3989422804014327


def normalize(values):
    center = values - jnp.mean(values, axis=-1, keepdims=True)
    inv_std = lax.rsqrt(jnp.mean(center * center, axis=-1, keepdims=True) + NORM_EPS)
    return (center * inv_std, inv_std)


def norm_back(grad_in, normed, inv_std, gain_vec):
    scaled = grad_in * gain_vec
    mean_plain = jnp.mean(scaled, axis=-1, keepdims=True)
    mean_mixed = jnp.mean(scaled * normed, axis=-1, keepdims=True)
    return inv_std * (scaled - mean_plain - normed * mean_mixed)


def gelu_value(pre_act):
    return 0.5 * pre_act * (1.0 + lax.erf(pre_act * SQRT_HALF))


def gelu_slope(pre_act):
    return 0.5 * (1.0 + lax.erf(pre_act * SQRT_HALF)) + pre_act * INV_ROOT_TWO_PI * jnp.exp(
        -0.5 * pre_act * pre_act
    )


def swap(values, axis, mask):
    size = lax.axis_size(axis)
    return lax.ppermute(values, axis, [(index, index ^ mask) for index in range(size)])


def gather_shared(shard, mine):
    groups = lax.axis_size("dp")
    rows = shard.shape[0]
    if groups != 4:
        return [lax.all_gather(shard, "dp", axis=0, tiled=True)], [jnp.int32(0)]
    me = lax.axis_index("dp")
    core = lax.axis_index("expert") % 2
    half = rows // 2
    part = half // 2
    from_one = swap(mine, "dp", 1)
    from_two = swap(mine, "dp", 2)
    far_low = swap(from_one[:part], "dp", 2)
    far_high = swap(from_two[part:], "dp", 1)
    other_one = swap(from_one, "expert", 1)
    other_two = swap(from_two, "expert", 1)
    other_low = swap(far_low, "expert", 1)
    other_high = swap(far_high, "expert", 1)
    base = core * half
    other = half - base
    one, two, far = (me ^ 1) * rows, (me ^ 2) * rows, (me ^ 3) * rows
    starts = [me * rows, one + base, two + base, far + base, far + base + part]
    starts += [one + other, two + other, far + other, far + other + part]
    pieces = [shard, from_one, from_two, far_low, far_high]
    pieces += [other_one, other_two, other_low, other_high]
    return pieces, starts


def gather_near(rows):
    groups = lax.axis_size("dp")
    return [swap(rows, "dp", mask) for mask in ((1, 2) if groups == 4 else range(1, groups))]


def gather_far(near):
    if lax.axis_size("dp") != 4:
        return []
    one, two = near
    half = one.shape[0] // 2
    return [swap(one[:half], "dp", 2), swap(two[half:], "dp", 1)]


def exchange(blocks):
    return [blocks[0]] + [swap(blocks[mask], "expert", mask) for mask in range(1, len(blocks))]


def in_order(pieces, me, axis):
    stack = jnp.stack(pieces)
    return jnp.concatenate(
        [
            lax.dynamic_index_in_dim(stack, me ^ index, 0, keepdims=False)
            for index in range(len(pieces))
        ],
        axis=axis,
    )


VMEM = pl.BlockSpec(memory_space=pltpu.VMEM)
SMEM = pl.BlockSpec(memory_space=pltpu.SMEM)
NARROW = jnp.bfloat16
WIDE = jnp.float32
MIB = 1024 * 1024


def like(shape, dtype):
    return jax.ShapeDtypeStruct(shape, dtype)


def run(
    body, outs, operands, flops, moved, mib, scalars=0, scratch=(), out_specs=None, name=None, marks=()
):
    marks = list(marks)
    count = len(operands)

    def marked_body(*refs):
        body(*refs[:count], *refs[count + len(marks) :])

    return pl.pallas_call(
        marked_body,
        out_shape=outs,
        in_specs=[SMEM] * scalars
        + [VMEM] * (count - scalars)
        + [pl.BlockSpec(memory_space=pl.ANY)] * len(marks),
        out_specs=out_specs or jax.tree.map(lambda _: VMEM, outs),
        scratch_shapes=list(scratch),
        compiler_params=pltpu.CompilerParams(vmem_limit_bytes=mib * MIB),
        cost_estimate=pl.CostEstimate(flops=1, bytes_accessed=1, transcendentals=0),
        name=name,
    )(*operands, *marks)


def mm(left, right):
    return jnp.dot(left, right, preferred_element_type=WIDE)


def mm_rows(left, right):
    return lax.dot_general(left, right, (((1,), (1,)), ((), ())), preferred_element_type=WIDE)


def mm_cols(left, right):
    return lax.dot_general(left, right, (((0,), (0,)), ((), ())), preferred_element_type=WIDE)


def head_masks(rows):
    lanes = lax.broadcasted_iota(jnp.int32, (rows, 2 * HEAD_DIM), 1)
    return [lanes < HEAD_DIM, lanes >= HEAD_DIM]


def join_body(count, *refs):
    out_ref, wide_ref = refs[count], refs[count + 1]
    at = 0
    for ref in refs[:count]:
        wide_ref[at : at + ref.shape[0], :] = ref[...].astype(WIDE)
        at += ref.shape[0]
    out_ref[...] = wide_ref[...].astype(NARROW)


def join(pieces):
    rows = sum(piece.shape[0] for piece in pieces)
    columns = pieces[0].shape[1]
    return run(
        functools.partial(join_body, len(pieces)),
        like((rows, columns), NARROW),
        pieces,
        rows * columns,
        4 * rows * columns,
        16,
        scratch=[pltpu.VMEM((rows, columns), WIDE)],
        name="join",
    )


def slot_rows(targets, total, tokens):
    ids = lax.broadcasted_iota(jnp.int32, (total, tokens), 0)
    return ids == targets[0:1, :], ids == targets[1:2, :]


def grad_slots_body(experts, d_ref, routes_ref, targets_ref, out_ref):
    tokens, width = d_ref.shape
    slots = out_ref.shape[1]
    first, second = slot_rows(targets_ref[...], experts * slots, tokens)
    first, second = first.astype(NARROW), second.astype(NARROW)
    rows = mm(first + second, d_ref[...]).astype(NARROW)
    lanes = lax.broadcasted_iota(jnp.int32, (tokens, 128), 1)
    other_first = (lanes == routes_ref[:, 1:2]).astype(NARROW)
    other_second = (lanes == routes_ref[:, 0:1]).astype(NARROW)
    marks = (mm(first, other_first) + mm(second, other_second)).astype(NARROW)
    for index in range(experts):
        out_ref[index, :, :width] = rows[index * slots : (index + 1) * slots, :]
        out_ref[index, :, width:] = marks[index * slots : (index + 1) * slots, :]


def order_body(me_ref, *refs):
    out_ref, wide_ref = refs[-2:]
    slots = refs[0].shape[0]
    for mask, ref in enumerate(refs[:-2]):
        at = pl.multiple_of((me_ref[0] ^ mask) * slots, 8)
        wide_ref[pl.ds(at, slots), :] = ref[...].astype(WIDE)
    out_ref[...] = wide_ref[...].astype(NARROW)


def attend_body(count, *refs):
    starts_ref, x_ref, columns_ref = refs[0], refs[1], refs[2]
    pieces = refs[3 : 3 + count]
    full_ref, vec_ref, qkv_ref, ctx_ref, lse_ref, keep_ref, give_ref = refs[3 + count : 10 + count]
    side_ref = refs[10 + count]
    tokens, width = x_ref.shape
    for index, piece in enumerate(pieces):
        rows = piece.shape[0]
        at = starts_ref[index] if count > 1 else 0
        if count > 1:
            at = pl.multiple_of(at, 16)
        full_ref[pl.ds(at, rows), :] = piece[:, : 3 * width]
        side_ref[pl.ds(at, rows), :] = piece[:, 3 * width :]
    side = jnp.transpose(side_ref[...].astype(WIDE))
    vec_ref[...] = side[: vec_ref.shape[0], :]
    bias_q, bias_v = vec_ref[0:1, :], vec_ref[1:2, :]
    gain, bias = vec_ref[3:4, :], vec_ref[4:5, :]
    normed, _ = normalize(x_ref[...].astype(WIDE))
    a_in = (normed * gain + bias).astype(NARROW)
    qkv_ref[:, :width] = (mm(a_in, full_ref[:, :width]) + bias_q).astype(NARROW)
    qkv_ref[:, width : 2 * width] = mm(a_in, full_ref[:, width : 2 * width]).astype(NARROW)
    qkv_ref[:, 2 * width :] = (
        mm(a_in, full_ref[:, 2 * width : 3 * width]) + bias_v
    ).astype(NARROW)
    masks = head_masks(tokens)
    lanes = lax.broadcasted_iota(jnp.int32, (tokens, 128), 1)
    lse_all = jnp.zeros((tokens, 128), WIDE)
    pair = 2 * HEAD_DIM
    for group in range(width // pair):
        at = group * pair
        query = qkv_ref[:, at : at + pair]
        keys = qkv_ref[:, width + at : width + at + pair]
        values = qkv_ref[:, 2 * width + at : 2 * width + at + pair]
        outs = []
        for index in range(2):
            scores = mm_rows(jnp.where(masks[index], query, 0), keys) * (
                1.0 / math.sqrt(HEAD_DIM)
            )
            top = jnp.max(scores, axis=-1, keepdims=True)
            exps = jnp.exp(scores - top)
            total = jnp.sum(exps, axis=-1, keepdims=True)
            lse_all = jnp.where(lanes == 2 * group + index, top + jnp.log(total), lse_all)
            outs.append(mm((exps / total).astype(NARROW), values))
        ctx_ref[:, at : at + pair] = jnp.where(masks[0], outs[0], outs[1]).astype(NARROW)
    lse_ref[...] = lse_all
    ids = lax.broadcasted_iota(jnp.int32, (width, columns_ref.shape[1]), 0)
    hot = (ids == columns_ref[0:1, :]).astype(NARROW)
    half = width // 2
    chosen = mm(a_in, hot).astype(NARROW)
    keep_ref[:, :half] = chosen[:, :half]
    give_ref[:, :half] = chosen[:, half:]
    chosen = mm(ctx_ref[...], hot).astype(NARROW)
    keep_ref[:, half:] = chosen[:, :half]
    give_ref[:, half:] = chosen[:, half:]


def middle_body(experts, count, starts_ref, ctx_ref, x_ref, vec_ref, targets_ref, *refs):
    full_ref, hidden_ref, y_ref = refs[count : count + 3]
    outs = refs[count + 3 :]
    for index, piece in enumerate(refs[:count]):
        at = pl.multiple_of(starts_ref[index], 16) if count > 1 else 0
        full_ref[pl.ds(at, piece.shape[0]), :] = piece[...]
    hidden = x_ref[...].astype(WIDE) + mm(ctx_ref[...], full_ref[...]) + vec_ref[2:3, :]
    hidden_ref[...] = hidden
    normed, _ = normalize(hidden)
    y_in = (normed * vec_ref[5:6, :] + vec_ref[6:7, :]).astype(NARROW)
    y_ref[...] = y_in
    slots = outs[0].shape[0]
    first, second = slot_rows(targets_ref[...], experts * slots, x_ref.shape[0])
    rows = mm((first | second).astype(NARROW), y_in).astype(NARROW)
    for index, out in enumerate(outs):
        out[...] = rows[index * slots : (index + 1) * slots, :]


def in_terms(values):
    high = values.astype(NARROW)
    rest = values - high.astype(WIDE)
    middle = rest.astype(NARROW)
    return high, middle, (rest - middle.astype(WIDE)).astype(NARROW)


def slot_gates(rows, marks, router, mine):
    logits = mm_rows(rows, router)
    lanes = lax.broadcasted_iota(jnp.int32, logits.shape, 1)
    own = jnp.sum(jnp.where(lanes == mine, logits, 0.0), axis=-1, keepdims=True)
    other = jnp.sum(
        marks[:, : logits.shape[1]].astype(WIDE) * logits, axis=-1, keepdims=True
    )
    return 1.0 / (1.0 + jnp.exp(other - own))


def gelu_parts(pre_act):
    half = 0.5 * (1.0 + lax.erf(pre_act * SQRT_HALF))
    slope = half + pre_act * INV_ROOT_TWO_PI * jnp.exp(-0.5 * pre_act * pre_act)
    return pre_act * half, slope


def expert_body(experts, spare, me_ref, rows_ref, marked_ref, vec_ref, in_ref, bin_ref, out_ref, bout_ref, *refs):
    fresh_ref = refs[0]
    back_ref, sent_ref, acc_ref, dacc_ref = refs[1:]
    step = pl.program_id(0)
    width = rows_ref.shape[1]

    @pl.when(step == 0)
    def _():
        router = vec_ref[8:32, :].astype(NARROW)
        gate = slot_gates(rows_ref[...], marked_ref[:, width:], router, me_ref[0])
        sent_ref[...] = (gate * marked_ref[:, :width].astype(WIDE)).astype(NARROW)
        acc_ref[...] = jnp.zeros_like(acc_ref)
        dacc_ref[...] = jnp.zeros_like(dacc_ref)

    weight_in, weight_out = in_ref[...], out_ref[...]
    pre_act = mm(rows_ref[...], weight_in) + bin_ref[...].astype(WIDE)
    act, slope = gelu_parts(pre_act)
    acc_ref[...] += mm(act.astype(NARROW), weight_out)
    d_pre = mm_rows(sent_ref[...], weight_out) * slope
    dacc_ref[...] += mm_rows(d_pre.astype(NARROW), weight_in)

    @pl.when(step == pl.num_programs(0) - 1)
    def _():
        bias = bout_ref[...].astype(WIDE)
        slots = back_ref.shape[1]
        lanes = lax.broadcasted_iota(jnp.int32, (slots, 128), 1)
        lines = lax.broadcasted_iota(jnp.int32, (slots, 128), 0)
        line_hot = (lanes == lines).astype(NARROW)
        spare_hot = ((lines == lanes + spare) & (lanes < 3)).astype(NARROW)
        grads = marked_ref[:, :width].astype(WIDE)
        fresh_all = (acc_ref[...] + bias).astype(NARROW).astype(WIDE)
        acc_ref[...] = fresh_all
        terms = [
            term.astype(WIDE)
            for term in in_terms(jnp.sum(grads * fresh_all, axis=-1, keepdims=True))
        ]
        for index in range(experts):
            at = index * slots
            fresh_ref[index] = acc_ref[at : at + slots, :].astype(NARROW)
            mine = jnp.zeros((slots, 128), WIDE)
            for place, term in enumerate(terms):
                mine = jnp.where(lanes == place, term[at : at + slots, :], mine)
            packed = mm(spare_hot, mm_cols(mine.astype(NARROW), line_hot).astype(NARROW))
            back_ref[index, :, :128] = (dacc_ref[at : at + slots, :128] + packed).astype(NARROW)
            back_ref[index, :, 128:] = dacc_ref[at : at + slots, 128:].astype(
                NARROW
            )


def expert(me, rows, marked, vec, weight_in, b_in, weight_out, b_out, experts, slots, spare, chunk):
    total, width = rows.shape
    hidden_units = weight_in.shape[1]
    whole = lambda array: pl.BlockSpec(array.shape, lambda step: (0, 0))
    block = like((experts, slots, width), NARROW)
    return pl.pallas_call(
        functools.partial(expert_body, experts, spare),
        grid=(hidden_units // chunk,),
        out_shape=[block, block],
        in_specs=[
            SMEM,
            whole(rows),
            whole(marked),
            whole(vec),
            pl.BlockSpec((width, chunk), lambda step: (0, step)),
            pl.BlockSpec((1, chunk), lambda step: (0, step)),
            pl.BlockSpec((chunk, width), lambda step: (step, 0)),
            whole(b_out),
        ],
        out_specs=[pl.BlockSpec((experts, slots, width), lambda step: (0, 0, 0))] * 2,
        scratch_shapes=[
            pltpu.VMEM((total, width), NARROW),
            pltpu.VMEM((total, width), WIDE),
            pltpu.VMEM((total, width), WIDE),
        ],
        compiler_params=pltpu.CompilerParams(vmem_limit_bytes=58 * MIB),
        cost_estimate=pl.CostEstimate(flops=1, bytes_accessed=1, transcendentals=0),
        name="expert",
    )(me, rows, marked, vec, weight_in, b_in, weight_out, b_out)


def weights_body(count, me_ref, mark_ref, vec_ref, in_ref, bin_ref, out_ref, *refs):
    rows_in, marked_in = refs[: count[0]], refs[count[0] : sum(count)]
    dout_ref, own_ref = refs[sum(count) : sum(count) + 2]
    others = refs[sum(count) + 2 : -5]
    dbin_ref, dbout_ref, rows_ref, sent_ref, din_ref = refs[-5:]
    width = in_ref.shape[0]

    @pl.when(pl.program_id(0) == 0)
    def _():
        router = vec_ref[8:32, :].astype(NARROW)
        at = 0
        for rows in rows_in:
            rows_ref[at : at + rows.shape[0], :] = rows[...]
            at += rows.shape[0]
        at = 0
        total = jnp.zeros((1, width), WIDE)
        for marked in marked_in:
            size = marked.shape[0]
            gate = slot_gates(rows_ref[at : at + size, :], marked[:, width:], router, me_ref[0])
            sent = (gate * marked[:, :width].astype(WIDE)).astype(NARROW)
            sent_ref[at : at + size, :] = sent
            total += jnp.sum(sent.astype(WIDE), axis=0, keepdims=True)
            at += size
        dbout_ref[...] = total

    pre_act = mm(rows_ref[...], in_ref[...]) + bin_ref[...].astype(WIDE)
    act, slope = gelu_parts(pre_act)
    dout_ref[...] = mm_cols(act.astype(NARROW), sent_ref[...])
    d_pre = mm_rows(sent_ref[...], out_ref[...]) * slope
    dbin_ref[...] = jnp.sum(d_pre, axis=0, keepdims=True)
    din_ref[...] = mm_cols(rows_ref[...], d_pre.astype(NARROW))
    share = own_ref.shape[0]
    for mask, out in enumerate((own_ref,) + others):
        at = pl.multiple_of((me_ref[1] ^ mask) * share, 8)
        out[...] = din_ref[pl.ds(at, share), :].astype(out.dtype)


def expert_weights(me, mark, vec, weight_in, b_in, weight_out, rows, marked, groups, chunk):
    count = len(rows), len(marked)
    width, hidden_units = weight_in.shape
    units = hidden_units // groups
    share = width // groups
    steps = units // chunk
    total = sum(piece.shape[0] for piece in rows)
    whole = lambda array: pl.BlockSpec(array.shape, lambda step, at: (0, 0))
    wide = lambda size: pl.BlockSpec((size, chunk), lambda step, at: (0, step))
    return pl.pallas_call(
        functools.partial(weights_body, count),
        grid_spec=pltpu.PrefetchScalarGridSpec(
            num_scalar_prefetch=1,
            grid=(steps,),
            in_specs=[
                pl.BlockSpec(memory_space=pl.ANY),
                whole(vec),
                pl.BlockSpec((width, chunk), lambda step, at: (0, at[1] * steps + step)),
                pl.BlockSpec((1, chunk), lambda step, at: (0, at[1] * steps + step)),
                pl.BlockSpec((chunk, width), lambda step, at: (at[1] * steps + step, 0)),
            ]
            + [whole(piece) for piece in rows + marked],
            out_specs=[pl.BlockSpec((chunk, width), lambda step, at: (step, 0))]
            + [wide(share)] * groups
            + [wide(1), pl.BlockSpec((1, width), lambda step, at: (0, 0))],
            scratch_shapes=[
                pltpu.VMEM((total, width), NARROW),
                pltpu.VMEM((total, width), NARROW),
                pltpu.VMEM((width, chunk), WIDE),
            ],
        ),
        out_shape=[like((units, width), WIDE), like((share, units), WIDE)]
        + [like((share, units), NARROW)] * (groups - 1)
        + [like((1, units), WIDE), like((1, width), WIDE)],
        compiler_params=pltpu.CompilerParams(vmem_limit_bytes=58 * MIB),
        cost_estimate=pl.CostEstimate(flops=1, bytes_accessed=1, transcendentals=0),
        name="expert_weights",
    )(me, mark, vec, weight_in, b_in, weight_out, *rows, *marked)


def combine_body(experts, spare, *refs):
    hidden_ref, y_ref, d_ref, vec_ref, full_ref, routes_ref, slot_ref, targets_ref = refs[:8]
    back_ref, gate_ref, dh_ref, dctx_ref, sums_ref, dret_ref = refs[8:]
    tokens, width = hidden_ref.shape
    slots = back_ref.shape[1]
    for index in range(experts):
        at = index * slots
        dret_ref[at : at + slots, :] = back_ref[index].astype(WIDE)
    d_returned = dret_ref[...].astype(NARROW)
    lanes = lax.broadcasted_iota(jnp.int32, (tokens, experts * slots), 1)
    places = lax.broadcasted_iota(jnp.int32, (tokens, 128), 1)
    d_gates = []
    for choice in range(2):
        target = targets_ref[:, choice : choice + 1]
        slot = slot_ref[:, choice : choice + 1]
        line = jnp.where(target < 0, -8, target - slot + spare)
        found = None
        for term in range(3):
            hot = (lanes == line + term).astype(NARROW)
            new = mm(hot, d_returned[:, :128])
            found = new if found is None else found + new
        d_gates.append(
            jnp.sum(jnp.where(places == slot, found, 0.0), axis=-1, keepdims=True)
        )
    router = vec_ref[8:32, :].astype(NARROW)
    y_in = y_ref[...]
    logits = mm_rows(y_in, router)
    names = lax.broadcasted_iota(jnp.int32, logits.shape, 1)
    hot_first = (names == routes_ref[:, 0:1]).astype(WIDE)
    hot_second = (names == routes_ref[:, 1:2]).astype(WIDE)
    chosen_first = jnp.sum(logits * hot_first, axis=-1, keepdims=True)
    chosen_second = jnp.sum(logits * hot_second, axis=-1, keepdims=True)
    gate_first = 1.0 / (1.0 + jnp.exp(chosen_second - chosen_first))
    gate_second = 1.0 - gate_first
    gate_ref[...] = jnp.broadcast_to(gate_first, gate_ref.shape)
    grad = d_ref[...].astype(WIDE)
    d_diff = (d_gates[0] - d_gates[1]) * gate_first * gate_second
    d_logits = (d_diff * (hot_first - hot_second)).astype(NARROW)
    sums_ref[8:32, :] = mm_cols(d_logits, y_in)
    hot = ((lanes == targets_ref[:, 0:1]) | (lanes == targets_ref[:, 1:2])).astype(NARROW)
    d_y = mm(hot, d_returned) + mm(d_logits, router)
    normed, inv_std = normalize(hidden_ref[...])
    d_hidden = grad + norm_back(d_y, normed, inv_std, vec_ref[5:6, :])
    sums_ref[0:8, :] = jnp.zeros((8, width), WIDE)
    sums_ref[0:1, :] = jnp.sum(d_hidden, axis=0, keepdims=True)
    sums_ref[1:2, :] = jnp.sum(d_y * normed, axis=0, keepdims=True)
    sums_ref[2:3, :] = jnp.sum(d_y, axis=0, keepdims=True)
    dh_ref[...] = d_hidden
    dctx_ref[...] = mm_rows(d_hidden.astype(NARROW), full_ref[...]).astype(NARROW)


def output_body(hidden_ref, gate_ref, targets_ref, fresh_ref, out_ref, ret_ref):
    tokens = hidden_ref.shape[0]
    experts, slots, _ = fresh_ref.shape
    for index in range(experts):
        at = index * slots
        ret_ref[at : at + slots, :] = fresh_ref[index].astype(WIDE)
    returned = ret_ref[...].astype(NARROW)
    lanes = lax.broadcasted_iota(jnp.int32, (tokens, experts * slots), 1)
    first = mm((lanes == targets_ref[:, 0:1]).astype(NARROW), returned)
    second = mm((lanes == targets_ref[:, 1:2]).astype(NARROW), returned)
    gate = gate_ref[:, 0:1]
    out_ref[...] = (hidden_ref[...] + (gate * first + (1.0 - gate) * second)).astype(NARROW)


def back_body(qkv_ref, dctx_ref, lse_ref, full_ref, x_ref, vec_ref, dh_ref, early_ref, dx_ref, out_ref):
    tokens, width = dctx_ref.shape
    masks = head_masks(tokens)
    lanes = lax.broadcasted_iota(jnp.int32, (tokens, 128), 1)
    pair = 2 * HEAD_DIM
    scale = 1.0 / math.sqrt(HEAD_DIM)
    out_ref[tokens:, :] = jnp.zeros((out_ref.shape[0] - tokens, out_ref.shape[1]), NARROW)
    out_ref[:tokens, :width] = dh_ref[...].astype(NARROW)
    sums_q, sums_v = [], []
    for group in range(width // pair):
        at = group * pair
        query = qkv_ref[:, at : at + pair]
        keys = qkv_ref[:, width + at : width + at + pair]
        values = qkv_ref[:, 2 * width + at : 2 * width + at + pair]
        grads = dctx_ref[:, at : at + pair]
        d_query = d_keys = d_values = None
        for index in range(2):
            zero = jnp.zeros_like(query)
            query_h = jnp.where(masks[index], query, zero)
            keys_h = jnp.where(masks[index], keys, zero)
            grads_h = jnp.where(masks[index], grads, zero)
            head = 2 * group + index
            lse = jnp.sum(jnp.where(lanes == head, lse_ref[...], 0.0), axis=-1, keepdims=True)
            probs = jnp.exp(mm_rows(query_h, keys) * scale - lse)
            d_probs = mm_rows(grads_h, values)
            delta = jnp.sum(probs * d_probs, axis=-1, keepdims=True)
            d_scores = (probs * (d_probs - delta) * scale).astype(NARROW)
            new_values = mm_cols(probs.astype(NARROW), grads_h)
            new_query = mm(d_scores, keys_h)
            new_keys = mm_cols(d_scores, query_h)
            d_values = new_values if d_values is None else d_values + new_values
            d_query = new_query if d_query is None else d_query + new_query
            d_keys = new_keys if d_keys is None else d_keys + new_keys
        out_ref[:tokens, width + at : width + at + pair] = d_query.astype(NARROW)
        out_ref[:tokens, 2 * width + at : 2 * width + at + pair] = d_keys.astype(NARROW)
        out_ref[:tokens, 3 * width + at : 3 * width + at + pair] = d_values.astype(NARROW)
        sums_q.append(jnp.sum(d_query, axis=0, keepdims=True))
        sums_v.append(jnp.sum(d_values, axis=0, keepdims=True))
    d_a = mm_rows(out_ref[:tokens, width:], full_ref[...])
    normed, inv_std = normalize(x_ref[...].astype(WIDE))
    dx_ref[...] = dh_ref[...] + norm_back(d_a, normed, inv_std, vec_ref[3:4, :])
    rows = lax.broadcasted_iota(jnp.int32, (32, width), 0)
    sums = early_ref[...]
    new_rows = (
        jnp.concatenate(sums_q, axis=1),
        jnp.concatenate(sums_v, axis=1),
        jnp.sum(d_a * normed, axis=0, keepdims=True),
        jnp.sum(d_a, axis=0, keepdims=True),
    )
    for place, new in enumerate(new_rows, 3):
        sums = jnp.where(rows == place, new, sums)
    base = out_ref.shape[0] - 32
    for place, term in enumerate(in_terms(sums)):
        out_ref[base:, place * width : (place + 1) * width] = term


def backward_body(experts, spare, *refs):
    inputs = refs[:8]
    d_returned_ref, qkv_ref, lse_ref, qkv_weight_ref, x_ref = refs[8:13]
    gate_ref, dx_ref, all_ref, dret_ref, dh_ref, dctx_ref, sums_ref = refs[13:]
    vec_ref = refs[3]
    combine_body(
        experts, spare, *inputs, d_returned_ref, gate_ref, dh_ref, dctx_ref, sums_ref, dret_ref
    )
    back_body(
        qkv_ref, dctx_ref, lse_ref, qkv_weight_ref, x_ref, vec_ref, dh_ref, sums_ref, dx_ref, all_ref
    )


def outer_body(groups, columns_ref, keep_ref, other_ref, own_d_ref, other_d_ref, own_ref, *refs):
    peers = refs[: groups - 1]
    turned_ref, sems = refs[groups - 1 : groups + 1]
    outs = refs[groups + 1 :]
    tokens = keep_ref.shape[0]
    width = keep_ref.shape[1]
    half = width // 2
    rows = own_ref.shape[0]
    base = own_d_ref.shape[0] - 32
    sums = jnp.zeros((32, width), WIDE)
    for ref in (own_d_ref, other_d_ref):
        mine = ref[base:, :width].astype(WIDE) + ref[base:, width : 2 * width].astype(WIDE)
        sums = sums + (mine + ref[base:, 2 * width : 3 * width].astype(WIDE))
    turned_ref[...] = jnp.zeros_like(turned_ref)
    turned_ref[0:32, :] = sums
    turned = jnp.transpose(turned_ref[...]).astype(NARROW)
    ids = lax.broadcasted_iota(jnp.int32, (width, half), 0)
    hot = (ids == columns_ref[0:1, :half]).astype(NARROW)
    blocks = (
        (0, width, half),
        (width, 4 * width, 0),
        (4 * width, 4 * width + 128, None),
    )
    for low, high, left in blocks:
        if left is None:
            total = mm_cols(hot, turned)
        else:
            total = mm_cols(keep_ref[:, left : left + half], own_d_ref[:tokens, low:high])
            total = total + mm_cols(
                other_ref[:, left : left + half], other_d_ref[:tokens, low:high]
            )
        own_ref[:, low:high] = total[:rows, :]
        for index in range(1, groups):
            outs[index - 1][:, low:high] = total[index * rows : (index + 1) * rows, :].astype(
                NARROW
            )
    copies = [
        pltpu.make_async_copy(out, peer, sems.at[index])
        for index, (out, peer) in enumerate(zip(outs, peers))
    ]
    for copy in copies:
        copy.start()
    for copy in copies:
        copy.wait()


def sum_body(count, layers, own_ref, *refs):
    total = own_ref[...]
    for ref in refs[:count]:
        total = total + ref[...].astype(WIDE)
    part = own_ref.shape[0] // layers
    for index, out in enumerate(refs[count:]):
        out[...] = total[index * part : (index + 1) * part, :].astype(out.dtype)


def sum_blocks(own, others, layers, first):
    rows, columns = own.shape
    part = rows // layers
    return run(
        functools.partial(sum_body, len(others), layers),
        [like((part, columns), first)] + [like((part, columns), NARROW)] * (layers - 1),
        [own] + others,
        rows * columns,
        12 * rows * columns,
        16,
        name="sum_blocks",
    )


def ordered_body(experts, layers, width, place_ref, low_ref, high_ref, *outs):
    qkv_ref, proj_ref, router_ref = outs[:3]
    rows = qkv_ref.shape[0]
    half = rows // 2
    ids = lax.broadcasted_iota(jnp.int32, (rows, half), 0)
    hot_low = (ids == place_ref[0:1, :]).astype(NARROW)
    hot_high = (ids == place_ref[1:2, :]).astype(NARROW)

    def pick(low, high):
        return mm(hot_low, low_ref[:, low:high]) + mm(hot_high, high_ref[:, low:high])

    proj_ref[...] = pick(0, width)
    qkv_ref[...] = pick(width, 4 * width)
    side = pick(4 * width, 4 * width + 128)
    router_ref[...] = side[:, 8 : 8 + experts]
    lanes = lax.broadcasted_iota(jnp.int32, (rows, rows), 1)
    lines = lax.broadcasted_iota(jnp.int32, (rows, rows), 0)
    for index, out in enumerate(outs[3:]):
        out[...] = jnp.sum(
            jnp.where(lanes == lines, side[:, index : index + 1], 0.0), axis=0, keepdims=True
        )


def spread_body(me_ref, *refs):
    out_ref = refs[-1]
    units = refs[0].shape[1]
    for mask, ref in enumerate(refs[:-1]):
        at = pl.multiple_of((me_ref[1] ^ mask) * units, 128)
        out_ref[:, pl.ds(at, units)] = ref[...].astype(WIDE)


def pack_body(core_ref, qkv_ref, router_ref, *refs):
    out_ref, mine_ref = refs[7:]
    share, width = qkv_ref.shape[0], qkv_ref.shape[1] // 3
    lanes = lax.broadcasted_iota(jnp.int32, (share, share), 1)
    lines = lax.broadcasted_iota(jnp.int32, (share, share), 0)
    places = lax.broadcasted_iota(jnp.int32, (share, 128), 1)
    spread = (
        lax.broadcasted_iota(jnp.int32, (router_ref.shape[0], 128), 0) + 8
        == lax.broadcasted_iota(jnp.int32, (router_ref.shape[0], 128), 1)
    ).astype(NARROW)
    side = mm_cols(router_ref[...], spread)
    for index in range(7):
        line = refs[index][...].astype(WIDE).reshape(1, share)
        column = jnp.sum(jnp.where(lanes == lines, line, 0.0), axis=-1, keepdims=True)
        side = jnp.where(places == index, column, side)
    out_ref[:, : 3 * width] = qkv_ref[...]
    out_ref[:, 3 * width :] = side.astype(NARROW)
    rows = mine_ref.shape[0]
    at = pl.multiple_of(core_ref[0] * rows, 8)
    mine_ref[...] = out_ref[pl.ds(at, rows), :]


def expert_weights_plain(me, vec, my_in, my_bias, my_out, rows, marked):
    rows, marked = jnp.concatenate(rows, axis=0), jnp.concatenate(marked, axis=0)
    width = rows.shape[1]
    gate = slot_gates(rows, marked[:, width:], vec[8:32].astype(NARROW), me)
    sent = (gate * marked[:, :width].astype(WIDE)).astype(NARROW)
    act, slope = gelu_parts(mm(rows, my_in) + my_bias.astype(WIDE))
    d_pre = mm_rows(sent, my_out) * slope
    return (
        mm_cols(act.astype(NARROW), sent),
        mm_cols(rows, d_pre.astype(NARROW)),
        jnp.sum(d_pre, axis=0, keepdims=True),
        jnp.sum(sent.astype(WIDE), axis=0, keepdims=True),
    )


def per_device(
    block_input,
    w_qkv,
    b_q,
    b_v,
    w_proj,
    b_proj,
    ln1_gain,
    ln1_bias,
    ln2_gain,
    ln2_bias,
    w_router,
    w_in,
    b_in,
    w_out,
    b_out,
    routes,
    slot_index,
    d_out,
):
    tokens, width = block_input.shape
    hidden_units = w_in.shape[2]
    experts = w_in.shape[0] * lax.axis_size("expert")
    groups = lax.axis_size("dp")
    layers = lax.axis_size("expert") // 2
    capacity = 2 * tokens // experts
    slots = -(-(capacity + 3) // 8) * 8
    total = experts * slots
    share = width // groups
    half = width // 2
    dp_me = lax.axis_index("dp")
    expert_me = lax.axis_index("expert")
    core, layer = expert_me % 2, expert_me // 2
    me = jnp.stack([expert_me, dp_me]).astype(jnp.int32)
    vectors = [b_q, b_v, b_proj, ln1_gain, ln1_bias, ln2_gain, ln2_bias]
    wide = 4 * width + 128
    shard, mine = run(
        pack_body,
        [
            like((share, 3 * width + 128), NARROW),
            like((share // 2, 3 * width + 128), NARROW),
        ],
        [core.reshape(1).astype(jnp.int32), w_qkv, w_router.T] + vectors,
        0,
        6 * share * wide,
        58,
        scalars=1,
        name="pack",
    )
    pieces, starts = gather_shared(shard, mine)
    if groups == 4:
        later, pieces[3] = lax.optimization_barrier((w_proj, pieces[3]))
        proj_pieces = [later] + [swap(later, "dp", mask) for mask in range(1, groups)]
        proj_starts = jnp.stack([(dp_me ^ mask) * share for mask in range(groups)])
    else:
        proj_pieces = [lax.all_gather(w_proj, "dp", axis=0, tiled=True)]
        proj_starts = jnp.zeros((1,), jnp.int32)
    targets = jnp.where(slot_index < capacity, (routes ^ expert_me) * slots + slot_index, -1)
    targets_row = targets.T
    device_targets = jnp.where(slot_index < capacity, routes * slots + slot_index, -1)
    part = share // (2 * layers)
    order = jnp.arange(half, dtype=jnp.int32)
    spot = (order // (share // 2) ^ dp_me) * share + (
        order // part % layers ^ layer
    ) * part + order % part
    chosen_columns = jnp.concatenate(
        [spot + core * (share // 2), spot + (1 - core) * (share // 2)]
    )[None].astype(jnp.int32)

    marked_blocks = run(
        functools.partial(grad_slots_body, experts),
        like((experts, slots, width + 128), NARROW),
        [d_out, routes, device_targets.T],
        2 * total * tokens * width,
        4 * total * width,
        16,
        name="grad_slots",
        marks=pieces[1:3],
    )
    marked_blocks = lax.all_to_all(marked_blocks, "expert", 0, 0, tiled=True)
    marked = marked_blocks.reshape(total, width + 128)

    full_qkv, vec, qkv, context, log_total, keep, give = run(
        functools.partial(attend_body, len(pieces)),
        [
            like((width, 3 * width), NARROW),
            like((32, width), WIDE),
            like((tokens, 3 * width), NARROW),
            like((tokens, width), NARROW),
            like((tokens, 128), WIDE),
            like((tokens, width), NARROW),
            like((tokens, width), NARROW),
        ],
        [jnp.stack(starts).astype(jnp.int32), block_input, chosen_columns] + pieces,
        10 * tokens * width * width,
        4 * width * wide,
        58,
        scalars=1,
        scratch=[pltpu.VMEM((width, 128), NARROW)],
        name="attend",
    )
    middle = run(
        functools.partial(middle_body, experts, len(proj_pieces)),
        [like((width, width), NARROW), like((tokens, width), WIDE), like((tokens, width), NARROW)]
        + [like((slots, width), NARROW)] * experts,
        [proj_starts.astype(jnp.int32), context, block_input, vec, targets_row] + proj_pieces,
        4 * tokens * width * width,
        4 * width * width,
        58,
        scalars=1,
        name="middle",
    )
    full_proj, hidden, y_in = middle[:3]
    marked, y_in = lax.optimization_barrier((marked, y_in))
    weight_in, weight_out = w_in[0], w_out[0]
    units = hidden_units // groups
    arrived, marked_near = lax.optimization_barrier((exchange(middle[3:]), gather_near(marked)))
    rows = run(
        order_body,
        like((total, width), NARROW),
        [me] + arrived,
        0,
        0,
        16,
        scalars=1,
        scratch=[pltpu.VMEM((total, width), WIDE)],
        name="order",
    )
    results = expert(
        me, rows, marked, vec, weight_in, b_in, weight_out, b_out, experts, slots, capacity, 1024
    )
    fresh, d_expert_in = results
    d_expert_in, rows_near, marked_near = lax.optimization_barrier(
        (d_expert_in, gather_near(rows), marked_near)
    )
    d_returned = lax.all_to_all(d_expert_in, "expert", 0, 0, tiled=True)
    fresh, give = lax.optimization_barrier((fresh, give))
    other = swap(give, "expert", 1)
    d_returned, other = lax.optimization_barrier((d_returned, other))
    rows_all = [rows] + rows_near + gather_far(rows_near)
    marked_all = [marked] + marked_near + gather_far(marked_near)
    gates, d_input, d_all = run(
        functools.partial(backward_body, experts, capacity),
        [
            like((tokens, 128), WIDE),
            like((tokens, width), WIDE),
            like((240, 4 * width), NARROW),
        ],
        [hidden, y_in, d_out, vec, full_proj, routes, slot_index, device_targets, d_returned]
        + [qkv, log_total, full_qkv, block_input],
        0,
        0,
        58,
        scratch=[
            pltpu.VMEM((total, width), WIDE),
            pltpu.VMEM((tokens, width), WIDE),
            pltpu.VMEM((tokens, width), NARROW),
            pltpu.VMEM((32, width), WIDE),
        ],
        name="backward",
    )
    d_all, fresh, rows_all, marked_all = lax.optimization_barrier(
        (d_all, fresh, rows_all, marked_all)
    )
    d_other = swap(d_all, "expert", 1)
    returned = lax.all_to_all(fresh, "expert", 0, 0, tiled=True)
    sums = run(
        functools.partial(outer_body, groups),
        [like((share // 2, wide), WIDE)] + [like((share // 2, wide), NARROW)] * (groups - 1),
        [chosen_columns, keep, other, d_all, d_other],
        4 * tokens * half * wide,
        6 * half * wide,
        58,
        scratch=[pltpu.VMEM((128, width), WIDE), pltpu.SemaphoreType.DMA((groups - 1,))]
        + [pltpu.VMEM((share // 2, wide), NARROW)] * (groups - 1),
        out_specs=[VMEM] + [pl.BlockSpec(memory_space=pltpu.HBM)] * (groups - 1),
        name="outer",
    )
    if groups == 4:
        grads = expert_weights(
            me, sums[1], vec, weight_in, b_in, weight_out, rows_all, marked_all, groups, 384
        )
        part_w_out, blocks, (part_b_in, sum_sent) = grads[0], grads[1:-2], grads[-2:]
    else:
        my_in, my_out, my_bias = (
            lax.dynamic_slice_in_dim(array, dp_me * units, units, axis)
            for array, axis in zip((weight_in, weight_out, b_in), (1, 0, 1))
        )
        part_w_out, d_w_in, part_b_in, sum_sent = expert_weights_plain(
            expert_me, vec, my_in, my_bias, my_out, rows_all, marked_all
        )
        blocks = [
            lax.dynamic_slice_in_dim(d_w_in, (dp_me ^ mask) * share, share, 0).astype(
                NARROW if mask else WIDE
            )
            for mask in range(groups)
        ]
    part_b_out = lax.dynamic_slice_in_dim(sum_sent[0], dp_me * share, share, 0)
    sums = [sums[0]] + [swap(sums[mask], "dp", mask) for mask in range(1, groups)]
    sums, part_b_in, part_b_out, returned = lax.optimization_barrier(
        (sums, part_b_in, part_b_out, returned)
    )
    sums = sum_blocks(sums[0], sums[1:], layers, WIDE)
    sums, blocks = lax.optimization_barrier((sums, blocks))
    sums = [sums[0]] + [swap(sums[mask], "expert", 2 * mask) for mask in range(1, layers)]
    blocks = [blocks[0]] + [swap(blocks[mask], "dp", mask) for mask in range(1, groups)]
    done = sum_blocks(sums[0], sums[1:], 1, NARROW)[0]
    block_out = run(
        output_body,
        like((tokens, width), NARROW),
        [hidden, gates, device_targets, returned],
        4 * tokens * total * width,
        8 * tokens * width,
        24,
        scratch=[pltpu.VMEM((total, width), WIDE)],
        name="output",
        marks=[done],
    )
    if groups == 4:
        part_w_in = run(
            spread_body,
            like((share, hidden_units), WIDE),
            [me] + blocks,
            share * hidden_units,
            8 * share * hidden_units,
            24,
            scalars=1,
            name="spread",
            marks=[done],
        )
    else:
        part_w_in = in_order([block.astype(WIDE) for block in blocks], dp_me, 1)
    done_pieces = [done] + [swap(done, "expert", 2 * mask) for mask in range(1, layers)]
    done_pieces, part_w_in, block_out = lax.optimization_barrier(
        (done_pieces, part_w_in, block_out)
    )
    low = join(done_pieces)
    high = swap(low, "expert", 1)

    place = jnp.arange(share // 2, dtype=jnp.int32)
    place = (place // part ^ layer) * part + place % part
    place = jnp.stack([place + core * (share // 2), place + (1 - core) * (share // 2)])
    finals = run(
        functools.partial(ordered_body, experts, layers, width),
        [
            like((share, 3 * width), WIDE),
            like((share, width), WIDE),
            like((share, experts), WIDE),
        ]
        + [like((1, share), WIDE)] * 7,
        [place.astype(jnp.int32), low, high],
        2 * share * share * wide,
        8 * share * wide,
        24,
        name="ordered",
    )
    vector_sum = [value[0] for value in finals[3:]]
    return (
        block_out,
        d_input,
        finals[0],
        vector_sum[3],
        vector_sum[4],
        finals[1],
        vector_sum[0],
        vector_sum[5],
        vector_sum[6],
        vector_sum[1],
        vector_sum[2],
        finals[2],
        part_w_in[None],
        part_b_in,
        part_w_out[None],
        part_b_out[None],
    )


def solution(mesh):
    return jax.shard_map(
        per_device,
        mesh=mesh,
        in_specs=(
            P(("dp", "expert"), None),
            P("dp", None),
            P("dp"),
            P("dp"),
            P("dp", None),
            P("dp"),
            P("dp"),
            P("dp"),
            P("dp"),
            P("dp"),
            P("dp", None),
            P("expert", None, None),
            P("expert", None),
            P("expert", None, None),
            P("expert", None),
            P(("dp", "expert"), None),
            P(("dp", "expert"), None),
            P(("dp", "expert"), None),
        ),
        out_specs=(
            P(("dp", "expert"), None),
            P(("dp", "expert"), None),
            P("dp", None),
            P("dp"),
            P("dp"),
            P("dp", None),
            P("dp"),
            P("dp"),
            P("dp"),
            P("dp"),
            P("dp"),
            P("dp", None),
            P("expert", "dp", None),
            P("expert", "dp"),
            P("expert", "dp", None),
            P("expert", "dp"),
        ),
        check_vma=False,
    )
```

```python
import functools
import math

import jax
import jax.numpy as jnp
from jax import lax
from jax.experimental import pallas as pl
from jax.experimental.pallas import tpu as pltpu
from jax.sharding import PartitionSpec as P

HEAD_DIM = 64
SEQ = 197


NORM_EPS = 1e-06
SQRT_HALF = 0.7071067811865476
INV_ROOT_TWO_PI = 0.3989422804014327


def normalize(values):
    center = values - jnp.mean(values, axis=-1, keepdims=True)
    inv_std = lax.rsqrt(jnp.mean(center * center, axis=-1, keepdims=True) + NORM_EPS)
    return (center * inv_std, inv_std)


def norm_back(grad_in, normed, inv_std, gain_vec):
    scaled = grad_in * gain_vec
    mean_plain = jnp.mean(scaled, axis=-1, keepdims=True)
    mean_mixed = jnp.mean(scaled * normed, axis=-1, keepdims=True)
    return inv_std * (scaled - mean_plain - normed * mean_mixed)


def gelu_value(pre_act):
    return 0.5 * pre_act * (1.0 + lax.erf(pre_act * SQRT_HALF))


def gelu_slope(pre_act):
    return 0.5 * (1.0 + lax.erf(pre_act * SQRT_HALF)) + pre_act * INV_ROOT_TWO_PI * jnp.exp(
        -0.5 * pre_act * pre_act
    )


def swap(values, axis, mask):
    size = lax.axis_size(axis)
    return lax.ppermute(values, axis, [(index, index ^ mask) for index in range(size)])


def gather_shared(shard, mine):
    groups = lax.axis_size("dp")
    rows = shard.shape[0]
    if groups != 4:
        return [lax.all_gather(shard, "dp", axis=0, tiled=True)], [jnp.int32(0)]
    me = lax.axis_index("dp")
    core = lax.axis_index("expert") % 2
    half = rows // 2
    part = half // 2
    from_one = swap(mine, "dp", 1)
    from_two = swap(mine, "dp", 2)
    far_low = swap(from_one[:part], "dp", 2)
    far_high = swap(from_two[part:], "dp", 1)
    other_one = swap(from_one, "expert", 1)
    other_two = swap(from_two, "expert", 1)
    other_low = swap(far_low, "expert", 1)
    other_high = swap(far_high, "expert", 1)
    base = core * half
    other = half - base
    one, two, far = (me ^ 1) * rows, (me ^ 2) * rows, (me ^ 3) * rows
    starts = [me * rows, one + base, two + base, far + base, far + base + part]
    starts += [one + other, two + other, far + other, far + other + part]
    pieces = [shard, from_one, from_two, far_low, far_high]
    pieces += [other_one, other_two, other_low, other_high]
    return pieces, starts


def gather_near(rows):
    groups = lax.axis_size("dp")
    return [swap(rows, "dp", mask) for mask in ((1, 2) if groups == 4 else range(1, groups))]


def gather_far(near):
    if lax.axis_size("dp") != 4:
        return []
    one, two = near
    half = one.shape[0] // 2
    return [swap(one[:half], "dp", 2), swap(two[half:], "dp", 1)]


def exchange(blocks):
    return [blocks[0]] + [swap(blocks[mask], "expert", mask) for mask in range(1, len(blocks))]


def in_order(pieces, me, axis):
    stack = jnp.stack(pieces)
    return jnp.concatenate(
        [
            lax.dynamic_index_in_dim(stack, me ^ index, 0, keepdims=False)
            for index in range(len(pieces))
        ],
        axis=axis,
    )


VMEM = pl.BlockSpec(memory_space=pltpu.VMEM)
SMEM = pl.BlockSpec(memory_space=pltpu.SMEM)
NARROW = jnp.bfloat16
WIDE = jnp.float32
MIB = 1024 * 1024


def like(shape, dtype):
    return jax.ShapeDtypeStruct(shape, dtype)


def run(
    body, outs, operands, flops, moved, mib, scalars=0, scratch=(), out_specs=None, name=None, marks=()
):
    marks = list(marks)
    count = len(operands)

    def marked_body(*refs):
        body(*refs[:count], *refs[count + len(marks) :])

    return pl.pallas_call(
        marked_body,
        out_shape=outs,
        in_specs=[SMEM] * scalars
        + [VMEM] * (count - scalars)
        + [pl.BlockSpec(memory_space=pl.ANY)] * len(marks),
        out_specs=out_specs or jax.tree.map(lambda _: VMEM, outs),
        scratch_shapes=list(scratch),
        compiler_params=pltpu.CompilerParams(vmem_limit_bytes=mib * MIB),
        cost_estimate=pl.CostEstimate(flops=1, bytes_accessed=1, transcendentals=0),
        name=name,
    )(*operands, *marks)


def mm(left, right):
    return jnp.dot(left, right, preferred_element_type=WIDE)


def mm_rows(left, right):
    return lax.dot_general(left, right, (((1,), (1,)), ((), ())), preferred_element_type=WIDE)


def mm_cols(left, right):
    return lax.dot_general(left, right, (((0,), (0,)), ((), ())), preferred_element_type=WIDE)


def head_masks(rows):
    lanes = lax.broadcasted_iota(jnp.int32, (rows, 2 * HEAD_DIM), 1)
    return [lanes < HEAD_DIM, lanes >= HEAD_DIM]


def join_body(count, *refs):
    out_ref, wide_ref = refs[count], refs[count + 1]
    at = 0
    for ref in refs[:count]:
        wide_ref[at : at + ref.shape[0], :] = ref[...].astype(WIDE)
        at += ref.shape[0]
    out_ref[...] = wide_ref[...].astype(NARROW)


def join(pieces):
    rows = sum(piece.shape[0] for piece in pieces)
    columns = pieces[0].shape[1]
    return run(
        functools.partial(join_body, len(pieces)),
        like((rows, columns), NARROW),
        pieces,
        rows * columns,
        4 * rows * columns,
        16,
        scratch=[pltpu.VMEM((rows, columns), WIDE)],
        name="join",
    )


def slot_rows(targets, total, tokens):
    ids = lax.broadcasted_iota(jnp.int32, (total, tokens), 0)
    return ids == targets[0:1, :], ids == targets[1:2, :]


def grad_slots_body(experts, d_ref, routes_ref, targets_ref, out_ref):
    tokens, width = d_ref.shape
    slots = out_ref.shape[1]
    first, second = slot_rows(targets_ref[...], experts * slots, tokens)
    first, second = first.astype(NARROW), second.astype(NARROW)
    rows = mm(first + second, d_ref[...]).astype(NARROW)
    lanes = lax.broadcasted_iota(jnp.int32, (tokens, 128), 1)
    other_first = (lanes == routes_ref[:, 1:2]).astype(NARROW)
    other_second = (lanes == routes_ref[:, 0:1]).astype(NARROW)
    marks = (mm(first, other_first) + mm(second, other_second)).astype(NARROW)
    for index in range(experts):
        out_ref[index, :, :width] = rows[index * slots : (index + 1) * slots, :]
        out_ref[index, :, width:] = marks[index * slots : (index + 1) * slots, :]


def order_body(me_ref, *refs):
    out_ref, wide_ref = refs[-2:]
    slots = refs[0].shape[0]
    for mask, ref in enumerate(refs[:-2]):
        at = pl.multiple_of((me_ref[0] ^ mask) * slots, 8)
        wide_ref[pl.ds(at, slots), :] = ref[...].astype(WIDE)
    out_ref[...] = wide_ref[...].astype(NARROW)


def attend_body(count, *refs):
    starts_ref, x_ref, columns_ref = refs[0], refs[1], refs[2]
    pieces = refs[3 : 3 + count]
    full_ref, vec_ref, qkv_ref, ctx_ref, lse_ref, keep_ref, give_ref = refs[3 + count : 10 + count]
    side_ref = refs[10 + count]
    tokens, width = x_ref.shape
    for index, piece in enumerate(pieces):
        rows = piece.shape[0]
        at = starts_ref[index] if count > 1 else 0
        if count > 1:
            at = pl.multiple_of(at, 16)
        full_ref[pl.ds(at, rows), :] = piece[:, : 3 * width]
        side_ref[pl.ds(at, rows), :] = piece[:, 3 * width :]
    side = jnp.transpose(side_ref[...].astype(WIDE))
    vec_ref[...] = side[: vec_ref.shape[0], :]
    bias_q, bias_v = vec_ref[0:1, :], vec_ref[1:2, :]
    gain, bias = vec_ref[3:4, :], vec_ref[4:5, :]
    normed, _ = normalize(x_ref[...].astype(WIDE))
    a_in = (normed * gain + bias).astype(NARROW)
    qkv_ref[:, :width] = (mm(a_in, full_ref[:, :width]) + bias_q).astype(NARROW)
    qkv_ref[:, width : 2 * width] = mm(a_in, full_ref[:, width : 2 * width]).astype(NARROW)
    qkv_ref[:, 2 * width :] = (
        mm(a_in, full_ref[:, 2 * width : 3 * width]) + bias_v
    ).astype(NARROW)
    masks = head_masks(tokens)
    lanes = lax.broadcasted_iota(jnp.int32, (tokens, 128), 1)
    lse_all = jnp.zeros((tokens, 128), WIDE)
    pair = 2 * HEAD_DIM
    for group in range(width // pair):
        at = group * pair
        query = qkv_ref[:, at : at + pair]
        keys = qkv_ref[:, width + at : width + at + pair]
        values = qkv_ref[:, 2 * width + at : 2 * width + at + pair]
        outs = []
        for index in range(2):
            scores = mm_rows(jnp.where(masks[index], query, 0), keys) * (
                1.0 / math.sqrt(HEAD_DIM)
            )
            top = jnp.max(scores, axis=-1, keepdims=True)
            exps = jnp.exp(scores - top)
            total = jnp.sum(exps, axis=-1, keepdims=True)
            lse_all = jnp.where(lanes == 2 * group + index, top + jnp.log(total), lse_all)
            outs.append(mm((exps / total).astype(NARROW), values))
        ctx_ref[:, at : at + pair] = jnp.where(masks[0], outs[0], outs[1]).astype(NARROW)
    lse_ref[...] = lse_all
    ids = lax.broadcasted_iota(jnp.int32, (width, columns_ref.shape[1]), 0)
    hot = (ids == columns_ref[0:1, :]).astype(NARROW)
    half = width // 2
    chosen = mm(a_in, hot).astype(NARROW)
    keep_ref[:, :half] = chosen[:, :half]
    give_ref[:, :half] = chosen[:, half:]
    chosen = mm(ctx_ref[...], hot).astype(NARROW)
    keep_ref[:, half:] = chosen[:, :half]
    give_ref[:, half:] = chosen[:, half:]


def middle_body(experts, count, starts_ref, ctx_ref, x_ref, vec_ref, targets_ref, *refs):
    full_ref, hidden_ref, y_ref = refs[count : count + 3]
    outs = refs[count + 3 :]
    for index, piece in enumerate(refs[:count]):
        at = pl.multiple_of(starts_ref[index], 16) if count > 1 else 0
        full_ref[pl.ds(at, piece.shape[0]), :] = piece[...]
    hidden = x_ref[...].astype(WIDE) + mm(ctx_ref[...], full_ref[...]) + vec_ref[2:3, :]
    hidden_ref[...] = hidden
    normed, _ = normalize(hidden)
    y_in = (normed * vec_ref[5:6, :] + vec_ref[6:7, :]).astype(NARROW)
    y_ref[...] = y_in
    slots = outs[0].shape[0]
    first, second = slot_rows(targets_ref[...], experts * slots, x_ref.shape[0])
    rows = mm((first | second).astype(NARROW), y_in).astype(NARROW)
    for index, out in enumerate(outs):
        out[...] = rows[index * slots : (index + 1) * slots, :]


def in_terms(values):
    high = values.astype(NARROW)
    rest = values - high.astype(WIDE)
    middle = rest.astype(NARROW)
    return high, middle, (rest - middle.astype(WIDE)).astype(NARROW)


def slot_gates(rows, marks, router, mine):
    logits = mm_rows(rows, router)
    lanes = lax.broadcasted_iota(jnp.int32, logits.shape, 1)
    own = jnp.sum(jnp.where(lanes == mine, logits, 0.0), axis=-1, keepdims=True)
    other = jnp.sum(
        marks[:, : logits.shape[1]].astype(WIDE) * logits, axis=-1, keepdims=True
    )
    return 1.0 / (1.0 + jnp.exp(other - own))


def gelu_parts(pre_act):
    half = 0.5 * (1.0 + lax.erf(pre_act * SQRT_HALF))
    slope = half + pre_act * INV_ROOT_TWO_PI * jnp.exp(-0.5 * pre_act * pre_act)
    return pre_act * half, slope


def expert_body(experts, spare, me_ref, rows_ref, marked_ref, vec_ref, in_ref, bin_ref, out_ref, bout_ref, *refs):
    fresh_ref = refs[0]
    back_ref, sent_ref, acc_ref, dacc_ref = refs[1:]
    step = pl.program_id(0)
    width = rows_ref.shape[1]

    @pl.when(step == 0)
    def _():
        router = vec_ref[8:32, :].astype(NARROW)
        gate = slot_gates(rows_ref[...], marked_ref[:, width:], router, me_ref[0])
        sent_ref[...] = (gate * marked_ref[:, :width].astype(WIDE)).astype(NARROW)
        acc_ref[...] = jnp.zeros_like(acc_ref)
        dacc_ref[...] = jnp.zeros_like(dacc_ref)

    weight_in, weight_out = in_ref[...], out_ref[...]
    pre_act = mm(rows_ref[...], weight_in) + bin_ref[...].astype(WIDE)
    act, slope = gelu_parts(pre_act)
    acc_ref[...] += mm(act.astype(NARROW), weight_out)
    d_pre = mm_rows(sent_ref[...], weight_out) * slope
    dacc_ref[...] += mm_rows(d_pre.astype(NARROW), weight_in)

    @pl.when(step == pl.num_programs(0) - 1)
    def _():
        bias = bout_ref[...].astype(WIDE)
        slots = back_ref.shape[1]
        lanes = lax.broadcasted_iota(jnp.int32, (slots, 128), 1)
        lines = lax.broadcasted_iota(jnp.int32, (slots, 128), 0)
        line_hot = (lanes == lines).astype(NARROW)
        spare_hot = ((lines == lanes + spare) & (lanes < 3)).astype(NARROW)
        grads = marked_ref[:, :width].astype(WIDE)
        fresh_all = (acc_ref[...] + bias).astype(NARROW).astype(WIDE)
        acc_ref[...] = fresh_all
        terms = [
            term.astype(WIDE)
            for term in in_terms(jnp.sum(grads * fresh_all, axis=-1, keepdims=True))
        ]
        for index in range(experts):
            at = index * slots
            fresh_ref[index] = acc_ref[at : at + slots, :].astype(NARROW)
            mine = jnp.zeros((slots, 128), WIDE)
            for place, term in enumerate(terms):
                mine = jnp.where(lanes == place, term[at : at + slots, :], mine)
            packed = mm(spare_hot, mm_cols(mine.astype(NARROW), line_hot).astype(NARROW))
            back_ref[index, :, :128] = (dacc_ref[at : at + slots, :128] + packed).astype(NARROW)
            back_ref[index, :, 128:] = dacc_ref[at : at + slots, 128:].astype(
                NARROW
            )


def expert(me, rows, marked, vec, weight_in, b_in, weight_out, b_out, experts, slots, spare, chunk):
    total, width = rows.shape
    hidden_units = weight_in.shape[1]
    whole = lambda array: pl.BlockSpec(array.shape, lambda step: (0, 0))
    block = like((experts, slots, width), NARROW)
    return pl.pallas_call(
        functools.partial(expert_body, experts, spare),
        grid=(hidden_units // chunk,),
        out_shape=[block, block],
        in_specs=[
            SMEM,
            whole(rows),
            whole(marked),
            whole(vec),
            pl.BlockSpec((width, chunk), lambda step: (0, step)),
            pl.BlockSpec((1, chunk), lambda step: (0, step)),
            pl.BlockSpec((chunk, width), lambda step: (step, 0)),
            whole(b_out),
        ],
        out_specs=[pl.BlockSpec((experts, slots, width), lambda step: (0, 0, 0))] * 2,
        scratch_shapes=[
            pltpu.VMEM((total, width), NARROW),
            pltpu.VMEM((total, width), WIDE),
            pltpu.VMEM((total, width), WIDE),
        ],
        compiler_params=pltpu.CompilerParams(vmem_limit_bytes=58 * MIB),
        cost_estimate=pl.CostEstimate(flops=1, bytes_accessed=1, transcendentals=0),
        name="expert",
    )(me, rows, marked, vec, weight_in, b_in, weight_out, b_out)


def weights_body(count, me_ref, mark_ref, vec_ref, in_ref, bin_ref, out_ref, *refs):
    rows_in, marked_in = refs[: count[0]], refs[count[0] : sum(count)]
    dout_ref, own_ref = refs[sum(count) : sum(count) + 2]
    others = refs[sum(count) + 2 : -5]
    dbin_ref, dbout_ref, rows_ref, sent_ref, din_ref = refs[-5:]
    width = in_ref.shape[0]

    @pl.when(pl.program_id(0) == 0)
    def _():
        router = vec_ref[8:32, :].astype(NARROW)
        at = 0
        for rows in rows_in:
            rows_ref[at : at + rows.shape[0], :] = rows[...]
            at += rows.shape[0]
        at = 0
        total = jnp.zeros((1, width), WIDE)
        for marked in marked_in:
            size = marked.shape[0]
            gate = slot_gates(rows_ref[at : at + size, :], marked[:, width:], router, me_ref[0])
            sent = (gate * marked[:, :width].astype(WIDE)).astype(NARROW)
            sent_ref[at : at + size, :] = sent
            total += jnp.sum(sent.astype(WIDE), axis=0, keepdims=True)
            at += size
        dbout_ref[...] = total

    pre_act = mm(rows_ref[...], in_ref[...]) + bin_ref[...].astype(WIDE)
    act, slope = gelu_parts(pre_act)
    dout_ref[...] = mm_cols(act.astype(NARROW), sent_ref[...])
    d_pre = mm_rows(sent_ref[...], out_ref[...]) * slope
    dbin_ref[...] = jnp.sum(d_pre, axis=0, keepdims=True)
    din_ref[...] = mm_cols(rows_ref[...], d_pre.astype(NARROW))
    share = own_ref.shape[0]
    for mask, out in enumerate((own_ref,) + others):
        at = pl.multiple_of((me_ref[1] ^ mask) * share, 8)
        out[...] = din_ref[pl.ds(at, share), :].astype(out.dtype)


def expert_weights(me, mark, vec, weight_in, b_in, weight_out, rows, marked, groups, chunk):
    count = len(rows), len(marked)
    width, hidden_units = weight_in.shape
    units = hidden_units // groups
    share = width // groups
    steps = units // chunk
    total = sum(piece.shape[0] for piece in rows)
    whole = lambda array: pl.BlockSpec(array.shape, lambda step, at: (0, 0))
    wide = lambda size: pl.BlockSpec((size, chunk), lambda step, at: (0, step))
    return pl.pallas_call(
        functools.partial(weights_body, count),
        grid_spec=pltpu.PrefetchScalarGridSpec(
            num_scalar_prefetch=1,
            grid=(steps,),
            in_specs=[
                pl.BlockSpec(memory_space=pl.ANY),
                whole(vec),
                pl.BlockSpec((width, chunk), lambda step, at: (0, at[1] * steps + step)),
                pl.BlockSpec((1, chunk), lambda step, at: (0, at[1] * steps + step)),
                pl.BlockSpec((chunk, width), lambda step, at: (at[1] * steps + step, 0)),
            ]
            + [whole(piece) for piece in rows + marked],
            out_specs=[pl.BlockSpec((chunk, width), lambda step, at: (step, 0))]
            + [wide(share)] * groups
            + [wide(1), pl.BlockSpec((1, width), lambda step, at: (0, 0))],
            scratch_shapes=[
                pltpu.VMEM((total, width), NARROW),
                pltpu.VMEM((total, width), NARROW),
                pltpu.VMEM((width, chunk), WIDE),
            ],
        ),
        out_shape=[like((units, width), WIDE), like((share, units), WIDE)]
        + [like((share, units), NARROW)] * (groups - 1)
        + [like((1, units), WIDE), like((1, width), WIDE)],
        compiler_params=pltpu.CompilerParams(vmem_limit_bytes=58 * MIB),
        cost_estimate=pl.CostEstimate(flops=1, bytes_accessed=1, transcendentals=0),
        name="expert_weights",
    )(me, mark, vec, weight_in, b_in, weight_out, *rows, *marked)


def combine_body(experts, spare, *refs):
    hidden_ref, y_ref, d_ref, vec_ref, full_ref, routes_ref, slot_ref, targets_ref = refs[:8]
    back_ref, gate_ref, dh_ref, dctx_ref, sums_ref, dret_ref = refs[8:]
    tokens, width = hidden_ref.shape
    slots = back_ref.shape[1]
    for index in range(experts):
        at = index * slots
        dret_ref[at : at + slots, :] = back_ref[index].astype(WIDE)
    d_returned = dret_ref[...].astype(NARROW)
    lanes = lax.broadcasted_iota(jnp.int32, (tokens, experts * slots), 1)
    places = lax.broadcasted_iota(jnp.int32, (tokens, 128), 1)
    d_gates = []
    for choice in range(2):
        target = targets_ref[:, choice : choice + 1]
        slot = slot_ref[:, choice : choice + 1]
        line = jnp.where(target < 0, -8, target - slot + spare)
        found = None
        for term in range(3):
            hot = (lanes == line + term).astype(NARROW)
            new = mm(hot, d_returned[:, :128])
            found = new if found is None else found + new
        d_gates.append(
            jnp.sum(jnp.where(places == slot, found, 0.0), axis=-1, keepdims=True)
        )
    router = vec_ref[8:32, :].astype(NARROW)
    y_in = y_ref[...]
    logits = mm_rows(y_in, router)
    names = lax.broadcasted_iota(jnp.int32, logits.shape, 1)
    hot_first = (names == routes_ref[:, 0:1]).astype(WIDE)
    hot_second = (names == routes_ref[:, 1:2]).astype(WIDE)
    chosen_first = jnp.sum(logits * hot_first, axis=-1, keepdims=True)
    chosen_second = jnp.sum(logits * hot_second, axis=-1, keepdims=True)
    gate_first = 1.0 / (1.0 + jnp.exp(chosen_second - chosen_first))
    gate_second = 1.0 - gate_first
    gate_ref[...] = jnp.broadcast_to(gate_first, gate_ref.shape)
    grad = d_ref[...].astype(WIDE)
    d_diff = (d_gates[0] - d_gates[1]) * gate_first * gate_second
    d_logits = (d_diff * (hot_first - hot_second)).astype(NARROW)
    sums_ref[8:32, :] = mm_cols(d_logits, y_in)
    hot = ((lanes == targets_ref[:, 0:1]) | (lanes == targets_ref[:, 1:2])).astype(NARROW)
    d_y = mm(hot, d_returned) + mm(d_logits, router)
    normed, inv_std = normalize(hidden_ref[...])
    d_hidden = grad + norm_back(d_y, normed, inv_std, vec_ref[5:6, :])
    sums_ref[0:8, :] = jnp.zeros((8, width), WIDE)
    sums_ref[0:1, :] = jnp.sum(d_hidden, axis=0, keepdims=True)
    sums_ref[1:2, :] = jnp.sum(d_y * normed, axis=0, keepdims=True)
    sums_ref[2:3, :] = jnp.sum(d_y, axis=0, keepdims=True)
    dh_ref[...] = d_hidden
    dctx_ref[...] = mm_rows(d_hidden.astype(NARROW), full_ref[...]).astype(NARROW)


def output_body(hidden_ref, gate_ref, targets_ref, fresh_ref, out_ref, ret_ref):
    tokens = hidden_ref.shape[0]
    experts, slots, _ = fresh_ref.shape
    for index in range(experts):
        at = index * slots
        ret_ref[at : at + slots, :] = fresh_ref[index].astype(WIDE)
    returned = ret_ref[...].astype(NARROW)
    lanes = lax.broadcasted_iota(jnp.int32, (tokens, experts * slots), 1)
    first = mm((lanes == targets_ref[:, 0:1]).astype(NARROW), returned)
    second = mm((lanes == targets_ref[:, 1:2]).astype(NARROW), returned)
    gate = gate_ref[:, 0:1]
    out_ref[...] = (hidden_ref[...] + (gate * first + (1.0 - gate) * second)).astype(NARROW)


def back_body(qkv_ref, dctx_ref, lse_ref, full_ref, x_ref, vec_ref, dh_ref, early_ref, dx_ref, out_ref):
    tokens, width = dctx_ref.shape
    masks = head_masks(tokens)
    lanes = lax.broadcasted_iota(jnp.int32, (tokens, 128), 1)
    pair = 2 * HEAD_DIM
    scale = 1.0 / math.sqrt(HEAD_DIM)
    out_ref[tokens:, :] = jnp.zeros((out_ref.shape[0] - tokens, out_ref.shape[1]), NARROW)
    out_ref[:tokens, :width] = dh_ref[...].astype(NARROW)
    sums_q, sums_v = [], []
    for group in range(width // pair):
        at = group * pair
        query = qkv_ref[:, at : at + pair]
        keys = qkv_ref[:, width + at : width + at + pair]
        values = qkv_ref[:, 2 * width + at : 2 * width + at + pair]
        grads = dctx_ref[:, at : at + pair]
        d_query = d_keys = d_values = None
        for index in range(2):
            zero = jnp.zeros_like(query)
            query_h = jnp.where(masks[index], query, zero)
            keys_h = jnp.where(masks[index], keys, zero)
            grads_h = jnp.where(masks[index], grads, zero)
            head = 2 * group + index
            lse = jnp.sum(jnp.where(lanes == head, lse_ref[...], 0.0), axis=-1, keepdims=True)
            probs = jnp.exp(mm_rows(query_h, keys) * scale - lse)
            d_probs = mm_rows(grads_h, values)
            delta = jnp.sum(probs * d_probs, axis=-1, keepdims=True)
            d_scores = (probs * (d_probs - delta) * scale).astype(NARROW)
            new_values = mm_cols(probs.astype(NARROW), grads_h)
            new_query = mm(d_scores, keys_h)
            new_keys = mm_cols(d_scores, query_h)
            d_values = new_values if d_values is None else d_values + new_values
            d_query = new_query if d_query is None else d_query + new_query
            d_keys = new_keys if d_keys is None else d_keys + new_keys
        out_ref[:tokens, width + at : width + at + pair] = d_query.astype(NARROW)
        out_ref[:tokens, 2 * width + at : 2 * width + at + pair] = d_keys.astype(NARROW)
        out_ref[:tokens, 3 * width + at : 3 * width + at + pair] = d_values.astype(NARROW)
        sums_q.append(jnp.sum(d_query, axis=0, keepdims=True))
        sums_v.append(jnp.sum(d_values, axis=0, keepdims=True))
    d_a = mm_rows(out_ref[:tokens, width:], full_ref[...])
    normed, inv_std = normalize(x_ref[...].astype(WIDE))
    dx_ref[...] = dh_ref[...] + norm_back(d_a, normed, inv_std, vec_ref[3:4, :])
    rows = lax.broadcasted_iota(jnp.int32, (32, width), 0)
    sums = early_ref[...]
    new_rows = (
        jnp.concatenate(sums_q, axis=1),
        jnp.concatenate(sums_v, axis=1),
        jnp.sum(d_a * normed, axis=0, keepdims=True),
        jnp.sum(d_a, axis=0, keepdims=True),
    )
    for place, new in enumerate(new_rows, 3):
        sums = jnp.where(rows == place, new, sums)
    base = out_ref.shape[0] - 32
    for place, term in enumerate(in_terms(sums)):
        out_ref[base:, place * width : (place + 1) * width] = term


def backward_body(experts, spare, *refs):
    inputs = refs[:8]
    d_returned_ref, qkv_ref, lse_ref, qkv_weight_ref, x_ref = refs[8:13]
    gate_ref, dx_ref, all_ref, dret_ref, dh_ref, dctx_ref, sums_ref = refs[13:]
    vec_ref = refs[3]
    combine_body(
        experts, spare, *inputs, d_returned_ref, gate_ref, dh_ref, dctx_ref, sums_ref, dret_ref
    )
    back_body(
        qkv_ref, dctx_ref, lse_ref, qkv_weight_ref, x_ref, vec_ref, dh_ref, sums_ref, dx_ref, all_ref
    )


def outer_body(groups, columns_ref, keep_ref, other_ref, own_d_ref, other_d_ref, own_ref, *refs):
    peers = refs[: groups - 1]
    turned_ref, sems = refs[groups - 1 : groups + 1]
    outs = refs[groups + 1 :]
    tokens = keep_ref.shape[0]
    width = keep_ref.shape[1]
    half = width // 2
    rows = own_ref.shape[0]
    base = own_d_ref.shape[0] - 32
    sums = jnp.zeros((32, width), WIDE)
    for ref in (own_d_ref, other_d_ref):
        mine = ref[base:, :width].astype(WIDE) + ref[base:, width : 2 * width].astype(WIDE)
        sums = sums + (mine + ref[base:, 2 * width : 3 * width].astype(WIDE))
    turned_ref[...] = jnp.zeros_like(turned_ref)
    turned_ref[0:32, :] = sums
    turned = jnp.transpose(turned_ref[...]).astype(NARROW)
    ids = lax.broadcasted_iota(jnp.int32, (width, half), 0)
    hot = (ids == columns_ref[0:1, :half]).astype(NARROW)
    blocks = (
        (0, width, half),
        (width, 4 * width, 0),
        (4 * width, 4 * width + 128, None),
    )
    for low, high, left in blocks:
        if left is None:
            total = mm_cols(hot, turned)
        else:
            total = mm_cols(keep_ref[:, left : left + half], own_d_ref[:tokens, low:high])
            total = total + mm_cols(
                other_ref[:, left : left + half], other_d_ref[:tokens, low:high]
            )
        own_ref[:, low:high] = total[:rows, :]
        for index in range(1, groups):
            outs[index - 1][:, low:high] = total[index * rows : (index + 1) * rows, :].astype(
                NARROW
            )
    copies = [
        pltpu.make_async_copy(out, peer, sems.at[index])
        for index, (out, peer) in enumerate(zip(outs, peers))
    ]
    for copy in copies:
        copy.start()
    for copy in copies:
        copy.wait()


def sum_body(count, layers, own_ref, *refs):
    total = own_ref[...]
    for ref in refs[:count]:
        total = total + ref[...].astype(WIDE)
    part = own_ref.shape[0] // layers
    for index, out in enumerate(refs[count:]):
        out[...] = total[index * part : (index + 1) * part, :].astype(out.dtype)


def sum_blocks(own, others, layers, first):
    rows, columns = own.shape
    part = rows // layers
    return run(
        functools.partial(sum_body, len(others), layers),
        [like((part, columns), first)] + [like((part, columns), NARROW)] * (layers - 1),
        [own] + others,
        rows * columns,
        12 * rows * columns,
        16,
        name="sum_blocks",
    )


def ordered_body(experts, layers, width, place_ref, low_ref, high_ref, *outs):
    qkv_ref, proj_ref, router_ref = outs[:3]
    rows = qkv_ref.shape[0]
    half = rows // 2
    ids = lax.broadcasted_iota(jnp.int32, (rows, half), 0)
    hot_low = (ids == place_ref[0:1, :]).astype(NARROW)
    hot_high = (ids == place_ref[1:2, :]).astype(NARROW)

    def pick(low, high):
        return mm(hot_low, low_ref[:, low:high]) + mm(hot_high, high_ref[:, low:high])

    proj_ref[...] = pick(0, width)
    qkv_ref[...] = pick(width, 4 * width)
    side = pick(4 * width, 4 * width + 128)
    router_ref[...] = side[:, 8 : 8 + experts]
    lanes = lax.broadcasted_iota(jnp.int32, (rows, rows), 1)
    lines = lax.broadcasted_iota(jnp.int32, (rows, rows), 0)
    for index, out in enumerate(outs[3:]):
        out[...] = jnp.sum(
            jnp.where(lanes == lines, side[:, index : index + 1], 0.0), axis=0, keepdims=True
        )


def spread_body(me_ref, *refs):
    out_ref = refs[-1]
    units = refs[0].shape[1]
    for mask, ref in enumerate(refs[:-1]):
        at = pl.multiple_of((me_ref[1] ^ mask) * units, 128)
        out_ref[:, pl.ds(at, units)] = ref[...].astype(WIDE)


def pack_body(core_ref, qkv_ref, router_ref, *refs):
    out_ref, mine_ref = refs[7:]
    share, width = qkv_ref.shape[0], qkv_ref.shape[1] // 3
    lanes = lax.broadcasted_iota(jnp.int32, (share, share), 1)
    lines = lax.broadcasted_iota(jnp.int32, (share, share), 0)
    places = lax.broadcasted_iota(jnp.int32, (share, 128), 1)
    spread = (
        lax.broadcasted_iota(jnp.int32, (router_ref.shape[0], 128), 0) + 8
        == lax.broadcasted_iota(jnp.int32, (router_ref.shape[0], 128), 1)
    ).astype(NARROW)
    side = mm_cols(router_ref[...], spread)
    for index in range(7):
        line = refs[index][...].astype(WIDE).reshape(1, share)
        column = jnp.sum(jnp.where(lanes == lines, line, 0.0), axis=-1, keepdims=True)
        side = jnp.where(places == index, column, side)
    out_ref[:, : 3 * width] = qkv_ref[...]
    out_ref[:, 3 * width :] = side.astype(NARROW)
    rows = mine_ref.shape[0]
    at = pl.multiple_of(core_ref[0] * rows, 8)
    mine_ref[...] = out_ref[pl.ds(at, rows), :]


def expert_weights_plain(me, vec, my_in, my_bias, my_out, rows, marked):
    rows, marked = jnp.concatenate(rows, axis=0), jnp.concatenate(marked, axis=0)
    width = rows.shape[1]
    gate = slot_gates(rows, marked[:, width:], vec[8:32].astype(NARROW), me)
    sent = (gate * marked[:, :width].astype(WIDE)).astype(NARROW)
    act, slope = gelu_parts(mm(rows, my_in) + my_bias.astype(WIDE))
    d_pre = mm_rows(sent, my_out) * slope
    return (
        mm_cols(act.astype(NARROW), sent),
        mm_cols(rows, d_pre.astype(NARROW)),
        jnp.sum(d_pre, axis=0, keepdims=True),
        jnp.sum(sent.astype(WIDE), axis=0, keepdims=True),
    )


def per_device(
    block_input,
    w_qkv,
    b_q,
    b_v,
    w_proj,
    b_proj,
    ln1_gain,
    ln1_bias,
    ln2_gain,
    ln2_bias,
    w_router,
    w_in,
    b_in,
    w_out,
    b_out,
    routes,
    slot_index,
    d_out,
):
    tokens, width = block_input.shape
    hidden_units = w_in.shape[2]
    experts = w_in.shape[0] * lax.axis_size("expert")
    groups = lax.axis_size("dp")
    layers = lax.axis_size("expert") // 2
    capacity = 2 * tokens // experts
    slots = -(-(capacity + 3) // 8) * 8
    total = experts * slots
    share = width // groups
    half = width // 2
    dp_me = lax.axis_index("dp")
    expert_me = lax.axis_index("expert")
    core, layer = expert_me % 2, expert_me // 2
    me = jnp.stack([expert_me, dp_me]).astype(jnp.int32)
    vectors = [b_q, b_v, b_proj, ln1_gain, ln1_bias, ln2_gain, ln2_bias]
    wide = 4 * width + 128
    shard, mine = run(
        pack_body,
        [
            like((share, 3 * width + 128), NARROW),
            like((share // 2, 3 * width + 128), NARROW),
        ],
        [core.reshape(1).astype(jnp.int32), w_qkv, w_router.T] + vectors,
        0,
        6 * share * wide,
        58,
        scalars=1,
        name="pack",
    )
    pieces, starts = gather_shared(shard, mine)
    starts = jnp.stack(starts).astype(jnp.int32)
    if groups == 4:
        later, pieces[3] = lax.optimization_barrier((w_proj, pieces[3]))
        proj_pieces = [later] + [swap(later, "dp", mask) for mask in range(1, groups)]
        proj_starts = (jnp.arange(groups, dtype=jnp.int32) ^ dp_me) * share
    else:
        proj_pieces = [lax.all_gather(w_proj, "dp", axis=0, tiled=True)]
        proj_starts = jnp.zeros((1,), jnp.int32)
    targets = jnp.where(slot_index < capacity, (routes ^ expert_me) * slots + slot_index, -1)
    targets_row = targets.T
    device_targets = jnp.where(slot_index < capacity, routes * slots + slot_index, -1)
    part = share // (2 * layers)
    order = jnp.arange(half, dtype=jnp.int32)
    spot = (order // (share // 2) ^ dp_me) * share + (
        order // part % layers ^ layer
    ) * part + order % part
    chosen_columns = jnp.concatenate(
        [spot + core * (share // 2), spot + (1 - core) * (share // 2)]
    )[None].astype(jnp.int32)

    marked_blocks = run(
        functools.partial(grad_slots_body, experts),
        like((experts, slots, width + 128), NARROW),
        [d_out, routes, device_targets.T],
        2 * total * tokens * width,
        4 * total * width,
        16,
        name="grad_slots",
        marks=pieces[1:3] + [starts, proj_starts, chosen_columns, targets_row],
    )
    marked_blocks = lax.all_to_all(marked_blocks, "expert", 0, 0, tiled=True)
    marked = marked_blocks.reshape(total, width + 128)

    full_qkv, vec, qkv, context, log_total, keep, give = run(
        functools.partial(attend_body, len(pieces)),
        [
            like((width, 3 * width), NARROW),
            like((32, width), WIDE),
            like((tokens, 3 * width), NARROW),
            like((tokens, width), NARROW),
            like((tokens, 128), WIDE),
            like((tokens, width), NARROW),
            like((tokens, width), NARROW),
        ],
        [starts, block_input, chosen_columns] + pieces,
        10 * tokens * width * width,
        4 * width * wide,
        58,
        scalars=1,
        scratch=[pltpu.VMEM((width, 128), NARROW)],
        name="attend",
    )
    middle = run(
        functools.partial(middle_body, experts, len(proj_pieces)),
        [like((width, width), NARROW), like((tokens, width), WIDE), like((tokens, width), NARROW)]
        + [like((slots, width), NARROW)] * experts,
        [proj_starts, context, block_input, vec, targets_row] + proj_pieces,
        4 * tokens * width * width,
        4 * width * width,
        58,
        scalars=1,
        name="middle",
    )
    full_proj, hidden, y_in = middle[:3]
    marked, y_in = lax.optimization_barrier((marked, y_in))
    weight_in, weight_out = w_in[0], w_out[0]
    units = hidden_units // groups
    arrived, marked_near = lax.optimization_barrier((exchange(middle[3:]), gather_near(marked)))
    rows = run(
        order_body,
        like((total, width), NARROW),
        [me] + arrived,
        0,
        0,
        16,
        scalars=1,
        scratch=[pltpu.VMEM((total, width), WIDE)],
        name="order",
    )
    results = expert(
        me, rows, marked, vec, weight_in, b_in, weight_out, b_out, experts, slots, capacity, 1024
    )
    fresh, d_expert_in = results
    d_expert_in, rows_near, marked_near = lax.optimization_barrier(
        (d_expert_in, gather_near(rows), marked_near)
    )
    d_returned = lax.all_to_all(d_expert_in, "expert", 0, 0, tiled=True)
    fresh, give = lax.optimization_barrier((fresh, give))
    other = swap(give, "expert", 1)
    d_returned, other = lax.optimization_barrier((d_returned, other))
    rows_all = [rows] + rows_near + gather_far(rows_near)
    marked_all = [marked] + marked_near + gather_far(marked_near)
    gates, d_input, d_all = run(
        functools.partial(backward_body, experts, capacity),
        [
            like((tokens, 128), WIDE),
            like((tokens, width), WIDE),
            like((240, 4 * width), NARROW),
        ],
        [hidden, y_in, d_out, vec, full_proj, routes, slot_index, device_targets, d_returned]
        + [qkv, log_total, full_qkv, block_input],
        0,
        0,
        58,
        scratch=[
            pltpu.VMEM((total, width), WIDE),
            pltpu.VMEM((tokens, width), WIDE),
            pltpu.VMEM((tokens, width), NARROW),
            pltpu.VMEM((32, width), WIDE),
        ],
        name="backward",
    )
    d_all, fresh, rows_all, marked_all = lax.optimization_barrier(
        (d_all, fresh, rows_all, marked_all)
    )
    d_other = swap(d_all, "expert", 1)
    returned = lax.all_to_all(fresh, "expert", 0, 0, tiled=True)
    sums = run(
        functools.partial(outer_body, groups),
        [like((share // 2, wide), WIDE)] + [like((share // 2, wide), NARROW)] * (groups - 1),
        [chosen_columns, keep, other, d_all, d_other],
        4 * tokens * half * wide,
        6 * half * wide,
        58,
        scratch=[pltpu.VMEM((128, width), WIDE), pltpu.SemaphoreType.DMA((groups - 1,))]
        + [pltpu.VMEM((share // 2, wide), NARROW)] * (groups - 1),
        out_specs=[VMEM] + [pl.BlockSpec(memory_space=pltpu.HBM)] * (groups - 1),
        name="outer",
    )
    if groups == 4:
        grads = expert_weights(
            me, sums[1], vec, weight_in, b_in, weight_out, rows_all, marked_all, groups, 384
        )
        part_w_out, blocks, (part_b_in, sum_sent) = grads[0], grads[1:-2], grads[-2:]
    else:
        my_in, my_out, my_bias = (
            lax.dynamic_slice_in_dim(array, dp_me * units, units, axis)
            for array, axis in zip((weight_in, weight_out, b_in), (1, 0, 1))
        )
        part_w_out, d_w_in, part_b_in, sum_sent = expert_weights_plain(
            expert_me, vec, my_in, my_bias, my_out, rows_all, marked_all
        )
        blocks = [
            lax.dynamic_slice_in_dim(d_w_in, (dp_me ^ mask) * share, share, 0).astype(
                NARROW if mask else WIDE
            )
            for mask in range(groups)
        ]
    part_b_out = lax.dynamic_slice_in_dim(sum_sent[0], dp_me * share, share, 0)
    sums = [sums[0]] + [swap(sums[mask], "dp", mask) for mask in range(1, groups)]
    sums, part_b_in, part_b_out, returned = lax.optimization_barrier(
        (sums, part_b_in, part_b_out, returned)
    )
    sums = sum_blocks(sums[0], sums[1:], layers, WIDE)
    sums, blocks = lax.optimization_barrier((sums, blocks))
    sums = [sums[0]] + [swap(sums[mask], "expert", 2 * mask) for mask in range(1, layers)]
    blocks = [blocks[0]] + [swap(blocks[mask], "dp", mask) for mask in range(1, groups)]
    done = sum_blocks(sums[0], sums[1:], 1, NARROW)[0]
    block_out = run(
        output_body,
        like((tokens, width), NARROW),
        [hidden, gates, device_targets, returned],
        4 * tokens * total * width,
        8 * tokens * width,
        24,
        scratch=[pltpu.VMEM((total, width), WIDE)],
        name="output",
        marks=[done],
    )
    if groups == 4:
        part_w_in = run(
            spread_body,
            like((share, hidden_units), WIDE),
            [me] + blocks,
            share * hidden_units,
            8 * share * hidden_units,
            24,
            scalars=1,
            name="spread",
            marks=[done],
        )
    else:
        part_w_in = in_order([block.astype(WIDE) for block in blocks], dp_me, 1)
    done_pieces = [done] + [swap(done, "expert", 2 * mask) for mask in range(1, layers)]
    done_pieces, part_w_in, block_out = lax.optimization_barrier(
        (done_pieces, part_w_in, block_out)
    )
    low = join(done_pieces)
    high = swap(low, "expert", 1)

    place = jnp.arange(share // 2, dtype=jnp.int32)
    place = (place // part ^ layer) * part + place % part
    place = jnp.stack([place + core * (share // 2), place + (1 - core) * (share // 2)])
    finals = run(
        functools.partial(ordered_body, experts, layers, width),
        [
            like((share, 3 * width), WIDE),
            like((share, width), WIDE),
            like((share, experts), WIDE),
        ]
        + [like((1, share), WIDE)] * 7,
        [place.astype(jnp.int32), low, high],
        2 * share * share * wide,
        8 * share * wide,
        24,
        name="ordered",
    )
    vector_sum = [value[0] for value in finals[3:]]
    return (
        block_out,
        d_input,
        finals[0],
        vector_sum[3],
        vector_sum[4],
        finals[1],
        vector_sum[0],
        vector_sum[5],
        vector_sum[6],
        vector_sum[1],
        vector_sum[2],
        finals[2],
        part_w_in[None],
        part_b_in,
        part_w_out[None],
        part_b_out[None],
    )


def solution(mesh):
    return jax.shard_map(
        per_device,
        mesh=mesh,
        in_specs=(
            P(("dp", "expert"), None),
            P("dp", None),
            P("dp"),
            P("dp"),
            P("dp", None),
            P("dp"),
            P("dp"),
            P("dp"),
            P("dp"),
            P("dp"),
            P("dp", None),
            P("expert", None, None),
            P("expert", None),
            P("expert", None, None),
            P("expert", None),
            P(("dp", "expert"), None),
            P(("dp", "expert"), None),
            P(("dp", "expert"), None),
        ),
        out_specs=(
            P(("dp", "expert"), None),
            P(("dp", "expert"), None),
            P("dp", None),
            P("dp"),
            P("dp"),
            P("dp", None),
            P("dp"),
            P("dp"),
            P("dp"),
            P("dp"),
            P("dp"),
            P("dp", None),
            P("expert", "dp", None),
            P("expert", "dp"),
            P("expert", "dp", None),
            P("expert", "dp"),
        ),
        check_vma=False,
    )
```
